256 devices in a mesh: grp: 8 (over x, core), own: 32 (over z, y).
Axes of the slice: x: 4, y: 4, z: 8, core: 2. Of those that a mesh axis runs over, the one named last changes fastest.
Arguments:
- orbitals: bfloat16 [256, 32, 1024], P(('grp', 'own')), may hold values from -3 to 3
- offsets: int32 [256, 2], P(('grp', 'own')), may hold values from 0 to 32
- pairs: int32 [256, 2], P('grp'), may hold values from 0 to 31, as said below
- ext_pot: bfloat16 [32, 4096], replicated, may hold values from -6 to 6
Outputs:
- gradient: float32 [256, 32, 1024], P(('grp', 'own'))
The draws below stay inside these ranges and needn't reach their ends.
Inputs may be any that keep to these rules, and one draw needn't show every extreme that they name: `pairs`: rows g * 32 to g * 32 + 31 belong to group g; each row names two different orbitals of the group. Calling owner o the device holding orbital o of a group, at most 2 rows of a group have orbital o as their first orbital, and in every group some owner has exactly 2.
All inputs are finite; a program needn't handle non-finite values.
Results may differ from the reference program's by a relative error of at most 0.0006.
Values may be sent and summed in bfloat16 or wider, within the bound.
No kernel may reach another device: no remote copies, remote signals or barrier semaphores. Data moves between devices by JAX's collectives and lax.ppermute only.
A program may use at most 64 MiB of HBM per device.

```python
import math
import jax
import jax.numpy as jnp
from jax import lax

B = 32
BZ = 32
G = 64
ORB_DEV = 1
TASK_CAP = 2
GROUPS = 8
OWNERS = 32
ORB_GRP = 32
ORBITALS = 256
PAIRS_GRP = 32
PAIRS = 256


def draw_pairs(key, part):

    def one_group(group):
        base = jax.random.fold_in(jax.random.fold_in(key, 7001), group)
        keys = jax.random.split(base, 5)
        heavy = jax.random.randint(keys[0], (), 0, OWNERS)
        spare = jax.random.permutation(keys[1], (OWNERS - 1) * TASK_CAP)[:PAIRS_GRP - TASK_CAP]
        others = (spare // TASK_CAP).astype(jnp.int32)
        others = others + (others >= heavy).astype(jnp.int32)
        owners = jnp.concatenate([jnp.full((TASK_CAP,), heavy, jnp.int32), others])
        first = owners * ORB_DEV + jax.random.randint(keys[2], (PAIRS_GRP,), 0, ORB_DEV)
        second = (first + jax.random.randint(keys[3], (PAIRS_GRP,), 1, ORB_GRP)) % ORB_GRP
        listed = jnp.stack([first, second], axis=1)
        ranking = jax.random.permutation(keys[4], PAIRS_GRP)
        return listed[ranking]
    every = jax.vmap(one_group)(jnp.arange(GROUPS, dtype=jnp.int32))
    return every.reshape(PAIRS, 2).astype(jnp.int32)


def set_ends(drawn, stream_key, least, largest):
    longest = drawn.shape.index(max(drawn.shape))
    spots = []
    for shift in (0, 1):
        where = [jax.random.randint(jax.random.fold_in(stream_key, axis), (), 0, length) for axis, length in enumerate(drawn.shape)]
        where[longest] = (where[longest] + shift) % drawn.shape[longest]
        spots.append(tuple(where))
    return drawn.at[spots[0]].set(least).at[spots[1]].set(largest)


def block_scale(key, dims, shards, least, high):
    level, own = 1.0, jax.random.fold_in(key, 6)
    for position, blocks in shards:
        draws = jnp.exp(jax.random.uniform(jax.random.fold_in(own, position), (blocks,), jnp.float32, least / len(shards), high / len(shards)))
        level = level * jnp.repeat(draws, dims[position] // blocks).reshape([-1 if axis == position else 1 for axis in range(len(dims))])
    return level


def scatter_about(own_key, dims, scale, limit, cuts=(), kind=jnp.bfloat16):
    entries = jax.random.normal(own_key, dims, jnp.float32) * scale
    if len(cuts) > 0:
        entries = block_scale(own_key, dims, cuts, -0.22, 0.18) * entries
    return jnp.clip(entries, min=-limit, max=limit).astype(kind)


def setup_inputs(seed: int = 0) -> dict:
    splits = jax.random.split(jax.random.key(seed), 5)
    return {
        "orbitals": scatter_about(splits[0], (ORBITALS, BZ, B * B), 0.5, 3.0, ((0, 256),)),
        "offsets": set_ends(jax.random.randint(splits[1], (ORBITALS, 2), 0, G - B + 1), jax.random.fold_in(splits[1], 1), 0, G - B).astype(jnp.int32),
        "pairs": draw_pairs(jax.random.fold_in(splits[4], 71), 0),
        "ext_pot": scatter_about(splits[3], (BZ, G * G), 1.0, 6.0),
    }


SCREEN = 0.0025
MIXING = 0.25
EXCHANGE_COEF = (3.0 / math.pi) ** (1.0 / 3.0)


def wave_squares(length):
    positions = jnp.arange(length, dtype=jnp.int32)
    signed = jnp.where(positions < length // 2, positions, positions - length)
    wavenumber = (2.0 * math.pi / length) * signed.astype(jnp.float32)
    return wavenumber * wavenumber


def green_table(depth, width):
    along_z = wave_squares(2 * depth)
    along_y = wave_squares(2 * width)
    squared_sum = along_z[:, None, None] + along_y[None, :, None] + along_y[None, None, :]
    return (4.0 * math.pi) / (squared_sum + SCREEN)


def shifted(box_data, shift_y, shift_x):
    padded = jnp.pad(box_data, ((0, 0), (B, B), (B, B)))
    anchor = jnp.zeros((), jnp.int32)
    corner = (anchor, (B + shift_y).astype(jnp.int32), (B + shift_x).astype(jnp.int32))
    return lax.dynamic_slice(padded, corner, (BZ, B, B))


def poisson_solve(pair_density, green_values):
    padded = jnp.pad(pair_density, ((0, BZ), (0, B), (0, B)))
    spectrum = jnp.fft.fftn(padded) * green_values
    return jnp.real(jnp.fft.ifftn(spectrum))[:BZ, :B, :B]


def reference(orbitals, offsets, pairs, ext_pot):
    box_data = orbitals.astype(jnp.float32).reshape(ORBITALS, BZ, B, B)
    green_values = green_table(BZ, B)

    def add_pair(item, running):
        group = (item // PAIRS_GRP).astype(jnp.int32)
        first = (pairs[item, 0] + group * ORB_GRP).astype(jnp.int32)
        second = (pairs[item, 1] + group * ORB_GRP).astype(jnp.int32)
        shift = offsets[second] - offsets[first]
        near_box = box_data[first]
        moved_box = shifted(box_data[second], -shift[0], -shift[1])
        potential_box = poisson_solve(near_box * moved_box, green_values)
        running = running.at[first].add(potential_box * moved_box)
        return running.at[second].add(shifted(potential_box * near_box, shift[0], shift[1]))

    exchange = lax.fori_loop(0, PAIRS, add_pair, jnp.zeros((ORBITALS, BZ, B, B), jnp.float32))

    def add_box(item, density):
        anchor = jnp.zeros((), jnp.int32)
        corner = (anchor, offsets[item, 0].astype(jnp.int32), offsets[item, 1].astype(jnp.int32))
        current = lax.dynamic_slice(density, corner, (BZ, B, B))
        values = box_data[item]
        return lax.dynamic_update_slice(density, current + values * values, corner)

    density = lax.fori_loop(0, ORBITALS, add_box, jnp.zeros((BZ, G, G), jnp.float32))
    potential = ext_pot.astype(jnp.float32).reshape(BZ, G, G) - EXCHANGE_COEF * jnp.cbrt(density)

    def read_box(item):
        anchor = jnp.zeros((), jnp.int32)
        corner = (anchor, offsets[item, 0].astype(jnp.int32), offsets[item, 1].astype(jnp.int32))
        return lax.dynamic_slice(potential, corner, (BZ, B, B))

    local_potential = lax.map(read_box, jnp.arange(ORBITALS, dtype=jnp.int32))
    gradient = local_potential * box_data - MIXING * exchange
    return gradient.reshape(ORBITALS, BZ, B * B)
```

```python
import math

import jax
import jax.numpy as jnp
import numpy as np
from jax import lax
from jax.experimental import pallas as pl
from jax.experimental.pallas import tpu as pltpu
from jax.sharding import PartitionSpec as P

B = 32
BZ = 32
G = 64
N = 32
HALF = 16
SCREEN = 0.0025
MIXING = 0.25
EXCHANGE_COEF = (3.0 / math.pi) ** (1.0 / 3.0)
F32 = jnp.float32
BF16 = jnp.bfloat16
VM = pl.BlockSpec(memory_space=pltpu.VMEM)
SM = pl.BlockSpec(memory_space=pltpu.SMEM)


def axis_basis():
    position = np.arange(B) - 15.5
    cosine = np.cos(2 * np.pi / G * np.outer(position, np.arange(B)))
    sine = np.sin(2 * np.pi / G * np.outer(position, np.arange(1, B + 1)))
    return cosine, sine


def fold_matrix():
    fold = np.zeros((2, 4, B, 2, 2, 4, HALF))
    for h in range(2):
        for yy in range(4):
            row = yy if h == 0 else 3 - yy
            for x in range(B):
                col = x if x < HALF else B - 1 - x
                for py in range(2):
                    for px in range(2):
                        sign = (-1 if py and h else 1) * (-1 if px and x >= HALF else 1)
                        fold[h, yy, x, py, px, row, col] = sign
    return fold.reshape(256, 256)


def wave_info(parity):
    waves = np.arange(B) + parity
    weight = np.where((waves == 0) | (waves == B), 1.0, 2.0) / G
    return waves, weight


def split(value):
    high = value.astype(BF16)
    low = (value - high.astype(F32)).astype(BF16)
    return high, low


def np_split(value):
    value = value.astype(np.float32)
    high = value.astype(jnp.bfloat16)
    low = (value - high.astype(np.float32)).astype(jnp.bfloat16)
    return high, low


def dot(a, b):
    return jnp.dot(a, b, preferred_element_type=F32)


def torus_roll(load, by_y, by_x):
    lane = lax.broadcasted_iota(jnp.int32, (N, 128), 1)
    by_y = lax.rem(by_y, B)
    by_x = lax.rem(by_x, B)
    rows = lax.div(by_y, 4)
    rest = lax.rem(by_y, 4)
    shift = rest * B + by_x
    near = lax.rem(128 - shift, 128)
    far = lax.rem(128 + B - shift, 128)
    inside = lax.rem(lane, B) < B - by_x
    same = lax.div(lane, B) < 4 - rest
    moved = []
    for s in range(8):
        chunk = load(lax.rem(rows + s, 8))
        moved.append(
            jnp.where(inside, pltpu.roll(chunk, near, 1), pltpu.roll(chunk, far, 1))
        )
    return [jnp.where(same, moved[s], moved[(s + 1) % 8]) for s in range(8)]


def pack_kernel(offsets, box, out, planes):
    oy = offsets[0, 0]
    ox = offsets[0, 1]

    def load(c):
        return box[0, :, pl.ds(pl.multiple_of(c * 128, 128), 128)].astype(F32)

    chunks = torus_roll(load, B - lax.rem(oy, B), B - lax.rem(ox, B))
    for s in range(8):
        planes[pl.ds(s, N, stride=8), :] = chunks[s]
    row = lax.broadcasted_iota(jnp.int32, (8, 128), 0)
    extra = jnp.where(
        row == 0, oy.astype(F32), jnp.where(row == 1, ox.astype(F32), 0.0)
    )
    for z in range(N):
        both = jnp.concatenate([planes[8 * z : 8 * z + 8, :], extra], axis=0)
        out[z] = both.astype(BF16)


def pair_kernel(pairs, recv, rho, dens, phi, code):
    row = lax.broadcasted_iota(jnp.int32, (8, 128), 0)
    lane = lax.broadcasted_iota(jnp.int32, (8, 128), 1)
    y = (row * 4 + lax.div(lane, B)).astype(F32)
    x = lax.rem(lane, B).astype(F32)
    total = [jnp.zeros((8, 128), F32) for _ in range(4)]
    for n in range(N):
        value = recv[n].astype(F32)
        plane = value[:8]
        below = jnp.where(y < value[8:9], 2.0, 0.0)
        quarter = below + jnp.where(x < value[9:10], 1.0, 0.0)
        phi[n] = plane
        code[n] = quarter
        square = plane * plane
        for q in range(4):
            total[q] = total[q] + jnp.where(quarter == float(q), square, 0.0)
    for g in range(8):
        for q in range(4):
            dens[g, q] = total[q]
    for p in range(N):
        a = pairs[p, 0]
        b = pairs[p, 1]
        rho[p] = jnp.where(code[a] == code[b], phi[a] * phi[b], 0.0)


def table_kernel(rows_y, rows_x, cols_y, cols_x, ahead_hi, ahead_lo, back_hi, back_lo, green):
    for par in range(4):
        py, px = par // 2, par % 2
        for c in range(HALF):
            high, low = split(rows_y[py, c : c + 1, :] * rows_x[px])
            ahead_hi[par, c * HALF : (c + 1) * HALF, :] = high
            ahead_lo[par, c * HALF : (c + 1) * HALF, :] = low
        for k in range(B):
            high, low = split(cols_y[py, k : k + 1, :] * cols_x[px])
            back_hi[par, k * B : (k + 1) * B, :] = high
            back_lo[par, k * B : (k + 1) * B, :] = low
        kz = lax.broadcasted_iota(jnp.int32, (G, B * B), 0)
        pos = lax.broadcasted_iota(jnp.int32, (G, B * B), 1)
        kz = jnp.where(kz >= B, kz - (B - 1), kz)
        ky = lax.div(pos, B) + py
        kx = lax.rem(pos, B) + px
        weight = jnp.full((G, B * B), 4.0 * math.pi * 8.0 / G**3, F32)
        squares = jnp.full((G, B * B), SCREEN, F32)
        for k in (kx, ky, kz):
            weight = jnp.where((k == 0) | (k == B), weight * 0.5, weight)
            wave = 2.0 * math.pi / G * k.astype(F32)
            squares = squares + wave * wave
        green[par] = weight / squares


def solve_kernel(
    first, recv, rho, ahead_hi, ahead_lo, back_hi, back_lo, green, fold, unfold, z_ahead, z_back, out
):
    place = recv[first[0]].astype(F32)
    oy = jnp.max(place[8:9, :]).astype(jnp.int32)
    ox = jnp.max(place[9:10, :]).astype(jnp.int32)
    chunks = torus_roll(lambda c: rho[pl.ds(c, N, stride=8), :], oy, ox)
    lane = lax.broadcasted_iota(jnp.int32, (N, 128), 1)
    low_half = lane < 64

    stacked = jnp.concatenate(
        [jnp.concatenate([chunks[s], chunks[7 - s]], axis=1) for s in range(4)], axis=0
    )
    high, low = split(stacked)
    folded = dot(high, fold[...]) + dot(low, fold[...])

    def regroup(tile, par_low, parts):
        first_part, second_part = parts
        if par_low:
            return jnp.where(low_half, first_part, pltpu.roll(second_part, 64, 1))
        return jnp.where(low_half, pltpu.roll(first_part, 64, 1), second_part)

    solved = []
    for par in range(4):
        c = 128 * (par // 2)
        pieces = [folded[N * s : N * s + N, c : c + 128] for s in range(4)]
        data = jnp.concatenate(
            [regroup(t, par % 2 == 0, pieces[2 * t : 2 * t + 2]) for t in range(2)], axis=1
        )
        high, low = split(data)
        both = dot(jnp.concatenate([high, low], axis=0), ahead_hi[par])
        plane_waves = both[:N] + both[N:] + dot(high, ahead_lo[par])
        high, low = split(plane_waves)
        waves = dot(z_ahead[...], jnp.concatenate([high, high, low], axis=0)) * green[par]
        high, low = split(waves)
        back = dot(z_back[...], jnp.concatenate([high, high, low], axis=0))
        high, low = split(back)
        both = dot(jnp.concatenate([high, low], axis=0), back_hi[par])
        solved.append(both[:N] + both[N:] + dot(high, back_lo[par]))

    rows = []
    for s in range(4):
        t = 128 * (s // 2)
        tiles = []
        for half in range(2):
            even = solved[2 * half][:, t : t + 128]
            odd = solved[2 * half + 1][:, t : t + 128]
            tiles.append(regroup(half, s % 2 == 0, (even, odd)))
        rows.append(jnp.concatenate(tiles, axis=1))
    high, low = split(jnp.concatenate(rows, axis=0))
    spread = dot(high, unfold[...]) + dot(low, unfold[...])
    field = [spread[N * s : N * s + N, :128] for s in range(4)] + [
        spread[N * s : N * s + N, 128:] for s in range(3, -1, -1)
    ]
    chunk_store = out
    return field, oy, ox, chunk_store


def solve_and_send(
    first, recv, rho, ahead_hi, ahead_lo, back_hi, back_lo, green, fold, unfold, z_ahead, z_back, out, boxed
):
    field, oy, ox, _ = solve_kernel(
        first, recv, rho, ahead_hi, ahead_lo, back_hi, back_lo, green, fold, unfold, z_ahead, z_back, out
    )
    for s in range(8):
        boxed[s] = field[s]
    chunks = torus_roll(lambda c: boxed[c], B - lax.rem(oy, B), B - lax.rem(ox, B))
    for s in range(8):
        out[pl.ds(s, N, stride=8), :] = chunks[s]


def gradient_kernel(pairs, phi, code, field, pot, out, terms):
    for n in range(N):
        terms[n] = jnp.zeros((8, 128), F32)
    for p in range(N):
        a = pairs[p, 0]
        b = pairs[p, 1]
        value = jnp.where(code[a] == code[b], field[p], 0.0)
        terms[a] = terms[a] + value * phi[b]
        terms[b] = terms[b] + value * phi[a]
    quarters = [pot[q] for q in range(4)]
    for n in range(N):
        quarter = code[n]
        local = jnp.where(
            quarter < 1.5,
            jnp.where(quarter < 0.5, quarters[0], quarters[1]),
            jnp.where(quarter < 2.5, quarters[2], quarters[3]),
        )
        out[n] = local * phi[n] - MIXING * terms[n]


def unpack_kernel(offsets, planes, out):
    chunks = torus_roll(
        lambda c: planes[pl.ds(c, N, stride=8), :], offsets[0, 0], offsets[0, 1]
    )
    for s in range(8):
        out[0, :, 128 * s : 128 * s + 128] = chunks[s]


def shape(dims, dtype=F32):
    return jax.ShapeDtypeStruct(dims, dtype)


def constants():
    cosine, sine = axis_basis()
    bases = [cosine[:HALF], sine[:HALF]]
    rows_y = np.stack([np.repeat(b, B, axis=1) for b in bases])
    rows_x = np.stack([np.tile(b, (1, B)) for b in bases])
    cols_y = np.stack([np.repeat(b.T, HALF, axis=1) for b in bases])
    cols_x = np.stack([np.tile(b.T, (1, HALF)) for b in bases])
    fold = fold_matrix()
    z_basis = np.concatenate([cosine, sine], axis=1)
    ahead_hi, ahead_lo = np_split(z_basis.T)
    back_hi, back_lo = np_split(z_basis)
    return (
        [jnp.asarray(t.astype(np.float32)) for t in (rows_y, rows_x, cols_y, cols_x)],
        [jnp.asarray(t, BF16) for t in (fold, fold.T)],
        [
            jnp.asarray(np.concatenate([ahead_hi, ahead_lo, ahead_hi], axis=1)),
            jnp.asarray(np.concatenate([back_hi, back_lo, back_hi], axis=1)),
        ],
    )


def exchange(x):
    return lax.all_to_all(x, "own", 0, 0, tiled=True)


def body(orbitals, offsets, pairs, ext_pot):
    owner = lax.axis_index("own")
    bases, folds, z_tables = constants()

    sent = pl.pallas_call(
        pack_kernel,
        out_shape=shape((N, 16, 128), BF16),
        in_specs=[SM, VM],
        out_specs=VM,
        scratch_shapes=[pltpu.VMEM((8 * N, 128), F32)],
        name="pack",
    )(offsets, orbitals)
    recv = exchange(sent)

    tables = pl.pallas_call(
        table_kernel,
        out_shape=[
            shape((4, 256, 1024), BF16),
            shape((4, 256, 1024), BF16),
            shape((4, 1024, 256), BF16),
            shape((4, 1024, 256), BF16),
            shape((4, G, 1024)),
        ],
        in_specs=[VM] * 4,
        out_specs=[VM] * 5,
        compiler_params=pltpu.CompilerParams(vmem_limit_bytes=40 << 20),
        cost_estimate=pl.CostEstimate(flops=20_000_000, bytes_accessed=10_000_000, transcendentals=0),
        name="tables",
    )(*bases)

    rho, dens, phi, code = pl.pallas_call(
        pair_kernel,
        out_shape=[
            shape((N, 8, 128)),
            shape((8, 4, 8, 128)),
            shape((N, 8, 128)),
            shape((N, 8, 128)),
        ],
        in_specs=[SM, VM],
        out_specs=[VM] * 4,
        name="pair_products",
    )(pairs, recv)

    mine = exchange(rho)
    densities = lax.all_to_all(dens, "grp", 0, 0, tiled=True)
    first = lax.dynamic_slice_in_dim(pairs, owner, 1, 0)[0, :1]
    field = pl.pallas_call(
        solve_and_send,
        out_shape=shape((8 * N, 128)),
        in_specs=[SM] + [VM] * 11,
        out_specs=VM,
        scratch_shapes=[pltpu.VMEM((8, N, 128), F32)],
        compiler_params=pltpu.CompilerParams(vmem_limit_bytes=40 << 20),
        cost_estimate=pl.CostEstimate(flops=1_000_000_000, bytes_accessed=10_000_000, transcendentals=0),
        name="solve",
    )(first, recv, mine.reshape(8 * N, 128), *tables, *folds, *z_tables)
    fields = exchange(field.reshape(N, 8, 128))

    plane = lax.dynamic_slice_in_dim(ext_pot, owner, 1, 0).astype(F32)
    plane = plane.reshape(2, B, 2, B).transpose(0, 2, 1, 3).reshape(4, 8, 128)
    potential = plane - EXCHANGE_COEF * jnp.cbrt(jnp.sum(densities, axis=0))

    gradient = pl.pallas_call(
        gradient_kernel,
        out_shape=shape((N, 8, 128)),
        in_specs=[SM] + [VM] * 4,
        out_specs=VM,
        scratch_shapes=[pltpu.VMEM((N, 8, 128), F32)],
        name="gradient_planes",
    )(pairs, phi, code, fields, potential)
    back = exchange(gradient)

    return pl.pallas_call(
        unpack_kernel,
        out_shape=shape((1, BZ, B * B)),
        in_specs=[SM, VM],
        out_specs=VM,
        name="unpack",
    )(offsets, back.reshape(8 * N, 128))


def solution(mesh):
    spec = P(("grp", "own"), None, None)
    in_specs = (spec, P(("grp", "own"), None), P("grp", None), P())
    return jax.shard_map(body, mesh=mesh, in_specs=in_specs, out_specs=spec, check_vma=False)
```

```python
import math

import jax
import jax.numpy as jnp
import numpy as np
from jax import lax
from jax.experimental import pallas as pl
from jax.experimental.pallas import tpu as pltpu
from jax.sharding import PartitionSpec as P

B = 32
BZ = 32
G = 64
N = 32
HALF = 16
SCREEN = 0.0025
MIXING = 0.25
EXCHANGE_COEF = (3.0 / math.pi) ** (1.0 / 3.0)
F32 = jnp.float32
BF16 = jnp.bfloat16
VM = pl.BlockSpec(memory_space=pltpu.VMEM)
SM = pl.BlockSpec(memory_space=pltpu.SMEM)


def axis_basis():
    position = np.arange(B) - 15.5
    cosine = np.cos(2 * np.pi / G * np.outer(position, np.arange(B)))
    sine = np.sin(2 * np.pi / G * np.outer(position, np.arange(1, B + 1)))
    return cosine, sine


def fold_matrix():
    fold = np.zeros((2, 4, B, 2, 2, 4, HALF))
    for h in range(2):
        for yy in range(4):
            row = yy if h == 0 else 3 - yy
            for x in range(B):
                col = x if x < HALF else B - 1 - x
                for py in range(2):
                    for px in range(2):
                        sign = (-1 if py and h else 1) * (-1 if px and x >= HALF else 1)
                        fold[h, yy, x, py, px, row, col] = sign
    return fold.reshape(256, 256)


def wave_info(parity):
    waves = np.arange(B) + parity
    weight = np.where((waves == 0) | (waves == B), 1.0, 2.0) / G
    return waves, weight


def split(value):
    high = value.astype(BF16)
    low = (value - high.astype(F32)).astype(BF16)
    return high, low


def np_split(value):
    value = value.astype(np.float32)
    high = value.astype(jnp.bfloat16)
    low = (value - high.astype(np.float32)).astype(jnp.bfloat16)
    return high, low


def dot(a, b):
    return jnp.dot(a, b, preferred_element_type=F32)


def torus_roll(load, by_y, by_x):
    lane = lax.broadcasted_iota(jnp.int32, (N, 128), 1)
    by_y = lax.rem(by_y, B)
    by_x = lax.rem(by_x, B)
    rows = lax.div(by_y, 4)
    rest = lax.rem(by_y, 4)
    shift = rest * B + by_x
    near = lax.rem(128 - shift, 128)
    far = lax.rem(128 + B - shift, 128)
    inside = lax.rem(lane, B) < B - by_x
    same = lax.div(lane, B) < 4 - rest
    moved = []
    for s in range(8):
        chunk = load(lax.rem(rows + s, 8))
        moved.append(
            jnp.where(inside, pltpu.roll(chunk, near, 1), pltpu.roll(chunk, far, 1))
        )
    return [jnp.where(same, moved[s], moved[(s + 1) % 8]) for s in range(8)]


def pack_kernel(offsets, box, out, planes):
    oy = offsets[0, 0]
    ox = offsets[0, 1]

    def load(c):
        return box[0, :, pl.ds(pl.multiple_of(c * 128, 128), 128)].astype(F32)

    chunks = torus_roll(load, B - lax.rem(oy, B), B - lax.rem(ox, B))
    for s in range(8):
        planes[pl.ds(s, N, stride=8), :] = chunks[s]
    row = lax.broadcasted_iota(jnp.int32, (8, 128), 0)
    extra = jnp.where(
        row == 0, oy.astype(F32), jnp.where(row == 1, ox.astype(F32), 0.0)
    )
    for z in range(N):
        both = jnp.concatenate([planes[8 * z : 8 * z + 8, :], extra], axis=0)
        out[z] = both.astype(BF16)


def pair_kernel(pairs, recv, rho, dens, phi, code):
    row = lax.broadcasted_iota(jnp.int32, (8, 128), 0)
    lane = lax.broadcasted_iota(jnp.int32, (8, 128), 1)
    y = (row * 4 + lax.div(lane, B)).astype(F32)
    x = lax.rem(lane, B).astype(F32)
    total = [jnp.zeros((8, 128), F32) for _ in range(4)]
    for n in range(N):
        value = recv[n].astype(F32)
        plane = value[:8]
        below = jnp.where(y < value[8:9], 2.0, 0.0)
        quarter = below + jnp.where(x < value[9:10], 1.0, 0.0)
        phi[n] = plane
        code[n] = quarter
        square = plane * plane
        for q in range(4):
            total[q] = total[q] + jnp.where(quarter == float(q), square, 0.0)
    for q in range(4):
        dens[q] = total[q]
    for p in range(N):
        a = pairs[0, p]
        b = pairs[1, p]
        rho[p] = jnp.where(code[a] == code[b], phi[a] * phi[b], 0.0)


def table_kernel(bases, fixed, ahead, back, green):
    ahead[8, :, :768] = fixed[...]
    for par in range(4):
        py, px = par // 2, par % 2
        for c in range(HALF):
            row_y = bases[HALF * py + c : HALF * py + c + 1, :]
            row_x = bases[B + HALF * px : B + HALF * px + HALF, :]
            high, low = split(row_y * row_x)
            ahead[2 * par, c * HALF : (c + 1) * HALF, :] = high
            ahead[2 * par + 1, c * HALF : (c + 1) * HALF, :] = low
        for k in range(B):
            col_y = bases[2 * B + k : 2 * B + k + 1, 256 * py : 256 * py + 256]
            col_x = bases[2 * B :, 512 + 256 * px : 768 + 256 * px]
            high, low = split(col_y * col_x)
            back[par, 0, k * B : (k + 1) * B, :] = high
            back[par, 1, k * B : (k + 1) * B, :] = low
        kz = lax.broadcasted_iota(jnp.int32, (G, B * B), 0)
        pos = lax.broadcasted_iota(jnp.int32, (G, B * B), 1)
        kz = jnp.where(kz >= B, kz - (B - 1), kz)
        ky = lax.div(pos, B) + py
        kx = lax.rem(pos, B) + px
        weight = jnp.full((G, B * B), 4.0 * math.pi * 8.0 / G**3, F32)
        squares = jnp.full((G, B * B), SCREEN, F32)
        for k in (kx, ky, kz):
            weight = jnp.where((k == 0) | (k == B), weight * 0.5, weight)
            wave = 2.0 * math.pi / G * k.astype(F32)
            squares = squares + wave * wave
        green[par, :G, :] = weight / squares


def solve_kernel(
    first, recv, rho, dens, other, ahead_in, back_in, green_in,
    out, summed, fixed, ahead, back, green, boxed, sems,
):
    fetch = pltpu.make_async_copy(ahead_in.at[8], fixed, sems.at[4, 0])
    fetch.start()
    copies = []
    for par in range(4):
        for t, (source, target) in enumerate(
            (
                (ahead_in.at[pl.ds(2 * par, 2)], ahead.at[par]),
                (green_in.at[par, pl.ds(0, G)], green.at[par]),
                (back_in.at[par], back.at[par]),
            )
        ):
            copy = pltpu.make_async_copy(source, target, sems.at[par, t])
            copy.start()
            copies.append(copy)
    summed[...] = dens[...] + other[...]
    place = recv[first[0]].astype(F32)
    oy = jnp.max(place[8:9, :]).astype(jnp.int32)
    ox = jnp.max(place[9:10, :]).astype(jnp.int32)
    chunks = torus_roll(lambda c: rho[pl.ds(c, N, stride=8), :], oy, ox)
    lane = lax.broadcasted_iota(jnp.int32, (N, 128), 1)
    low_half = lane < 64

    fetch.wait()
    fold = fixed[:, :256]
    unfold = fixed[:, 256:512]
    z_ahead = fixed[:G, 512:608]
    z_back = fixed[G : G + N, 512:704]
    stacked = jnp.concatenate(
        [jnp.concatenate([chunks[s], chunks[7 - s]], axis=1) for s in range(4)], axis=0
    )
    high, low = split(stacked)
    folded = dot(high, fold) + dot(low, fold)

    def regroup(tile, par_low, parts):
        first_part, second_part = parts
        if par_low:
            return jnp.where(low_half, first_part, pltpu.roll(second_part, 64, 1))
        return jnp.where(low_half, pltpu.roll(first_part, 64, 1), second_part)

    solved = []
    for par in range(4):
        c = 128 * (par // 2)
        pieces = [folded[N * s : N * s + N, c : c + 128] for s in range(4)]
        data = jnp.concatenate(
            [regroup(t, par % 2 == 0, pieces[2 * t : 2 * t + 2]) for t in range(2)], axis=1
        )
        high, low = split(data)
        copies[3 * par].wait()
        both = dot(jnp.concatenate([high, low], axis=0), ahead[par, 0])
        plane_waves = both[:N] + both[N:] + dot(high, ahead[par, 1])
        high, low = split(plane_waves)
        copies[3 * par + 1].wait()
        waves = dot(z_ahead, jnp.concatenate([high, high, low], axis=0)) * green[par]
        high, low = split(waves)
        levels = dot(z_back, jnp.concatenate([high, high, low], axis=0))
        high, low = split(levels)
        copies[3 * par + 2].wait()
        both = dot(jnp.concatenate([high, low], axis=0), back[par, 0])
        solved.append(both[:N] + both[N:] + dot(high, back[par, 1]))

    rows = []
    for s in range(4):
        t = 128 * (s // 2)
        tiles = []
        for half in range(2):
            even = solved[2 * half][:, t : t + 128]
            odd = solved[2 * half + 1][:, t : t + 128]
            tiles.append(regroup(half, s % 2 == 0, (even, odd)))
        rows.append(jnp.concatenate(tiles, axis=1))
    high, low = split(jnp.concatenate(rows, axis=0))
    spread = dot(high, unfold) + dot(low, unfold)
    field = [spread[N * s : N * s + N, :128] for s in range(4)] + [
        spread[N * s : N * s + N, 128:] for s in range(3, -1, -1)
    ]
    for s in range(8):
        boxed[s] = field[s]
    chunks = torus_roll(lambda c: boxed[c], B - lax.rem(oy, B), B - lax.rem(ox, B))
    for s in range(8):
        out[pl.ds(s, N, stride=8), :] = chunks[s]


def cube_root(value):
    rough = jnp.exp(jnp.log(jnp.where(value > 0.0, value, 1.0)) * (1.0 / 3.0))
    finer = rough - (rough - value / (rough * rough)) * (1.0 / 3.0)
    return jnp.where(value > 0.0, finer, 0.0)


def gradient_kernel(pairs, phi, code, field, plane, dens, near, far, nearer, out, terms):
    for n in range(N):
        terms[n] = jnp.zeros((8, 128), F32)
    for p in range(N):
        a = pairs[0, p]
        b = pairs[1, p]
        value = jnp.where(code[a] == code[b], field[p], 0.0)
        terms[a] = terms[a] + value * phi[b]
        terms[b] = terms[b] + value * phi[a]
    quarters = []
    for q in range(4):
        density = (dens[q] + far[q]) + (near[q] + nearer[q])
        quarters.append(plane[q] - EXCHANGE_COEF * cube_root(density))
    for n in range(N):
        quarter = code[n]
        local = jnp.where(
            quarter < 1.5,
            jnp.where(quarter < 0.5, quarters[0], quarters[1]),
            jnp.where(quarter < 2.5, quarters[2], quarters[3]),
        )
        out[n] = local * phi[n] - MIXING * terms[n]


def unpack_kernel(offsets, planes, out):
    chunks = torus_roll(
        lambda c: planes[pl.ds(c, N, stride=8), :], offsets[0, 0], offsets[0, 1]
    )
    for s in range(8):
        out[0, :, 128 * s : 128 * s + 128] = chunks[s]


def shape(dims, dtype=F32):
    return jax.ShapeDtypeStruct(dims, dtype)


def constants():
    cosine, sine = axis_basis()
    bases = [cosine[:HALF], sine[:HALF]]
    rows_y = np.stack([np.repeat(b, B, axis=1) for b in bases])
    rows_x = np.stack([np.tile(b, (1, B)) for b in bases])
    cols_y = np.stack([np.repeat(b.T, HALF, axis=1) for b in bases])
    cols_x = np.stack([np.tile(b.T, (1, HALF)) for b in bases])
    fold = fold_matrix()
    z_basis = np.concatenate([cosine, sine], axis=1)
    ahead_hi, ahead_lo = np_split(z_basis.T)
    back_hi, back_lo = np_split(z_basis)
    fixed = np.zeros((256, 768), jnp.bfloat16)
    fixed[:, :256] = fold
    fixed[:, 256:512] = fold.T
    fixed[:G, 512:608] = np.concatenate([ahead_hi, ahead_lo, ahead_hi], axis=1)
    fixed[G : G + N, 512:704] = np.concatenate([back_hi, back_lo, back_hi], axis=1)
    packed = np.concatenate(
        [
            rows_y.reshape(B, 1024),
            rows_x.reshape(B, 1024),
            np.concatenate([*cols_y, *cols_x], axis=1),
        ]
    )
    return jnp.asarray(packed.astype(np.float32)), jnp.asarray(fixed)


def exchange(x):
    return lax.all_to_all(x, "own", 0, 0, tiled=True)


def kernel(call, out_shape, in_specs, name, vmem, scratch=(), flops=0, moved=0):
    many = isinstance(out_shape, list)
    return pl.pallas_call(
        call,
        out_shape=out_shape,
        in_specs=in_specs,
        out_specs=[VM] * len(out_shape) if many else VM,
        scratch_shapes=scratch,
        compiler_params=pltpu.CompilerParams(vmem_limit_bytes=vmem << 20),
        cost_estimate=pl.CostEstimate(flops=flops, bytes_accessed=moved, transcendentals=0),
        name=name,
    )


def from_group(x, step):
    if step == 1:
        return lax.ppermute(x, "grp", [(g, g ^ 1) for g in range(8)])
    return lax.ppermute(x, "grp", [(g, (g + step) % 8) for g in range(8)])


def body(orbitals, offsets, pairs, ext_pot):
    owner = lax.axis_index("own")
    bases, fixed = constants()
    pairs = pairs.T

    sent = kernel(
        pack_kernel,
        shape((N, 16, 128), BF16),
        [SM, VM],
        "pack",
        60,
        [pltpu.VMEM((8 * N, 128), F32)],
        moved=200_000,
    )(offsets, orbitals)
    sent, bases, pairs, ext_pot = lax.optimization_barrier((sent, bases, pairs, ext_pot))
    recv = exchange(sent)

    tables = kernel(
        table_kernel,
        [shape((9, 256, 1024), BF16), shape((4, 2, 1024, 256), BF16), shape((4, 2 * G, 1024))],
        [VM, VM],
        "tables",
        60,
        flops=20_000_000,
        moved=10_000_000,
    )(bases, fixed)
    first = lax.dynamic_slice_in_dim(pairs, owner, 1, 1)[:1, 0]
    plane = lax.dynamic_slice_in_dim(ext_pot, owner, 1, 0).astype(F32)
    plane = plane.reshape(2, B, 2, B).transpose(0, 2, 1, 3).reshape(4, 8, 128)
    pairs = jnp.clip(pairs, 0, N - 1)
    recv, tables, first, plane, pairs = lax.optimization_barrier(
        (recv, tables, first, plane, pairs)
    )

    rho, dens, phi, code = kernel(
        pair_kernel,
        [shape((N, 8, 128)), shape((4, 8, 128)), shape((N, 8, 128)), shape((N, 8, 128))],
        [SM, VM],
        "pair_products",
        4,
        moved=600_000,
    )(pairs, recv)

    mine = exchange(rho)
    other = from_group(dens, 1)
    hbm = pl.BlockSpec(memory_space=pltpu.HBM)
    field, chip_dens = kernel(
        solve_kernel,
        [shape((8 * N, 128)), shape((4, 8, 128))],
        [SM] + [VM] * 4 + [hbm] * 3,
        "solve",
        52,
        [
            pltpu.VMEM((256, 1024), BF16),
            pltpu.VMEM((4, 2, 256, 1024), BF16),
            pltpu.VMEM((4, 2, 1024, 256), BF16),
            pltpu.VMEM((4, G, 1024), F32),
            pltpu.VMEM((8, N, 128), F32),
            pltpu.SemaphoreType.DMA((5, 3)),
        ],
        flops=1_000_000_000,
        moved=10_000_000,
    )(first, recv, mine.reshape(8 * N, 128), dens, other, *tables)
    fields = exchange(field.reshape(N, 8, 128))
    others = [from_group(chip_dens, step) for step in (2, 4, 6)]

    gradient = kernel(
        gradient_kernel,
        shape((N, 8, 128)),
        [SM] + [VM] * 8,
        "gradient_planes",
        4,
        [pltpu.VMEM((N, 8, 128), F32)],
        moved=600_000,
    )(pairs, phi, code, fields, plane, chip_dens, *others)
    back = exchange(gradient)

    return kernel(
        unpack_kernel, shape((1, BZ, B * B)), [SM, VM], "unpack", 4, moved=300_000
    )(offsets, back.reshape(8 * N, 128))


def solution(mesh):
    spec = P(("grp", "own"), None, None)
    in_specs = (spec, P(("grp", "own"), None), P("grp", None), P())
    return jax.shard_map(body, mesh=mesh, in_specs=in_specs, out_specs=spec, check_vma=False)
```

```python
import math

import jax
import jax.numpy as jnp
import numpy as np
from jax import lax
from jax.experimental import pallas as pl
from jax.experimental.pallas import tpu as pltpu
from jax.sharding import PartitionSpec as P

B = 32
BZ = 32
G = 64
N = 32
SCREEN = 0.0025
MIXING = 0.25
EXCHANGE_COEF = (3.0 / math.pi) ** (1.0 / 3.0)
F32 = jnp.float32
BF16 = jnp.bfloat16
VM = pl.BlockSpec(memory_space=pltpu.VMEM)
SM = pl.BlockSpec(memory_space=pltpu.SMEM)


def axis_basis():
    position = np.arange(B) - 15.5
    cosine = np.cos(2 * np.pi / G * np.outer(position, np.arange(B)))
    sine = np.sin(2 * np.pi / G * np.outer(position, np.arange(1, B + 1)))
    return cosine, sine


def split(value):
    high = value.astype(BF16)
    low = (value - high.astype(F32)).astype(BF16)
    return high, low


def np_split(value):
    value = value.astype(np.float32)
    high = value.astype(jnp.bfloat16)
    low = (value - high.astype(np.float32)).astype(jnp.bfloat16)
    return high, low


def dot(a, b):
    return jnp.dot(a, b, preferred_element_type=F32)


def torus_roll(load, by_y, by_x):
    lane = lax.broadcasted_iota(jnp.int32, (N, 128), 1)
    by_y = lax.rem(by_y, B)
    by_x = lax.rem(by_x, B)
    rows = lax.div(by_y, 4)
    rest = lax.rem(by_y, 4)
    shift = rest * B + by_x
    near = lax.rem(128 - shift, 128)
    far = lax.rem(128 + B - shift, 128)
    inside = lax.rem(lane, B) < B - by_x
    same = lax.div(lane, B) < 4 - rest
    moved = []
    for s in range(8):
        chunk = load(lax.rem(rows + s, 8))
        moved.append(
            jnp.where(inside, pltpu.roll(chunk, near, 1), pltpu.roll(chunk, far, 1))
        )
    return [jnp.where(same, moved[s], moved[(s + 1) % 8]) for s in range(8)]


def pack_kernel(offsets, box, out, planes):
    oy = offsets[0, 0]
    ox = offsets[0, 1]

    def load(c):
        return box[0, :, pl.ds(pl.multiple_of(c * 128, 128), 128)].astype(F32)

    chunks = torus_roll(load, B - lax.rem(oy, B), B - lax.rem(ox, B))
    for s in range(8):
        planes[pl.ds(s, N, stride=8), :] = chunks[s]
    row = lax.broadcasted_iota(jnp.int32, (8, 128), 0)
    extra = jnp.where(
        row == 0, oy.astype(F32), jnp.where(row == 1, ox.astype(F32), 0.0)
    )
    for z in range(N):
        both = jnp.concatenate([planes[8 * z : 8 * z + 8, :], extra], axis=0)
        out[z] = both.astype(BF16)


def pair_kernel(pairs, recv, rho, dens, phi, code):
    row = lax.broadcasted_iota(jnp.int32, (8, 128), 0)
    lane = lax.broadcasted_iota(jnp.int32, (8, 128), 1)
    y = (row * 4 + lax.div(lane, B)).astype(F32)
    x = lax.rem(lane, B).astype(F32)
    total = [jnp.zeros((8, 128), F32) for _ in range(4)]
    for n in range(N):
        value = recv[n].astype(F32)
        plane = value[:8]
        below = jnp.where(y < value[8:9], 2.0, 0.0)
        quarter = below + jnp.where(x < value[9:10], 1.0, 0.0)
        phi[n] = plane
        code[n] = quarter
        square = plane * plane
        for q in range(4):
            total[q] = total[q] + jnp.where(quarter == float(q), square, 0.0)
    for q in range(4):
        dens[q] = total[q]
    for p in range(N):
        a = pairs[0, p]
        b = pairs[1, p]
        rho[p] = jnp.where(code[a] == code[b], phi[a] * phi[b], 0.0)


def wave(index):
    return jnp.where(index < B, index, index - (B - 1))


def weigh(index, value):
    k = wave(index)
    return jnp.where((k == 0) | (k == B), value * 0.5, value)


def square(index):
    k = 2.0 * math.pi / G * wave(index).astype(F32)
    return k * k


def table_kernel(fixed_in, pairs_in, offsets_in, fixed, pairs, offsets, green):
    fixed[...] = fixed_in[...]
    pairs[...] = pairs_in[...]
    offsets[...] = offsets_in[...]
    ky = lax.broadcasted_iota(jnp.int32, (G, 256), 0)
    lane = lax.broadcasted_iota(jnp.int32, (G, 256), 1)
    kx = lax.rem(lane, G)
    level = square(ky) + square(kx) + SCREEN
    weight = weigh(ky, weigh(kx, jnp.full((G, 256), 4.0 * math.pi * 8.0 / G**3, F32)))
    top = lax.div(lax.broadcasted_iota(jnp.int32, (8, 256), 1), G)
    for part in range(16):
        kz = top + 4 * part
        factor = weigh(kz, jnp.ones((8, 256), F32))[:1]
        green[G * part : G * part + G, :] = weight * factor / (level + square(kz)[:1])


def exchange_groups(tiles):
    group = lax.div(lax.broadcasted_iota(jnp.int32, (8, 128), 1), B)
    low = group < 2
    even = lax.rem(group, 2) == 0
    t0, t1, t2, t3 = tiles

    def far(first, second):
        return (
            jnp.where(low, first, pltpu.roll(second, 64, 1)),
            jnp.where(low, pltpu.roll(first, 64, 1), second),
        )

    def near(first, second):
        return (
            jnp.where(even, first, pltpu.roll(second, 32, 1)),
            jnp.where(even, pltpu.roll(first, 96, 1), second),
        )

    u0, u2 = far(t0, t2)
    u1, u3 = far(t1, t3)
    v0, v1 = near(u0, u1)
    v2, v3 = near(u2, u3)
    return [v0, v1, v2, v3]


def thrice(value):
    high, low = split(value)
    return jnp.concatenate([high, high, low], axis=0)


def solve_kernel(owner, pairs, recv, rho, dens, other, fixed, green, out, summed, work):
    summed[...] = dens[...] + other[...]
    place = recv[pairs[0, owner[0]]].astype(F32)
    oy = jnp.max(place[8:9, :]).astype(jnp.int32)
    ox = jnp.max(place[9:10, :]).astype(jnp.int32)
    chunks = torus_roll(lambda c: rho[pl.ds(c, N, stride=8), :], oy, ox)

    waves = dot(fixed[:G, 768:864], thrice(jnp.concatenate(chunks, axis=1)))
    for s in range(8):
        work[pl.ds(s, G, stride=8), :] = waves[:, 128 * s : 128 * s + 128]

    ahead_y = fixed[G : 2 * G, 768:864]
    back_y = fixed[160:192, 768:960]
    for part in range(4):
        turned = []
        for c in range(4 * part, 4 * part + 4):
            tiles = [work[8 * k : 8 * k + 8, :] for k in range(4 * c, 4 * c + 4)]
            turned.append(jnp.concatenate(exchange_groups(tiles), axis=0))
        waves = dot(ahead_y, thrice(jnp.concatenate(turned, axis=1)))
        rows = jnp.concatenate([waves[:, 128 * c : 128 * c + 128] for c in range(4)], axis=0)
        high, low = split(rows)
        waves = dot(jnp.concatenate([high, low], axis=1), fixed[:, :256])
        waves = waves + dot(high, fixed[:128, 256:512])
        high, low = split(waves * green[256 * part : 256 * part + 256, :])
        both = dot(high, fixed[:, 512:768])
        rows = both[:, :128] + both[:, 128:] + dot(low, fixed[:, 512:640])
        levels = jnp.concatenate([rows[G * c : G * c + G, :] for c in range(4)], axis=1)
        levels = dot(back_y, thrice(levels))
        for c in range(4):
            tiles = [levels[8 * q : 8 * q + 8, 128 * c : 128 * c + 128] for q in range(4)]
            for i, tile in enumerate(exchange_groups(tiles)):
                k = 16 * part + 4 * c + i
                work[8 * k : 8 * k + 8, :] = tile

    levels = jnp.concatenate([work[pl.ds(s, G, stride=8), :] for s in range(8)], axis=1)
    field = dot(fixed[128:160, 768:960], thrice(levels))
    for s in range(8):
        work[N * s : N * s + N, :] = field[:, 128 * s : 128 * s + 128]

    def load(c):
        return work[pl.ds(pl.multiple_of(c * N, N), N), :]

    chunks = torus_roll(load, B - lax.rem(oy, B), B - lax.rem(ox, B))
    for s in range(8):
        out[pl.ds(s, N, stride=8), :] = chunks[s]


def cube_root(value):
    rough = jnp.exp(jnp.log(jnp.where(value > 0.0, value, 1.0)) * (1.0 / 3.0))
    finer = rough - (rough - value / (rough * rough)) * (1.0 / 3.0)
    return jnp.where(value > 0.0, finer, 0.0)


def gradient_kernel(pairs, phi, code, field, plane, dens, near, far, nearer, out, terms):
    for n in range(N):
        terms[n] = jnp.zeros((8, 128), F32)
    for p in range(N):
        a = pairs[0, p]
        b = pairs[1, p]
        value = jnp.where(code[a] == code[b], field[p], 0.0)
        terms[a] = terms[a] + value * phi[b]
        terms[b] = terms[b] + value * phi[a]
    quarters = []
    for q in range(4):
        density = (dens[q] + far[q]) + (near[q] + nearer[q])
        quarters.append(plane[q] - EXCHANGE_COEF * cube_root(density))
    for n in range(N):
        quarter = code[n]
        local = jnp.where(
            quarter < 1.5,
            jnp.where(quarter < 0.5, quarters[0], quarters[1]),
            jnp.where(quarter < 2.5, quarters[2], quarters[3]),
        )
        out[n] = local * phi[n] - MIXING * terms[n]


def unpack_kernel(offsets, planes, out):
    chunks = torus_roll(
        lambda c: planes[pl.ds(c, N, stride=8), :], offsets[0, 0], offsets[0, 1]
    )
    for s in range(8):
        out[0, :, 128 * s : 128 * s + 128] = chunks[s]


def shape(dims, dtype=F32):
    return jax.ShapeDtypeStruct(dims, dtype)


def constants():
    basis = np.concatenate(axis_basis(), axis=1)
    order = np.array([4 * s + q for q in range(4) for s in range(8)])

    def left(matrix):
        high, low = np_split(matrix)
        return np.concatenate([high, low, high], axis=1)

    high, low = np_split(np.kron(np.eye(4), basis))
    back_high, back_low = np_split(np.kron(np.eye(4), basis.T))
    fixed = np.zeros((256, 1024), jnp.bfloat16)
    fixed[:128, :256] = high
    fixed[128:, :256] = high
    fixed[:128, 256:512] = low
    fixed[:, 512:640] = back_high
    fixed[:, 640:768] = back_low
    fixed[:G, 768:864] = left(basis.T)
    fixed[G : 2 * G, 768:864] = left(basis[order].T)
    fixed[128:160, 768:960] = left(basis)
    fixed[160:192, 768:960] = left(basis[order])
    return jnp.asarray(fixed)


def exchange(x):
    return lax.all_to_all(x, "own", 0, 0, tiled=True)


def kernel(call, out_shape, in_specs, name, vmem, scratch=(), flops=0, moved=0):
    many = isinstance(out_shape, list)
    return pl.pallas_call(
        call,
        out_shape=out_shape,
        in_specs=in_specs,
        out_specs=[VM] * len(out_shape) if many else VM,
        scratch_shapes=scratch,
        compiler_params=pltpu.CompilerParams(vmem_limit_bytes=vmem << 20),
        cost_estimate=pl.CostEstimate(flops=flops, bytes_accessed=moved, transcendentals=0),
        name=name,
    )


def from_group(x, step):
    if step == 1:
        return lax.ppermute(x, "grp", [(g, g ^ 1) for g in range(8)])
    return lax.ppermute(x, "grp", [(g, (g + step) % 8) for g in range(8)])


def body(orbitals, offsets, pairs, ext_pot):
    owner = lax.axis_index("own")
    fixed = constants()
    pairs = pairs.T

    sent = kernel(
        pack_kernel,
        shape((N, 16, 128), BF16),
        [SM, VM],
        "pack",
        60,
        [pltpu.VMEM((8 * N, 128), F32)],
        moved=200_000,
    )(offsets, orbitals)
    sent, fixed, pairs, ext_pot = lax.optimization_barrier((sent, fixed, pairs, ext_pot))
    recv = exchange(sent)

    fixed, pairs, offsets, green = kernel(
        table_kernel,
        [
            shape((256, 1024), BF16),
            shape((2, N), jnp.int32),
            shape((1, 2), jnp.int32),
            shape((1024, 256)),
        ],
        [VM] * 3,
        "tables",
        16,
        flops=2_000_000,
        moved=3_000_000,
    )(fixed, pairs, offsets)
    plane = lax.dynamic_slice_in_dim(ext_pot, owner, 1, 0).astype(F32)
    plane = plane.reshape(2, B, 2, B).transpose(0, 2, 1, 3).reshape(4, 8, 128)
    recv, fixed, pairs, green, plane = lax.optimization_barrier(
        (recv, fixed, pairs, green, plane)
    )

    rho, dens, phi, code = kernel(
        pair_kernel,
        [shape((N, 8, 128)), shape((4, 8, 128)), shape((N, 8, 128)), shape((N, 8, 128))],
        [SM, VM],
        "pair_products",
        4,
        moved=600_000,
    )(pairs, recv)

    mine = exchange(rho)
    other = from_group(dens, 1)
    field, chip_dens = kernel(
        solve_kernel,
        [shape((8 * N, 128)), shape((4, 8, 128))],
        [SM, SM] + [VM] * 6,
        "solve",
        16,
        [pltpu.VMEM((8 * G, 128), F32)],
        flops=1_000_000_000,
        moved=3_000_000,
    )(owner.reshape(1), pairs, recv, mine.reshape(8 * N, 128), dens, other, fixed, green)
    fields = exchange(field.reshape(N, 8, 128))
    others = [from_group(chip_dens, step) for step in (2, 4, 6)]

    gradient = kernel(
        gradient_kernel,
        shape((N, 8, 128)),
        [SM] + [VM] * 8,
        "gradient_planes",
        4,
        [pltpu.VMEM((N, 8, 128), F32)],
        moved=600_000,
    )(pairs, phi, code, fields, plane, chip_dens, *others)
    back = exchange(gradient)

    return kernel(
        unpack_kernel, shape((1, BZ, B * B)), [SM, VM], "unpack", 4, moved=300_000
    )(offsets, back.reshape(8 * N, 128))


def solution(mesh):
    spec = P(("grp", "own"), None, None)
    in_specs = (spec, P(("grp", "own"), None), P("grp", None), P())
    return jax.shard_map(body, mesh=mesh, in_specs=in_specs, out_specs=spec, check_vma=False)
```

```python
import math

import jax
import jax.numpy as jnp
import numpy as np
from jax import lax
from jax.experimental import pallas as pl
from jax.experimental.pallas import tpu as pltpu
from jax.sharding import PartitionSpec as P

B = 32
BZ = 32
G = 64
N = 32
SCREEN = 0.0025
MIXING = 0.25
EXCHANGE_COEF = (3.0 / math.pi) ** (1.0 / 3.0)
F32 = jnp.float32
BF16 = jnp.bfloat16
VM = pl.BlockSpec(memory_space=pltpu.VMEM)
SM = pl.BlockSpec(memory_space=pltpu.SMEM)


def axis_basis():
    position = np.arange(B) - 15.5
    cosine = np.cos(2 * np.pi / G * np.outer(position, np.arange(B)))
    sine = np.sin(2 * np.pi / G * np.outer(position, np.arange(1, B + 1)))
    return cosine, sine


def split(value):
    high = value.astype(BF16)
    low = (value - high.astype(F32)).astype(BF16)
    return high, low


def np_split(value):
    value = value.astype(np.float32)
    high = value.astype(jnp.bfloat16)
    low = (value - high.astype(np.float32)).astype(jnp.bfloat16)
    return high, low


def dot(a, b):
    return jnp.dot(a, b, preferred_element_type=F32)


def torus_roll(load, by_y, by_x):
    lane = lax.broadcasted_iota(jnp.int32, (N, 128), 1)
    by_y = lax.rem(by_y, B)
    by_x = lax.rem(by_x, B)
    rows = lax.div(by_y, 4)
    rest = lax.rem(by_y, 4)
    shift = rest * B + by_x
    near = lax.rem(128 - shift, 128)
    far = lax.rem(128 + B - shift, 128)
    inside = lax.rem(lane, B) < B - by_x
    same = lax.div(lane, B) < 4 - rest
    moved = []
    for s in range(8):
        chunk = load(lax.rem(rows + s, 8))
        moved.append(
            jnp.where(inside, pltpu.roll(chunk, near, 1), pltpu.roll(chunk, far, 1))
        )
    return [jnp.where(same, moved[s], moved[(s + 1) % 8]) for s in range(8)]


def pack_kernel(offsets, box, out, planes):
    oy = offsets[0, 0]
    ox = offsets[0, 1]

    def load(c):
        return box[0, :, pl.ds(pl.multiple_of(c * 128, 128), 128)].astype(F32)

    chunks = torus_roll(load, B - lax.rem(oy, B), B - lax.rem(ox, B))
    for s in range(8):
        planes[pl.ds(s, N, stride=8), :] = chunks[s]
    row = lax.broadcasted_iota(jnp.int32, (8, 128), 0)
    extra = jnp.where(
        row == 0, oy.astype(F32), jnp.where(row == 1, ox.astype(F32), 0.0)
    )
    for z in range(N):
        both = jnp.concatenate([planes[8 * z : 8 * z + 8, :], extra], axis=0)
        out[z] = both.astype(BF16)


def pair_kernel(pairs, recv, rho, dens, phi, code):
    row = lax.broadcasted_iota(jnp.int32, (8, 128), 0)
    lane = lax.broadcasted_iota(jnp.int32, (8, 128), 1)
    y = (row * 4 + lax.div(lane, B)).astype(F32)
    x = lax.rem(lane, B).astype(F32)
    total = [jnp.zeros((8, 128), F32) for _ in range(4)]
    for n in range(N):
        value = recv[n].astype(F32)
        plane = value[:8]
        below = jnp.where(y < value[8:9], 2.0, 0.0)
        quarter = below + jnp.where(x < value[9:10], 1.0, 0.0)
        phi[n] = plane
        code[n] = quarter
        square = plane * plane
        for q in range(4):
            total[q] = total[q] + jnp.where(quarter == float(q), square, 0.0)
    for q in range(4):
        dens[q] = total[q]
    for p in range(N):
        a = pairs[0, p]
        b = pairs[1, p]
        rho[p] = jnp.where(code[a] == code[b], phi[a] * phi[b], 0.0)


def wave(index):
    return jnp.where(index < B, index, index - (B - 1))


def weigh(index, value):
    k = wave(index)
    return jnp.where((k == 0) | (k == B), value * 0.5, value)


def square(index):
    k = 2.0 * math.pi / G * wave(index).astype(F32)
    return k * k


def table_kernel(fixed_in, pairs_in, offsets_in, fixed, pairs, offsets, green):
    fixed[...] = fixed_in[...]
    pairs[...] = pairs_in[...]
    offsets[...] = offsets_in[...]
    ky = lax.broadcasted_iota(jnp.int32, (G, 256), 0)
    lane = lax.broadcasted_iota(jnp.int32, (G, 256), 1)
    kx = lax.rem(lane, G)
    level = square(ky) + square(kx) + SCREEN
    weight = weigh(ky, weigh(kx, jnp.full((G, 256), 4.0 * math.pi * 8.0 / G**3, F32)))
    top = lax.div(lax.broadcasted_iota(jnp.int32, (8, 256), 1), G)
    for part in range(16):
        kz = top + 4 * part
        factor = weigh(kz, jnp.ones((8, 256), F32))[:1]
        green[G * part : G * part + G, :] = weight * factor / (level + square(kz)[:1])


def exchange_groups(tiles):
    group = lax.div(lax.broadcasted_iota(jnp.int32, (8, 128), 1), B)
    low = group < 2
    even = lax.rem(group, 2) == 0
    t0, t1, t2, t3 = tiles

    def far(first, second):
        return (
            jnp.where(low, first, pltpu.roll(second, 64, 1)),
            jnp.where(low, pltpu.roll(first, 64, 1), second),
        )

    def near(first, second):
        return (
            jnp.where(even, first, pltpu.roll(second, 32, 1)),
            jnp.where(even, pltpu.roll(first, 96, 1), second),
        )

    u0, u2 = far(t0, t2)
    u1, u3 = far(t1, t3)
    v0, v1 = near(u0, u1)
    v2, v3 = near(u2, u3)
    return [v0, v1, v2, v3]


def thrice(value):
    high, low = split(value)
    return jnp.concatenate([high, high, low], axis=0)


def solve_kernel(owner, pairs, recv, rho, fixed, green, out, work):
    place = recv[pairs[0, owner[0]]].astype(F32)
    oy = jnp.max(place[8:9, :]).astype(jnp.int32)
    ox = jnp.max(place[9:10, :]).astype(jnp.int32)
    chunks = torus_roll(lambda c: rho[pl.ds(c, N, stride=8), :], oy, ox)

    waves = dot(fixed[:G, 768:864], thrice(jnp.concatenate(chunks, axis=1)))
    for s in range(8):
        work[pl.ds(s, G, stride=8), :] = waves[:, 128 * s : 128 * s + 128]

    ahead_y = fixed[G : 2 * G, 768:864]
    back_y = fixed[160:192, 768:960]
    for part in range(4):
        turned = []
        for c in range(4 * part, 4 * part + 4):
            tiles = [work[8 * k : 8 * k + 8, :] for k in range(4 * c, 4 * c + 4)]
            turned.append(jnp.concatenate(exchange_groups(tiles), axis=0))
        waves = dot(ahead_y, thrice(jnp.concatenate(turned, axis=1)))
        rows = jnp.concatenate([waves[:, 128 * c : 128 * c + 128] for c in range(4)], axis=0)
        high, low = split(rows)
        waves = dot(jnp.concatenate([high, low], axis=1), fixed[:, :256])
        waves = waves + dot(high, fixed[:128, 256:512])
        high, low = split(waves * green[256 * part : 256 * part + 256, :])
        both = dot(high, fixed[:, 512:768])
        rows = both[:, :128] + both[:, 128:] + dot(low, fixed[:, 512:640])
        levels = jnp.concatenate([rows[G * c : G * c + G, :] for c in range(4)], axis=1)
        levels = dot(back_y, thrice(levels))
        for c in range(4):
            tiles = [levels[8 * q : 8 * q + 8, 128 * c : 128 * c + 128] for q in range(4)]
            for i, tile in enumerate(exchange_groups(tiles)):
                k = 16 * part + 4 * c + i
                work[8 * k : 8 * k + 8, :] = tile

    levels = jnp.concatenate([work[pl.ds(s, G, stride=8), :] for s in range(8)], axis=1)
    field = dot(fixed[128:160, 768:960], thrice(levels))
    for s in range(8):
        work[N * s : N * s + N, :] = field[:, 128 * s : 128 * s + 128]

    def load(c):
        return work[pl.ds(pl.multiple_of(c * N, N), N), :]

    chunks = torus_roll(load, B - lax.rem(oy, B), B - lax.rem(ox, B))
    for s in range(8):
        out[pl.ds(s, N, stride=8), :] = chunks[s]


def cube_root(value):
    rough = jnp.exp(jnp.log(jnp.where(value > 0.0, value, 1.0)) * (1.0 / 3.0))
    finer = rough - (rough - value / (rough * rough)) * (1.0 / 3.0)
    return jnp.where(value > 0.0, finer, 0.0)


def gradient_kernel(pairs, phi, code, field, plane, dens, other, out, terms):
    for n in range(N):
        terms[n] = jnp.zeros((8, 128), F32)
    for p in range(N):
        a = pairs[0, p]
        b = pairs[1, p]
        value = jnp.where(code[a] == code[b], field[p], 0.0)
        terms[a] = terms[a] + value * phi[b]
        terms[b] = terms[b] + value * phi[a]
    quarters = []
    for q in range(4):
        quarters.append(plane[q] - EXCHANGE_COEF * cube_root(dens[q] + other[q]))
    for n in range(N):
        quarter = code[n]
        local = jnp.where(
            quarter < 1.5,
            jnp.where(quarter < 0.5, quarters[0], quarters[1]),
            jnp.where(quarter < 2.5, quarters[2], quarters[3]),
        )
        out[n] = local * phi[n] - MIXING * terms[n]


def unpack_kernel(offsets, planes, out):
    chunks = torus_roll(
        lambda c: planes[pl.ds(c, N, stride=8), :], offsets[0, 0], offsets[0, 1]
    )
    for s in range(8):
        out[0, :, 128 * s : 128 * s + 128] = chunks[s]


def shape(dims, dtype=F32):
    return jax.ShapeDtypeStruct(dims, dtype)


def constants():
    basis = np.concatenate(axis_basis(), axis=1)
    order = np.array([4 * s + q for q in range(4) for s in range(8)])

    def left(matrix):
        high, low = np_split(matrix)
        return np.concatenate([high, low, high], axis=1)

    high, low = np_split(np.kron(np.eye(4), basis))
    back_high, back_low = np_split(np.kron(np.eye(4), basis.T))
    fixed = np.zeros((256, 1024), jnp.bfloat16)
    fixed[:128, :256] = high
    fixed[128:, :256] = high
    fixed[:128, 256:512] = low
    fixed[:, 512:640] = back_high
    fixed[:, 640:768] = back_low
    fixed[:G, 768:864] = left(basis.T)
    fixed[G : 2 * G, 768:864] = left(basis[order].T)
    fixed[128:160, 768:960] = left(basis)
    fixed[160:192, 768:960] = left(basis[order])
    return jnp.asarray(fixed)


def exchange(x):
    return lax.all_to_all(x, "own", 0, 0, tiled=True)


def kernel(call, out_shape, in_specs, name, vmem, scratch=(), flops=0, moved=0):
    many = isinstance(out_shape, list)
    return pl.pallas_call(
        call,
        out_shape=out_shape,
        in_specs=in_specs,
        out_specs=[VM] * len(out_shape) if many else VM,
        scratch_shapes=scratch,
        compiler_params=pltpu.CompilerParams(vmem_limit_bytes=vmem << 20),
        cost_estimate=pl.CostEstimate(flops=flops, bytes_accessed=moved, transcendentals=0),
        name=name,
    )


def from_group(x, step):
    if step == 1:
        return lax.ppermute(x, "grp", [(g, g ^ 1) for g in range(8)])
    return lax.ppermute(x, "grp", [(g, (g + step) % 8) for g in range(8)])


def body(orbitals, offsets, pairs, ext_pot):
    owner = lax.axis_index("own")
    fixed = constants()
    pairs = pairs.T

    sent = kernel(
        pack_kernel,
        shape((N, 16, 128), BF16),
        [SM, VM],
        "pack",
        60,
        [pltpu.VMEM((8 * N, 128), F32)],
        moved=200_000,
    )(offsets, orbitals)
    sent, fixed, pairs, ext_pot = lax.optimization_barrier((sent, fixed, pairs, ext_pot))
    recv = exchange(sent)

    fixed, pairs, offsets, green = kernel(
        table_kernel,
        [
            shape((256, 1024), BF16),
            shape((2, N), jnp.int32),
            shape((1, 2), jnp.int32),
            shape((1024, 256)),
        ],
        [VM] * 3,
        "tables",
        16,
        flops=2_000_000,
        moved=3_000_000,
    )(fixed, pairs, offsets)
    plane = lax.dynamic_slice_in_dim(ext_pot, owner, 1, 0).astype(F32)
    plane = plane.reshape(2, B, 2, B).transpose(0, 2, 1, 3).reshape(4, 8, 128)
    recv, fixed, pairs, green, plane = lax.optimization_barrier(
        (recv, fixed, pairs, green, plane)
    )

    rho, dens, phi, code = kernel(
        pair_kernel,
        [shape((N, 8, 128)), shape((4, 8, 128)), shape((N, 8, 128)), shape((N, 8, 128))],
        [SM, VM],
        "pair_products",
        4,
        moved=600_000,
    )(pairs, recv)

    mine = exchange(rho)
    others = [from_group(dens, step) for step in (2, 4, 6)]
    field = kernel(
        solve_kernel,
        shape((8 * N, 128)),
        [SM, SM] + [VM] * 4,
        "solve",
        16,
        [pltpu.VMEM((8 * G, 128), F32)],
        flops=1_000_000_000,
        moved=3_000_000,
    )(owner.reshape(1), pairs, recv, mine.reshape(8 * N, 128), fixed, green)
    fields = exchange(field.reshape(N, 8, 128))
    dens = (dens + others[1]) + (others[0] + others[2])
    other = from_group(dens, 1)

    gradient = kernel(
        gradient_kernel,
        shape((N, 8, 128)),
        [SM] + [VM] * 6,
        "gradient_planes",
        4,
        [pltpu.VMEM((N, 8, 128), F32)],
        moved=600_000,
    )(pairs, phi, code, fields, plane, dens, other)
    back = exchange(gradient)

    return kernel(
        unpack_kernel, shape((1, BZ, B * B)), [SM, VM], "unpack", 4, moved=300_000
    )(offsets, back.reshape(8 * N, 128))


def solution(mesh):
    spec = P(("grp", "own"), None, None)
    in_specs = (spec, P(("grp", "own"), None), P("grp", None), P())
    return jax.shard_map(body, mesh=mesh, in_specs=in_specs, out_specs=spec, check_vma=False)
```

```python
import math

import jax
import jax.numpy as jnp
import numpy as np
from jax import lax
from jax.experimental import pallas as pl
from jax.experimental.pallas import tpu as pltpu
from jax.sharding import PartitionSpec as P

B = 32
BZ = 32
G = 64
N = 32
SCREEN = 0.0025
MIXING = 0.25
EXCHANGE_COEF = (3.0 / math.pi) ** (1.0 / 3.0)
F32 = jnp.float32
BF16 = jnp.bfloat16
VM = pl.BlockSpec(memory_space=pltpu.VMEM)
SM = pl.BlockSpec(memory_space=pltpu.SMEM)


def axis_basis():
    position = np.arange(B) - 15.5
    cosine = np.cos(2 * np.pi / G * np.outer(position, np.arange(B)))
    sine = np.sin(2 * np.pi / G * np.outer(position, np.arange(1, B + 1)))
    return cosine, sine


def split(value):
    high = value.astype(BF16)
    low = (value - high.astype(F32)).astype(BF16)
    return high, low


def np_split(value):
    value = value.astype(np.float32)
    high = value.astype(jnp.bfloat16)
    low = (value - high.astype(np.float32)).astype(jnp.bfloat16)
    return high, low


def dot(a, b):
    return jnp.dot(a, b, preferred_element_type=F32)


def torus_roll(load, by_y, by_x):
    lane = lax.broadcasted_iota(jnp.int32, (N, 128), 1)
    by_y = lax.rem(by_y, B)
    by_x = lax.rem(by_x, B)
    rows = lax.div(by_y, 4)
    rest = lax.rem(by_y, 4)
    shift = rest * B + by_x
    near = lax.rem(128 - shift, 128)
    far = lax.rem(128 + B - shift, 128)
    inside = lax.rem(lane, B) < B - by_x
    same = lax.div(lane, B) < 4 - rest
    moved = []
    for s in range(8):
        chunk = load(lax.rem(rows + s, 8))
        moved.append(
            jnp.where(inside, pltpu.roll(chunk, near, 1), pltpu.roll(chunk, far, 1))
        )
    return [jnp.where(same, moved[s], moved[(s + 1) % 8]) for s in range(8)]


def pack_kernel(offsets, box, out, planes):
    oy = offsets[0, 0]
    ox = offsets[0, 1]

    def load(c):
        return box[0, :, pl.ds(pl.multiple_of(c * 128, 128), 128)].astype(F32)

    chunks = torus_roll(load, B - lax.rem(oy, B), B - lax.rem(ox, B))
    for s in range(8):
        planes[pl.ds(s, N, stride=8), :] = chunks[s]
    row = lax.broadcasted_iota(jnp.int32, (8, 128), 0)
    extra = jnp.where(
        row == 0, oy.astype(F32), jnp.where(row == 1, ox.astype(F32), 0.0)
    )
    for z in range(N):
        both = jnp.concatenate([planes[8 * z : 8 * z + 8, :], extra], axis=0)
        out[z] = both.astype(BF16)


def pair_kernel(listed, recv, rho, dens, phi, code, place, pairs, sem):
    fetch = pltpu.make_async_copy(listed, pairs, sem)
    fetch.start()
    row = lax.broadcasted_iota(jnp.int32, (8, 128), 0)
    lane = lax.broadcasted_iota(jnp.int32, (8, 128), 1)
    y = (row * 4 + lax.div(lane, B)).astype(F32)
    x = lax.rem(lane, B).astype(F32)
    total = [jnp.zeros((8, 128), F32) for _ in range(4)]
    for n in range(N):
        value = recv[n].astype(F32)
        plane = value[:8]
        below = jnp.where(y < value[8:9], 2.0, 0.0)
        quarter = below + jnp.where(x < value[9:10], 1.0, 0.0)
        phi[n] = plane
        code[n] = quarter
        square = plane * plane
        for q in range(4):
            total[q] = total[q] + jnp.where(quarter == float(q), square, 0.0)
    for q in range(4):
        dens[q] = total[q]
    fetch.wait()
    place[...] = recv[pairs[0, pairs[2, 0]]].astype(F32)[8:]
    for p in range(N):
        a = pairs[0, p]
        b = pairs[1, p]
        rho[p] = jnp.where(code[a] == code[b], phi[a] * phi[b], 0.0)


def wave(index):
    return jnp.where(index < B, index, index - (B - 1))


def weigh(index, value):
    k = wave(index)
    return jnp.where((k == 0) | (k == B), value * 0.5, value)


def square(index):
    k = 2.0 * math.pi / G * wave(index).astype(F32)
    return k * k


def table_kernel(owner, corner, fixed_in, pairs_in, fixed, pairs, offsets, green):
    fixed[...] = fixed_in[...]
    pairs[...] = jnp.full((8, 128), owner[0], jnp.int32)
    pairs[:2, :N] = pairs_in[...]
    offsets[:1, :] = jnp.full((1, 128), corner[0, 0], jnp.int32)
    offsets[1:2, :] = jnp.full((1, 128), corner[0, 1], jnp.int32)
    ky = lax.broadcasted_iota(jnp.int32, (G, 256), 0)
    lane = lax.broadcasted_iota(jnp.int32, (G, 256), 1)
    kx = lax.rem(lane, G)
    level = square(ky) + square(kx) + SCREEN
    weight = weigh(ky, weigh(kx, jnp.full((G, 256), 4.0 * math.pi * 8.0 / G**3, F32)))
    top = lax.div(lax.broadcasted_iota(jnp.int32, (8, 256), 1), G)
    for part in range(16):
        kz = top + 4 * part
        factor = weigh(kz, jnp.ones((8, 256), F32))[:1]
        green[G * part : G * part + G, :] = weight * factor / (level + square(kz)[:1])


def exchange_groups(tiles):
    group = lax.div(lax.broadcasted_iota(jnp.int32, (8, 128), 1), B)
    low = group < 2
    even = lax.rem(group, 2) == 0
    t0, t1, t2, t3 = tiles

    def far(first, second):
        return (
            jnp.where(low, first, pltpu.roll(second, 64, 1)),
            jnp.where(low, pltpu.roll(first, 64, 1), second),
        )

    def near(first, second):
        return (
            jnp.where(even, first, pltpu.roll(second, 32, 1)),
            jnp.where(even, pltpu.roll(first, 96, 1), second),
        )

    u0, u2 = far(t0, t2)
    u1, u3 = far(t1, t3)
    v0, v1 = near(u0, u1)
    v2, v3 = near(u2, u3)
    return [v0, v1, v2, v3]


def thrice(value):
    high, low = split(value)
    return jnp.concatenate([high, high, low], axis=0)


def solve_kernel(place, rho, fixed, green, out, work):
    oy = jnp.max(place[0:1, :]).astype(jnp.int32)
    ox = jnp.max(place[1:2, :]).astype(jnp.int32)
    chunks = torus_roll(lambda c: rho[pl.ds(c, N, stride=8), :], oy, ox)

    waves = dot(fixed[:G, 768:864], thrice(jnp.concatenate(chunks, axis=1)))
    for s in range(8):
        work[pl.ds(s, G, stride=8), :] = waves[:, 128 * s : 128 * s + 128]

    ahead_y = fixed[G : 2 * G, 768:864]
    back_y = fixed[160:192, 768:960]
    turned = []
    for c in range(16):
        tiles = [work[8 * k : 8 * k + 8, :] for k in range(4 * c, 4 * c + 4)]
        turned.append(jnp.concatenate(exchange_groups(tiles), axis=0))
    waves = dot(ahead_y, thrice(jnp.concatenate(turned, axis=1)))
    rows = jnp.concatenate([waves[:, 128 * c : 128 * c + 128] for c in range(16)], axis=0)
    high, low = split(rows)
    waves = dot(jnp.concatenate([high, low], axis=1), fixed[:, :256])
    waves = waves + dot(high, fixed[:128, 256:512])
    high, low = split(waves * green[...])
    both = dot(high, fixed[:, 512:768])
    rows = both[:, :128] + both[:, 128:] + dot(low, fixed[:, 512:640])
    levels = jnp.concatenate([rows[G * c : G * c + G, :] for c in range(16)], axis=1)
    levels = dot(back_y, thrice(levels))
    for c in range(16):
        tiles = [levels[8 * q : 8 * q + 8, 128 * c : 128 * c + 128] for q in range(4)]
        for i, tile in enumerate(exchange_groups(tiles)):
            k = 4 * c + i
            work[8 * k : 8 * k + 8, :] = tile

    levels = jnp.concatenate([work[pl.ds(s, G, stride=8), :] for s in range(8)], axis=1)
    field = dot(fixed[128:160, 768:960], thrice(levels))
    for s in range(8):
        work[N * s : N * s + N, :] = field[:, 128 * s : 128 * s + 128]

    def load(c):
        return work[pl.ds(pl.multiple_of(c * N, N), N), :]

    chunks = torus_roll(load, B - lax.rem(oy, B), B - lax.rem(ox, B))
    for s in range(8):
        out[pl.ds(s, N, stride=8), :] = chunks[s]


def cube_root(value):
    rough = jnp.exp(jnp.log(jnp.where(value > 0.0, value, 1.0)) * (1.0 / 3.0))
    finer = rough - (rough - value / (rough * rough)) * (1.0 / 3.0)
    return jnp.where(value > 0.0, finer, 0.0)


def gradient_kernel(listed, phi, code, field, plane, dens, other, out, terms, pairs, sem):
    fetch = pltpu.make_async_copy(listed, pairs, sem)
    fetch.start()
    quarters = []
    for q in range(4):
        quarters.append(plane[q] - EXCHANGE_COEF * cube_root(dens[q] + other[q]))
    for n in range(N):
        terms[n] = jnp.zeros((8, 128), F32)
    fetch.wait()
    for p in range(N):
        a = pairs[0, p]
        b = pairs[1, p]
        value = jnp.where(code[a] == code[b], field[p], 0.0)
        terms[a] = terms[a] + value * phi[b]
        terms[b] = terms[b] + value * phi[a]
    for n in range(N):
        quarter = code[n]
        local = jnp.where(
            quarter < 1.5,
            jnp.where(quarter < 0.5, quarters[0], quarters[1]),
            jnp.where(quarter < 2.5, quarters[2], quarters[3]),
        )
        out[n] = local * phi[n] - MIXING * terms[n]


def unpack_kernel(offsets, planes, out):
    oy = jnp.max(offsets[0:1, :])
    ox = jnp.max(offsets[1:2, :])
    chunks = torus_roll(lambda c: planes[pl.ds(c, N, stride=8), :], oy, ox)
    for s in range(8):
        out[0, :, 128 * s : 128 * s + 128] = chunks[s]


def shape(dims, dtype=F32):
    return jax.ShapeDtypeStruct(dims, dtype)


def constants():
    basis = np.concatenate(axis_basis(), axis=1)
    order = np.array([4 * s + q for q in range(4) for s in range(8)])

    def left(matrix):
        high, low = np_split(matrix)
        return np.concatenate([high, low, high], axis=1)

    high, low = np_split(np.kron(np.eye(4), basis))
    back_high, back_low = np_split(np.kron(np.eye(4), basis.T))
    fixed = np.zeros((256, 1024), jnp.bfloat16)
    fixed[:128, :256] = high
    fixed[128:, :256] = high
    fixed[:128, 256:512] = low
    fixed[:, 512:640] = back_high
    fixed[:, 640:768] = back_low
    fixed[:G, 768:864] = left(basis.T)
    fixed[G : 2 * G, 768:864] = left(basis[order].T)
    fixed[128:160, 768:960] = left(basis)
    fixed[160:192, 768:960] = left(basis[order])
    return jnp.asarray(fixed)


def exchange(x):
    return lax.all_to_all(x, "own", 0, 0, tiled=True)


def kernel(call, out_shape, in_specs, name, vmem, scratch=(), flops=0, moved=0):
    many = isinstance(out_shape, list)
    return pl.pallas_call(
        call,
        out_shape=out_shape,
        in_specs=in_specs,
        out_specs=[VM] * len(out_shape) if many else VM,
        scratch_shapes=scratch,
        compiler_params=pltpu.CompilerParams(vmem_limit_bytes=vmem << 20),
        cost_estimate=pl.CostEstimate(flops=flops, bytes_accessed=moved, transcendentals=0),
        name=name,
    )


def from_group(x, step):
    if step == 1:
        return lax.ppermute(x, "grp", [(g, g ^ 1) for g in range(8)])
    return lax.ppermute(x, "grp", [(g, (g + step) % 8) for g in range(8)])


def body(orbitals, offsets, pairs, ext_pot):
    owner = lax.axis_index("own")
    fixed = constants()
    pairs = pairs.T

    sent = kernel(
        pack_kernel,
        shape((N, 16, 128), BF16),
        [SM, VM],
        "pack",
        60,
        [pltpu.VMEM((8 * N, 128), F32)],
        moved=200_000,
    )(offsets, orbitals)
    sent, fixed, pairs, ext_pot = lax.optimization_barrier((sent, fixed, pairs, ext_pot))
    recv = exchange(sent)

    fixed, pairs, offsets, green = kernel(
        table_kernel,
        [
            shape((256, 1024), BF16),
            shape((8, 128), jnp.int32),
            shape((8, 128), jnp.int32),
            shape((1024, 256)),
        ],
        [SM, SM, VM, VM],
        "tables",
        16,
        flops=2_000_000,
        moved=3_000_000,
    )(owner.reshape(1), offsets, fixed, pairs)
    plane = lax.dynamic_slice_in_dim(ext_pot, owner, 1, 0).astype(F32)
    plane = plane.reshape(2, B, 2, B).transpose(0, 2, 1, 3).reshape(4, 8, 128)
    recv, fixed, pairs, offsets, green, plane = lax.optimization_barrier(
        (recv, fixed, pairs, offsets, green, plane)
    )

    listing = [pltpu.SMEM((8, 128), jnp.int32), pltpu.SemaphoreType.DMA(())]
    planes = shape((N, 8, 128))
    rho, dens, phi, code, place = kernel(
        pair_kernel,
        [planes, shape((4, 8, 128)), planes, planes, shape((8, 128))],
        [VM, VM],
        "pair_products",
        4,
        listing,
        moved=600_000,
    )(pairs, recv)

    mine = exchange(rho)
    others = [from_group(dens, step) for step in (2, 4, 6)]
    field = kernel(
        solve_kernel,
        shape((8 * N, 128)),
        [VM] * 4,
        "solve",
        16,
        [pltpu.VMEM((8 * G, 128), F32)],
        flops=1_000_000_000,
        moved=3_000_000,
    )(place, mine.reshape(8 * N, 128), fixed, green)
    fields = exchange(field.reshape(N, 8, 128))
    dens = (dens + others[1]) + (others[0] + others[2])
    other = from_group(dens, 1)

    gradient = kernel(
        gradient_kernel,
        shape((N, 8, 128)),
        [VM] * 7,
        "gradient_planes",
        4,
        [pltpu.VMEM((N, 8, 128), F32)] + listing,
        moved=600_000,
    )(pairs, phi, code, fields, plane, dens, other)
    back = exchange(gradient)

    return kernel(
        unpack_kernel, shape((1, BZ, B * B)), [VM, VM], "unpack", 4, moved=300_000
    )(offsets, back.reshape(8 * N, 128))


def solution(mesh):
    spec = P(("grp", "own"), None, None)
    in_specs = (spec, P(("grp", "own"), None), P("grp", None), P())
    return jax.shard_map(body, mesh=mesh, in_specs=in_specs, out_specs=spec, check_vma=False)
```

```python
import math

import jax
import jax.numpy as jnp
import numpy as np
from jax import lax
from jax.experimental import pallas as pl
from jax.experimental.pallas import tpu as pltpu
from jax.sharding import PartitionSpec as P

B = 32
BZ = 32
G = 64
N = 32
SCREEN = 0.0025
MIXING = 0.25
EXCHANGE_COEF = (3.0 / math.pi) ** (1.0 / 3.0)
F32 = jnp.float32
BF16 = jnp.bfloat16
VM = pl.BlockSpec(memory_space=pltpu.VMEM)
SM = pl.BlockSpec(memory_space=pltpu.SMEM)


def axis_basis():
    position = np.arange(B) - 15.5
    cosine = np.cos(2 * np.pi / G * np.outer(position, np.arange(B)))
    sine = np.sin(2 * np.pi / G * np.outer(position, np.arange(1, B + 1)))
    return cosine, sine


def split(value):
    high = value.astype(BF16)
    low = (value - high.astype(F32)).astype(BF16)
    return high, low


def np_split(value):
    value = value.astype(np.float32)
    high = value.astype(jnp.bfloat16)
    low = (value - high.astype(np.float32)).astype(jnp.bfloat16)
    return high, low


def dot(a, b):
    return jnp.dot(a, b, preferred_element_type=F32)


def torus_roll(load, by_y, by_x):
    lane = lax.broadcasted_iota(jnp.int32, (N, 128), 1)
    by_y = lax.rem(by_y, B)
    by_x = lax.rem(by_x, B)
    rows = lax.div(by_y, 4)
    rest = lax.rem(by_y, 4)
    shift = rest * B + by_x
    near = lax.rem(128 - shift, 128)
    far = lax.rem(128 + B - shift, 128)
    inside = lax.rem(lane, B) < B - by_x
    same = lax.div(lane, B) < 4 - rest
    moved = []
    for s in range(8):
        chunk = load(lax.rem(rows + s, 8))
        moved.append(
            jnp.where(inside, pltpu.roll(chunk, near, 1), pltpu.roll(chunk, far, 1))
        )
    return [jnp.where(same, moved[s], moved[(s + 1) % 8]) for s in range(8)]


def pack_kernel(offsets, box, out, planes):
    oy = offsets[0, 0]
    ox = offsets[0, 1]

    def load(c):
        return box[0, :, pl.ds(pl.multiple_of(c * 128, 128), 128)].astype(F32)

    chunks = torus_roll(load, B - lax.rem(oy, B), B - lax.rem(ox, B))
    for s in range(8):
        planes[pl.ds(s, N, stride=8), :] = chunks[s]
    row = lax.broadcasted_iota(jnp.int32, (8, 128), 0)
    extra = jnp.where(
        row == 0, oy.astype(F32), jnp.where(row == 1, ox.astype(F32), 0.0)
    )
    for z in range(N):
        both = jnp.concatenate([planes[8 * z : 8 * z + 8, :], extra], axis=0)
        out[z] = both.astype(BF16)


def pair_numbers(pairs):
    words = [jnp.max(pairs[r : r + 1, 0:1]) for r in range(11)]
    numbers = []
    for p in range(N):
        pair = lax.shift_right_logical(words[p // 3], jnp.int32(10 * (p % 3)))
        second = lax.bitwise_and(pair, jnp.int32(31))
        first = lax.bitwise_and(lax.shift_right_logical(pair, jnp.int32(5)), jnp.int32(31))
        numbers.append((first, second))
    return numbers


def pair_kernel(pairs, recv, rho, dens, phi, code, place):
    numbers = pair_numbers(pairs)
    first = jnp.max(pairs[11:12, 0:1])
    row = lax.broadcasted_iota(jnp.int32, (8, 128), 0)
    lane = lax.broadcasted_iota(jnp.int32, (8, 128), 1)
    y = (row * 4 + lax.div(lane, B)).astype(F32)
    x = lax.rem(lane, B).astype(F32)
    total = [jnp.zeros((8, 128), F32) for _ in range(4)]
    for n in range(N):
        value = recv[n].astype(F32)
        plane = value[:8]
        below = jnp.where(y < value[8:9], 2.0, 0.0)
        quarter = below + jnp.where(x < value[9:10], 1.0, 0.0)
        phi[n] = plane
        code[n] = quarter
        square = plane * plane
        for q in range(4):
            total[q] = total[q] + jnp.where(quarter == float(q), square, 0.0)
    for q in range(4):
        dens[q] = total[q]
    place[...] = recv[first].astype(F32)[8:]
    for p in range(N):
        a, b = numbers[p]
        rho[p] = jnp.where(code[a] == code[b], phi[a] * phi[b], 0.0)


def wave(index):
    return jnp.where(index < B, index, index - (B - 1))


def weigh(index, value):
    k = wave(index)
    return jnp.where((k == 0) | (k == B), value * 0.5, value)


def square(index):
    k = 2.0 * math.pi / G * wave(index).astype(F32)
    return k * k


def table_kernel(owner, corner, fixed_in, pairs_in, fixed, pairs, offsets, green):
    fixed[...] = fixed_in[...]
    row = lax.broadcasted_iota(jnp.int32, (16, N), 0)
    spot = lax.broadcasted_iota(jnp.int32, (16, N), 1) - 3 * row
    both = pairs_in[0:1, :] * 32 + pairs_in[1:2, :]
    own = lax.broadcasted_iota(jnp.int32, (1, N), 1) == owner[0]
    word = jnp.max(jnp.where(own, pairs_in[0:1, :], 0), axis=1, keepdims=True)
    word = jnp.where(row[:, :1] == 11, word, 0)
    for i in range(3):
        part = jnp.max(jnp.where(spot == i, both, 0), axis=1, keepdims=True)
        word = word + part * (1024**i)
    pairs[...] = jnp.broadcast_to(word, (16, 128))
    offsets[:1, :] = jnp.full((1, 128), corner[0, 0], jnp.int32)
    offsets[1:2, :] = jnp.full((1, 128), corner[0, 1], jnp.int32)
    ky = lax.broadcasted_iota(jnp.int32, (G, 256), 0)
    lane = lax.broadcasted_iota(jnp.int32, (G, 256), 1)
    kx = lax.rem(lane, G)
    level = square(ky) + square(kx) + SCREEN
    weight = weigh(ky, weigh(kx, jnp.full((G, 256), 4.0 * math.pi * 8.0 / G**3, F32)))
    top = lax.div(lax.broadcasted_iota(jnp.int32, (8, 256), 1), G)
    for part in range(16):
        kz = top + 4 * part
        factor = weigh(kz, jnp.ones((8, 256), F32))[:1]
        green[G * part : G * part + G, :] = weight * factor / (level + square(kz)[:1])


def exchange_groups(tiles):
    group = lax.div(lax.broadcasted_iota(jnp.int32, (8, 128), 1), B)
    low = group < 2
    even = lax.rem(group, 2) == 0
    t0, t1, t2, t3 = tiles

    def far(first, second):
        return (
            jnp.where(low, first, pltpu.roll(second, 64, 1)),
            jnp.where(low, pltpu.roll(first, 64, 1), second),
        )

    def near(first, second):
        return (
            jnp.where(even, first, pltpu.roll(second, 32, 1)),
            jnp.where(even, pltpu.roll(first, 96, 1), second),
        )

    u0, u2 = far(t0, t2)
    u1, u3 = far(t1, t3)
    v0, v1 = near(u0, u1)
    v2, v3 = near(u2, u3)
    return [v0, v1, v2, v3]


def thrice(value):
    high, low = split(value)
    return jnp.concatenate([high, high, low], axis=0)


def solve_kernel(place, rho, fixed, green, out, work):
    oy = jnp.max(place[0:1, :]).astype(jnp.int32)
    ox = jnp.max(place[1:2, :]).astype(jnp.int32)
    chunks = torus_roll(lambda c: rho[pl.ds(c, N, stride=8), :], oy, ox)

    waves = dot(fixed[:G, 768:864], thrice(jnp.concatenate(chunks, axis=1)))
    for s in range(8):
        work[pl.ds(s, G, stride=8), :] = waves[:, 128 * s : 128 * s + 128]

    ahead_y = fixed[G : 2 * G, 768:864]
    back_y = fixed[160:192, 768:960]
    turned = []
    for c in range(16):
        tiles = [work[8 * k : 8 * k + 8, :] for k in range(4 * c, 4 * c + 4)]
        turned.append(jnp.concatenate(exchange_groups(tiles), axis=0))
    waves = dot(ahead_y, thrice(jnp.concatenate(turned, axis=1)))
    rows = jnp.concatenate([waves[:, 128 * c : 128 * c + 128] for c in range(16)], axis=0)
    high, low = split(rows)
    waves = dot(jnp.concatenate([high, low], axis=1), fixed[:, :256])
    waves = waves + dot(high, fixed[:128, 256:512])
    high, low = split(waves * green[...])
    both = dot(high, fixed[:, 512:768])
    rows = both[:, :128] + both[:, 128:] + dot(low, fixed[:, 512:640])
    levels = jnp.concatenate([rows[G * c : G * c + G, :] for c in range(16)], axis=1)
    levels = dot(back_y, thrice(levels))
    for c in range(16):
        tiles = [levels[8 * q : 8 * q + 8, 128 * c : 128 * c + 128] for q in range(4)]
        for i, tile in enumerate(exchange_groups(tiles)):
            k = 4 * c + i
            work[8 * k : 8 * k + 8, :] = tile

    levels = jnp.concatenate([work[pl.ds(s, G, stride=8), :] for s in range(8)], axis=1)
    field = dot(fixed[128:160, 768:960], thrice(levels))
    for s in range(8):
        work[N * s : N * s + N, :] = field[:, 128 * s : 128 * s + 128]

    def load(c):
        return work[pl.ds(pl.multiple_of(c * N, N), N), :]

    chunks = torus_roll(load, B - lax.rem(oy, B), B - lax.rem(ox, B))
    for s in range(8):
        out[pl.ds(s, N, stride=8), :] = chunks[s]


def cube_root(value):
    rough = jnp.exp(jnp.log(jnp.where(value > 0.0, value, 1.0)) * (1.0 / 3.0))
    finer = rough - (rough - value / (rough * rough)) * (1.0 / 3.0)
    return jnp.where(value > 0.0, finer, 0.0)


def gradient_kernel(pairs, phi, code, field, plane, dens, other, out, terms):
    numbers = pair_numbers(pairs)
    quarters = []
    for q in range(4):
        quarters.append(plane[q] - EXCHANGE_COEF * cube_root(dens[q] + other[q]))
    for n in range(N):
        terms[n] = jnp.zeros((8, 128), F32)
    for p in range(N):
        a, b = numbers[p]
        value = jnp.where(code[a] == code[b], field[p], 0.0)
        terms[a] = terms[a] + value * phi[b]
        terms[b] = terms[b] + value * phi[a]
    for n in range(N):
        quarter = code[n]
        local = jnp.where(
            quarter < 1.5,
            jnp.where(quarter < 0.5, quarters[0], quarters[1]),
            jnp.where(quarter < 2.5, quarters[2], quarters[3]),
        )
        out[n] = local * phi[n] - MIXING * terms[n]


def unpack_kernel(offsets, planes, out):
    oy = jnp.max(offsets[0:1, :])
    ox = jnp.max(offsets[1:2, :])
    chunks = torus_roll(lambda c: planes[pl.ds(c, N, stride=8), :], oy, ox)
    for s in range(8):
        out[0, :, 128 * s : 128 * s + 128] = chunks[s]


def shape(dims, dtype=F32):
    return jax.ShapeDtypeStruct(dims, dtype)


def constants():
    basis = np.concatenate(axis_basis(), axis=1)
    order = np.array([4 * s + q for q in range(4) for s in range(8)])

    def left(matrix):
        high, low = np_split(matrix)
        return np.concatenate([high, low, high], axis=1)

    high, low = np_split(np.kron(np.eye(4), basis))
    back_high, back_low = np_split(np.kron(np.eye(4), basis.T))
    fixed = np.zeros((256, 1024), jnp.bfloat16)
    fixed[:128, :256] = high
    fixed[128:, :256] = high
    fixed[:128, 256:512] = low
    fixed[:, 512:640] = back_high
    fixed[:, 640:768] = back_low
    fixed[:G, 768:864] = left(basis.T)
    fixed[G : 2 * G, 768:864] = left(basis[order].T)
    fixed[128:160, 768:960] = left(basis)
    fixed[160:192, 768:960] = left(basis[order])
    return jnp.asarray(fixed)


def exchange(x):
    return lax.all_to_all(x, "own", 0, 0, tiled=True)


def kernel(call, out_shape, in_specs, name, vmem, scratch=(), flops=0, moved=0):
    many = isinstance(out_shape, list)
    return pl.pallas_call(
        call,
        out_shape=out_shape,
        in_specs=in_specs,
        out_specs=[VM] * len(out_shape) if many else VM,
        scratch_shapes=scratch,
        compiler_params=pltpu.CompilerParams(vmem_limit_bytes=vmem << 20),
        cost_estimate=pl.CostEstimate(flops=flops, bytes_accessed=moved, transcendentals=0),
        name=name,
    )


def from_group(x, step):
    if step == 1:
        return lax.ppermute(x, "grp", [(g, g ^ 1) for g in range(8)])
    return lax.ppermute(x, "grp", [(g, (g + step) % 8) for g in range(8)])


def body(orbitals, offsets, pairs, ext_pot):
    owner = lax.axis_index("own")
    fixed = constants()
    pairs = pairs.T

    sent = kernel(
        pack_kernel,
        shape((N, 16, 128), BF16),
        [SM, VM],
        "pack",
        60,
        [pltpu.VMEM((8 * N, 128), F32)],
        moved=200_000,
    )(offsets, orbitals)
    sent, fixed, pairs, ext_pot = lax.optimization_barrier((sent, fixed, pairs, ext_pot))
    recv = exchange(sent)

    fixed, pairs, offsets, green = kernel(
        table_kernel,
        [
            shape((256, 1024), BF16),
            shape((16, 128), jnp.int32),
            shape((8, 128), jnp.int32),
            shape((1024, 256)),
        ],
        [SM, SM, VM, VM],
        "tables",
        16,
        flops=2_000_000,
        moved=3_000_000,
    )(owner.reshape(1), offsets, fixed, pairs)
    plane = lax.dynamic_slice_in_dim(ext_pot, owner, 1, 0).astype(F32)
    plane = plane.reshape(2, B, 2, B).transpose(0, 2, 1, 3).reshape(4, 8, 128)
    recv, fixed, pairs, offsets, green, plane = lax.optimization_barrier(
        (recv, fixed, pairs, offsets, green, plane)
    )

    planes = shape((N, 8, 128))
    rho, dens, phi, code, place = kernel(
        pair_kernel,
        [planes, shape((4, 8, 128)), planes, planes, shape((8, 128))],
        [VM, VM],
        "pair_products",
        4,
        moved=600_000,
    )(pairs, recv)

    mine = exchange(rho)
    others = [from_group(dens, step) for step in (2, 4, 6)]
    field = kernel(
        solve_kernel,
        shape((8 * N, 128)),
        [VM] * 4,
        "solve",
        16,
        [pltpu.VMEM((8 * G, 128), F32)],
        flops=1_000_000_000,
        moved=3_000_000,
    )(place, mine.reshape(8 * N, 128), fixed, green)
    fields = exchange(field.reshape(N, 8, 128))
    dens = (dens + others[1]) + (others[0] + others[2])
    other = from_group(dens, 1)

    gradient = kernel(
        gradient_kernel,
        shape((N, 8, 128)),
        [VM] * 7,
        "gradient_planes",
        4,
        [pltpu.VMEM((N, 8, 128), F32)],
        moved=600_000,
    )(pairs, phi, code, fields, plane, dens, other)
    back = exchange(gradient)

    return kernel(
        unpack_kernel, shape((1, BZ, B * B)), [VM, VM], "unpack", 4, moved=300_000
    )(offsets, back.reshape(8 * N, 128))


def solution(mesh):
    spec = P(("grp", "own"), None, None)
    in_specs = (spec, P(("grp", "own"), None), P("grp", None), P())
    return jax.shard_map(body, mesh=mesh, in_specs=in_specs, out_specs=spec, check_vma=False)
```

```python
import math

import jax
import jax.numpy as jnp
import numpy as np
from jax import lax
from jax.experimental import pallas as pl
from jax.experimental.pallas import tpu as pltpu
from jax.sharding import PartitionSpec as P

B = 32
BZ = 32
G = 64
N = 32
SCREEN = 0.0025
MIXING = 0.25
EXCHANGE_COEF = (3.0 / math.pi) ** (1.0 / 3.0)
F32 = jnp.float32
BF16 = jnp.bfloat16
VM = pl.BlockSpec(memory_space=pltpu.VMEM)
SM = pl.BlockSpec(memory_space=pltpu.SMEM)


def axis_basis():
    position = np.arange(B) - 15.5
    cosine = np.cos(2 * np.pi / G * np.outer(position, np.arange(B)))
    sine = np.sin(2 * np.pi / G * np.outer(position, np.arange(1, B + 1)))
    return cosine, sine


def split(value):
    high = value.astype(BF16)
    low = (value - high.astype(F32)).astype(BF16)
    return high, low


def np_split(value):
    value = value.astype(np.float32)
    high = value.astype(jnp.bfloat16)
    low = (value - high.astype(np.float32)).astype(jnp.bfloat16)
    return high, low


def dot(a, b):
    return jnp.dot(a, b, preferred_element_type=F32)


def torus_roll(load, by_y, by_x):
    lane = lax.broadcasted_iota(jnp.int32, (N, 128), 1)
    by_y = lax.rem(by_y, B)
    by_x = lax.rem(by_x, B)
    rows = lax.div(by_y, 4)
    rest = lax.rem(by_y, 4)
    shift = rest * B + by_x
    near = lax.rem(128 - shift, 128)
    far = lax.rem(128 + B - shift, 128)
    inside = lax.rem(lane, B) < B - by_x
    same = lax.div(lane, B) < 4 - rest
    moved = []
    for s in range(8):
        chunk = load(lax.rem(rows + s, 8))
        moved.append(
            jnp.where(inside, pltpu.roll(chunk, near, 1), pltpu.roll(chunk, far, 1))
        )
    return [jnp.where(same, moved[s], moved[(s + 1) % 8]) for s in range(8)]


def pack_kernel(offsets, box, out, planes):
    oy = offsets[0, 0]
    ox = offsets[0, 1]

    def load(c):
        return box[0, :, pl.ds(pl.multiple_of(c * 128, 128), 128)].astype(F32)

    chunks = torus_roll(load, B - lax.rem(oy, B), B - lax.rem(ox, B))
    for s in range(8):
        planes[pl.ds(s, N, stride=8), :] = chunks[s]
    row = lax.broadcasted_iota(jnp.int32, (8, 128), 0)
    extra = jnp.where(
        row == 0, oy.astype(F32), jnp.where(row == 1, ox.astype(F32), 0.0)
    )
    for z in range(N):
        both = jnp.concatenate([planes[8 * z : 8 * z + 8, :], extra], axis=0)
        out[z] = both.astype(BF16)


def pair_numbers(pairs):
    words = [jnp.max(pairs[r : r + 1, 0:1]) for r in range(11)]
    numbers = []
    for p in range(N):
        pair = lax.shift_right_logical(words[p // 3], jnp.int32(10 * (p % 3)))
        second = lax.bitwise_and(pair, jnp.int32(31))
        first = lax.bitwise_and(lax.shift_right_logical(pair, jnp.int32(5)), jnp.int32(31))
        numbers.append((first, second))
    return numbers


def pair_kernel(pairs, recv, rho, dens, phi, code, place):
    numbers = pair_numbers(pairs)
    first = jnp.max(pairs[11:12, 0:1])
    row = lax.broadcasted_iota(jnp.int32, (8, 128), 0)
    lane = lax.broadcasted_iota(jnp.int32, (8, 128), 1)
    y = (row * 4 + lax.div(lane, B)).astype(F32)
    x = lax.rem(lane, B).astype(F32)
    total = [jnp.zeros((8, 128), F32) for _ in range(4)]
    for n in range(N):
        value = recv[n].astype(F32)
        plane = value[:8]
        below = jnp.where(y < value[8:9], 2.0, 0.0)
        quarter = below + jnp.where(x < value[9:10], 1.0, 0.0)
        phi[n] = plane
        code[n] = quarter
        square = plane * plane
        for q in range(4):
            total[q] = total[q] + jnp.where(quarter == float(q), square, 0.0)
    for q in range(4):
        dens[q] = total[q]
    place[...] = recv[first].astype(F32)[8:]
    for p in range(N):
        a, b = numbers[p]
        rho[p] = jnp.where(code[a] == code[b], phi[a] * phi[b], 0.0)


def wave(index):
    return jnp.where(index < B, index, index - (B - 1))


def weigh(index, value):
    k = wave(index)
    return jnp.where((k == 0) | (k == B), value * 0.5, value)


def square(index):
    k = 2.0 * math.pi / G * wave(index).astype(F32)
    return k * k


def table_kernel(owner, corner, fixed_in, pairs_in, fixed, pairs, offsets, green):
    fixed[...] = fixed_in[...]
    row = lax.broadcasted_iota(jnp.int32, (16, N), 0)
    spot = lax.broadcasted_iota(jnp.int32, (16, N), 1) - 3 * row
    both = pairs_in[0:1, :] * 32 + pairs_in[1:2, :]
    own = lax.broadcasted_iota(jnp.int32, (1, N), 1) == owner[0]
    word = jnp.max(jnp.where(own, pairs_in[0:1, :], 0), axis=1, keepdims=True)
    word = jnp.where(row[:, :1] == 11, word, 0)
    for i in range(3):
        part = jnp.max(jnp.where(spot == i, both, 0), axis=1, keepdims=True)
        word = word + part * (1024**i)
    pairs[...] = jnp.broadcast_to(word, (16, 128))
    offsets[:1, :] = jnp.full((1, 128), corner[0, 0], jnp.int32)
    offsets[1:2, :] = jnp.full((1, 128), corner[0, 1], jnp.int32)
    ky = lax.broadcasted_iota(jnp.int32, (G, 256), 0)
    lane = lax.broadcasted_iota(jnp.int32, (G, 256), 1)
    kx = lax.rem(lane, G)
    level = square(ky) + square(kx) + SCREEN
    weight = weigh(ky, weigh(kx, jnp.full((G, 256), 4.0 * math.pi * 8.0 / G**3, F32)))
    top = lax.div(lax.broadcasted_iota(jnp.int32, (8, 256), 1), G)
    for part in range(16):
        kz = top + 4 * part
        factor = weigh(kz, jnp.ones((8, 256), F32))[:1]
        green[G * part : G * part + G, :] = weight * factor / (level + square(kz)[:1])


def exchange_groups(tiles):
    group = lax.div(lax.broadcasted_iota(jnp.int32, (8, 128), 1), B)
    low = group < 2
    even = lax.rem(group, 2) == 0
    t0, t1, t2, t3 = tiles

    def far(first, second):
        return (
            jnp.where(low, first, pltpu.roll(second, 64, 1)),
            jnp.where(low, pltpu.roll(first, 64, 1), second),
        )

    def near(first, second):
        return (
            jnp.where(even, first, pltpu.roll(second, 32, 1)),
            jnp.where(even, pltpu.roll(first, 96, 1), second),
        )

    u0, u2 = far(t0, t2)
    u1, u3 = far(t1, t3)
    v0, v1 = near(u0, u1)
    v2, v3 = near(u2, u3)
    return [v0, v1, v2, v3]


def thrice(value):
    high, low = split(value)
    return jnp.concatenate([high, high, low], axis=0)


def turn(table, wave_index, cell, start):
    odd = lax.rem(wave(wave_index), 2) == 1
    return jnp.where(odd & (cell < start), -table.astype(F32), table.astype(F32)).astype(BF16)


def solve_kernel(place, rho, fixed, green, out, work):
    oy = jnp.max(place[0:1, :]).astype(jnp.int32)
    ox = jnp.max(place[1:2, :]).astype(jnp.int32)

    def index(dims, axis):
        return lax.broadcasted_iota(jnp.int32, dims, axis)

    def row_of(k):
        k = lax.rem(k, B)
        return lax.rem(k, 8) * 4 + lax.div(k, 8)

    ahead_y = turn(
        fixed[G : 2 * G, 768:864], index((G, 96), 0), row_of(index((G, 96), 1)), oy
    )
    back_y = turn(
        fixed[160:192, 768:960],
        lax.rem(index((N, 192), 1), G),
        row_of(index((N, 192), 0)),
        oy,
    )
    square = (256, 256)
    wave_x = lax.rem(index(square, 1), G)
    cell_x = lax.rem(index(square, 0), B)
    ahead_x = turn(fixed[:, :256], wave_x, cell_x, ox)
    ahead_x_low = turn(fixed[:128, 256:512], wave_x[:128], cell_x[:128], ox)
    wave_x = lax.rem(index(square, 0), G)
    cell_x = lax.rem(index(square, 1), B)
    back_x = turn(fixed[:, 512:768], wave_x, cell_x, ox)

    chunks = [rho[pl.ds(s, N, stride=8), :] for s in range(8)]
    waves = dot(fixed[:G, 768:864], thrice(jnp.concatenate(chunks, axis=1)))
    for s in range(8):
        work[pl.ds(s, G, stride=8), :] = waves[:, 128 * s : 128 * s + 128]

    turned = []
    for c in range(16):
        tiles = [work[8 * k : 8 * k + 8, :] for k in range(4 * c, 4 * c + 4)]
        turned.append(jnp.concatenate(exchange_groups(tiles), axis=0))
    waves = dot(ahead_y, thrice(jnp.concatenate(turned, axis=1)))
    rows = jnp.concatenate([waves[:, 128 * c : 128 * c + 128] for c in range(16)], axis=0)
    high, low = split(rows)
    waves = dot(jnp.concatenate([high, low], axis=1), ahead_x)
    waves = waves + dot(high, ahead_x_low)
    high, low = split(waves * green[...])
    both = dot(high, back_x)
    rows = both[:, :128] + both[:, 128:] + dot(low, back_x[:, :128])
    levels = jnp.concatenate([rows[G * c : G * c + G, :] for c in range(16)], axis=1)
    levels = dot(back_y, thrice(levels))
    for c in range(16):
        tiles = [levels[8 * q : 8 * q + 8, 128 * c : 128 * c + 128] for q in range(4)]
        for i, tile in enumerate(exchange_groups(tiles)):
            k = 4 * c + i
            work[8 * k : 8 * k + 8, :] = tile

    levels = jnp.concatenate([work[pl.ds(s, G, stride=8), :] for s in range(8)], axis=1)
    field = dot(fixed[128:160, 768:960], thrice(levels))
    for s in range(8):
        out[pl.ds(s, N, stride=8), :] = field[:, 128 * s : 128 * s + 128]


def cube_root(value):
    rough = jnp.exp(jnp.log(jnp.where(value > 0.0, value, 1.0)) * (1.0 / 3.0))
    finer = rough - (rough - value / (rough * rough)) * (1.0 / 3.0)
    return jnp.where(value > 0.0, finer, 0.0)


def gradient_kernel(pairs, phi, code, field, plane, dens, other, out, terms):
    numbers = pair_numbers(pairs)
    quarters = []
    for q in range(4):
        quarters.append(plane[q] - EXCHANGE_COEF * cube_root(dens[q] + other[q]))
    for n in range(N):
        terms[n] = jnp.zeros((8, 128), F32)
    for p in range(N):
        a, b = numbers[p]
        value = jnp.where(code[a] == code[b], field[p], 0.0)
        terms[a] = terms[a] + value * phi[b]
        terms[b] = terms[b] + value * phi[a]
    for n in range(N):
        quarter = code[n]
        local = jnp.where(
            quarter < 1.5,
            jnp.where(quarter < 0.5, quarters[0], quarters[1]),
            jnp.where(quarter < 2.5, quarters[2], quarters[3]),
        )
        out[n] = local * phi[n] - MIXING * terms[n]


def unpack_kernel(offsets, planes, out):
    oy = jnp.max(offsets[0:1, :])
    ox = jnp.max(offsets[1:2, :])
    chunks = torus_roll(lambda c: planes[pl.ds(c, N, stride=8), :], oy, ox)
    for s in range(8):
        out[0, :, 128 * s : 128 * s + 128] = chunks[s]


def shape(dims, dtype=F32):
    return jax.ShapeDtypeStruct(dims, dtype)


def constants():
    basis = np.concatenate(axis_basis(), axis=1)
    order = np.array([4 * s + q for q in range(4) for s in range(8)])

    def left(matrix):
        high, low = np_split(matrix)
        return np.concatenate([high, low, high], axis=1)

    high, low = np_split(np.kron(np.eye(4), basis))
    back_high, back_low = np_split(np.kron(np.eye(4), basis.T))
    fixed = np.zeros((256, 1024), jnp.bfloat16)
    fixed[:128, :256] = high
    fixed[128:, :256] = high
    fixed[:128, 256:512] = low
    fixed[:, 512:640] = back_high
    fixed[:, 640:768] = back_low
    fixed[:G, 768:864] = left(basis.T)
    fixed[G : 2 * G, 768:864] = left(basis[order].T)
    fixed[128:160, 768:960] = left(basis)
    fixed[160:192, 768:960] = left(basis[order])
    return jnp.asarray(fixed)


def exchange(x):
    return lax.all_to_all(x, "own", 0, 0, tiled=True)


def kernel(call, out_shape, in_specs, name, vmem, scratch=(), flops=0, moved=0):
    many = isinstance(out_shape, list)
    return pl.pallas_call(
        call,
        out_shape=out_shape,
        in_specs=in_specs,
        out_specs=[VM] * len(out_shape) if many else VM,
        scratch_shapes=scratch,
        compiler_params=pltpu.CompilerParams(vmem_limit_bytes=vmem << 20),
        cost_estimate=pl.CostEstimate(flops=flops, bytes_accessed=moved, transcendentals=0),
        name=name,
    )


def from_group(x, step):
    if step == 1:
        return lax.ppermute(x, "grp", [(g, g ^ 1) for g in range(8)])
    return lax.ppermute(x, "grp", [(g, (g + step) % 8) for g in range(8)])


def body(orbitals, offsets, pairs, ext_pot):
    owner = lax.axis_index("own")
    fixed = constants()
    pairs = pairs.T

    sent = kernel(
        pack_kernel,
        shape((N, 16, 128), BF16),
        [SM, VM],
        "pack",
        60,
        [pltpu.VMEM((8 * N, 128), F32)],
        moved=200_000,
    )(offsets, orbitals)
    sent, fixed, pairs, ext_pot = lax.optimization_barrier((sent, fixed, pairs, ext_pot))
    recv = exchange(sent)

    fixed, pairs, offsets, green = kernel(
        table_kernel,
        [
            shape((256, 1024), BF16),
            shape((16, 128), jnp.int32),
            shape((8, 128), jnp.int32),
            shape((1024, 256)),
        ],
        [SM, SM, VM, VM],
        "tables",
        16,
        flops=2_000_000,
        moved=3_000_000,
    )(owner.reshape(1), offsets, fixed, pairs)
    plane = lax.dynamic_slice_in_dim(ext_pot, owner, 1, 0).astype(F32)
    plane = plane.reshape(2, B, 2, B).transpose(0, 2, 1, 3).reshape(4, 8, 128)
    recv, fixed, pairs, offsets, green, plane = lax.optimization_barrier(
        (recv, fixed, pairs, offsets, green, plane)
    )

    planes = shape((N, 8, 128))
    rho, dens, phi, code, place = kernel(
        pair_kernel,
        [planes, shape((4, 8, 128)), planes, planes, shape((8, 128))],
        [VM, VM],
        "pair_products",
        4,
        moved=600_000,
    )(pairs, recv)

    mine = exchange(rho)
    others = [from_group(dens, step) for step in (2, 4, 6)]
    field = kernel(
        solve_kernel,
        shape((8 * N, 128)),
        [VM] * 4,
        "solve",
        16,
        [pltpu.VMEM((8 * G, 128), F32)],
        flops=1_000_000_000,
        moved=3_000_000,
    )(place, mine.reshape(8 * N, 128), fixed, green)
    fields = exchange(field.reshape(N, 8, 128))
    dens = (dens + others[1]) + (others[0] + others[2])
    other = from_group(dens, 1)

    gradient = kernel(
        gradient_kernel,
        shape((N, 8, 128)),
        [VM] * 7,
        "gradient_planes",
        4,
        [pltpu.VMEM((N, 8, 128), F32)],
        moved=600_000,
    )(pairs, phi, code, fields, plane, dens, other)
    back = exchange(gradient)

    return kernel(
        unpack_kernel, shape((1, BZ, B * B)), [VM, VM], "unpack", 4, moved=300_000
    )(offsets, back.reshape(8 * N, 128))


def solution(mesh):
    spec = P(("grp", "own"), None, None)
    in_specs = (spec, P(("grp", "own"), None), P("grp", None), P())
    return jax.shard_map(body, mesh=mesh, in_specs=in_specs, out_specs=spec, check_vma=False)
```

```python
import math

import jax
import jax.numpy as jnp
import numpy as np
from jax import lax
from jax.experimental import pallas as pl
from jax.experimental.pallas import tpu as pltpu
from jax.sharding import PartitionSpec as P

B = 32
BZ = 32
G = 64
N = 32
SCREEN = 0.0025
MIXING = 0.25
EXCHANGE_COEF = (3.0 / math.pi) ** (1.0 / 3.0)
F32 = jnp.float32
BF16 = jnp.bfloat16
VM = pl.BlockSpec(memory_space=pltpu.VMEM)
SM = pl.BlockSpec(memory_space=pltpu.SMEM)


def axis_basis():
    position = np.arange(B) - 15.5
    cosine = np.cos(2 * np.pi / G * np.outer(position, np.arange(B)))
    sine = np.sin(2 * np.pi / G * np.outer(position, np.arange(1, B + 1)))
    return cosine, sine


def split(value):
    high = value.astype(BF16)
    low = (value - high.astype(F32)).astype(BF16)
    return high, low


def np_split(value):
    value = value.astype(np.float32)
    high = value.astype(jnp.bfloat16)
    low = (value - high.astype(np.float32)).astype(jnp.bfloat16)
    return high, low


def dot(a, b):
    return jnp.dot(a, b, preferred_element_type=F32)


def torus_roll(load, by_y, by_x):
    lane = lax.broadcasted_iota(jnp.int32, (N, 128), 1)
    by_y = lax.rem(by_y, B)
    by_x = lax.rem(by_x, B)
    rows = lax.div(by_y, 4)
    rest = lax.rem(by_y, 4)
    shift = rest * B + by_x
    near = lax.rem(128 - shift, 128)
    far = lax.rem(128 + B - shift, 128)
    inside = lax.rem(lane, B) < B - by_x
    same = lax.div(lane, B) < 4 - rest
    moved = []
    for s in range(8):
        chunk = load(lax.rem(rows + s, 8))
        moved.append(
            jnp.where(inside, pltpu.roll(chunk, near, 1), pltpu.roll(chunk, far, 1))
        )
    return [jnp.where(same, moved[s], moved[(s + 1) % 8]) for s in range(8)]


def pack_kernel(offsets, box, out, planes):
    oy = offsets[0, 0]
    ox = offsets[0, 1]

    def load(c):
        return box[0, :, pl.ds(pl.multiple_of(c * 128, 128), 128)].astype(F32)

    chunks = torus_roll(load, B - lax.rem(oy, B), B - lax.rem(ox, B))
    for s in range(8):
        planes[pl.ds(s, N, stride=8), :] = chunks[s]
    row = lax.broadcasted_iota(jnp.int32, (8, 128), 0)
    extra = jnp.where(
        row == 0, oy.astype(F32), jnp.where(row == 1, ox.astype(F32), 0.0)
    )
    for z in range(N):
        both = jnp.concatenate([planes[8 * z : 8 * z + 8, :], extra], axis=0)
        out[z] = both.astype(BF16)


def pair_numbers(pairs):
    words = [jnp.max(pairs[r : r + 1, 0:1]) for r in range(11)]
    numbers = []
    for p in range(N):
        pair = lax.shift_right_logical(words[p // 3], jnp.int32(10 * (p % 3)))
        second = lax.bitwise_and(pair, jnp.int32(31))
        first = lax.bitwise_and(lax.shift_right_logical(pair, jnp.int32(5)), jnp.int32(31))
        numbers.append((first, second))
    return numbers


def pair_kernel(pairs, recv, rho, dens, phi, code, place):
    numbers = pair_numbers(pairs)
    first = jnp.max(pairs[11:12, 0:1])
    row = lax.broadcasted_iota(jnp.int32, (8, 128), 0)
    lane = lax.broadcasted_iota(jnp.int32, (8, 128), 1)
    y = (row * 4 + lax.div(lane, B)).astype(F32)
    x = lax.rem(lane, B).astype(F32)
    total = [jnp.zeros((8, 128), F32) for _ in range(4)]
    for n in range(N):
        value = recv[n].astype(F32)
        plane = value[:8]
        below = jnp.where(y < value[8:9], 2.0, 0.0)
        quarter = below + jnp.where(x < value[9:10], 1.0, 0.0)
        phi[n] = plane
        code[n] = quarter
        square = plane * plane
        for q in range(4):
            total[q] = total[q] + jnp.where(quarter == float(q), square, 0.0)
    for q in range(4):
        dens[q] = total[q]
    place[...] = recv[first].astype(F32)[8:]
    for p in range(N):
        a, b = numbers[p]
        rho[p] = jnp.where(code[a] == code[b], phi[a] * phi[b], 0.0)


def wave(index):
    return jnp.where(index < B, index, index - (B - 1))


def weigh(index, value):
    k = wave(index)
    return jnp.where((k == 0) | (k == B), value * 0.5, value)


def square(index):
    k = 2.0 * math.pi / G * wave(index).astype(F32)
    return k * k


def table_kernel(owner, corner, fixed_in, pairs_in, fixed, pairs, offsets, green):
    fixed[...] = fixed_in[...]
    row = lax.broadcasted_iota(jnp.int32, (16, N), 0)
    spot = lax.broadcasted_iota(jnp.int32, (16, N), 1) - 3 * row
    both = pairs_in[0:1, :] * 32 + pairs_in[1:2, :]
    own = lax.broadcasted_iota(jnp.int32, (1, N), 1) == owner[0]
    word = jnp.max(jnp.where(own, pairs_in[0:1, :], 0), axis=1, keepdims=True)
    word = jnp.where(row[:, :1] == 11, word, 0)
    for i in range(3):
        part = jnp.max(jnp.where(spot == i, both, 0), axis=1, keepdims=True)
        word = word + part * (1024**i)
    pairs[...] = jnp.broadcast_to(word, (16, 128))
    offsets[:1, :] = jnp.full((1, 128), corner[0, 0], jnp.int32)
    offsets[1:2, :] = jnp.full((1, 128), corner[0, 1], jnp.int32)
    ky = lax.broadcasted_iota(jnp.int32, (G, 256), 0)
    lane = lax.broadcasted_iota(jnp.int32, (G, 256), 1)
    kx = lax.rem(lane, G)
    level = square(ky) + square(kx) + SCREEN
    weight = weigh(ky, weigh(kx, jnp.full((G, 256), 4.0 * math.pi * 8.0 / G**3, F32)))
    top = lax.div(lax.broadcasted_iota(jnp.int32, (8, 256), 1), G)
    for part in range(16):
        kz = top + 4 * part
        factor = weigh(kz, jnp.ones((8, 256), F32))[:1]
        green[G * part : G * part + G, :] = weight * factor / (level + square(kz)[:1])


def exchange_groups(tiles):
    group = lax.div(lax.broadcasted_iota(jnp.int32, (8, 128), 1), B)
    low = group < 2
    even = lax.rem(group, 2) == 0
    t0, t1, t2, t3 = tiles

    def far(first, second):
        return (
            jnp.where(low, first, pltpu.roll(second, 64, 1)),
            jnp.where(low, pltpu.roll(first, 64, 1), second),
        )

    def near(first, second):
        return (
            jnp.where(even, first, pltpu.roll(second, 32, 1)),
            jnp.where(even, pltpu.roll(first, 96, 1), second),
        )

    u0, u2 = far(t0, t2)
    u1, u3 = far(t1, t3)
    v0, v1 = near(u0, u1)
    v2, v3 = near(u2, u3)
    return [v0, v1, v2, v3]


def thrice(value):
    high, low = split(value)
    return jnp.concatenate([high, high, low], axis=0)


def turn(table, wave_index, cell, start):
    odd = lax.rem(wave(wave_index), 2) == 1
    return jnp.where(odd & (cell < start), -table.astype(F32), table.astype(F32)).astype(BF16)


def solve_kernel(place, rho, fixed, green, out, work):
    oy = jnp.max(place[0:1, :]).astype(jnp.int32)
    ox = jnp.max(place[1:2, :]).astype(jnp.int32)

    def index(dims, axis):
        return lax.broadcasted_iota(jnp.int32, dims, axis)

    def row_of(k):
        k = lax.rem(k, B)
        return lax.rem(k, 8) * 4 + lax.div(k, 8)

    ahead_y = turn(
        fixed[G : 2 * G, 768:864], index((G, 96), 0), row_of(index((G, 96), 1)), oy
    )
    back_y = turn(
        fixed[160:192, 768:960],
        lax.rem(index((N, 192), 1), G),
        row_of(index((N, 192), 0)),
        oy,
    )
    square = (256, 256)
    wave_x = lax.rem(index(square, 1), G)
    cell_x = lax.rem(index(square, 0), B)
    ahead_x = turn(fixed[:, :256], wave_x, cell_x, ox)
    ahead_x_low = turn(fixed[:128, 256:512], wave_x[:128], cell_x[:128], ox)
    wave_x = lax.rem(index(square, 0), G)
    cell_x = lax.rem(index(square, 1), B)
    back_x = turn(fixed[:, 512:768], wave_x, cell_x, ox)

    chunks = [rho[pl.ds(s, N, stride=8), :] for s in range(8)]
    waves = dot(fixed[:G, 768:864], thrice(jnp.concatenate(chunks, axis=1)))
    for s in range(8):
        work[pl.ds(s, G, stride=8), :] = waves[:, 128 * s : 128 * s + 128]

    turned = []
    for c in range(16):
        tiles = [work[8 * k : 8 * k + 8, :] for k in range(4 * c, 4 * c + 4)]
        turned.append(jnp.concatenate(exchange_groups(tiles), axis=0))
    waves = dot(ahead_y, thrice(jnp.concatenate(turned, axis=1)))
    rows = jnp.concatenate([waves[:, 128 * c : 128 * c + 128] for c in range(16)], axis=0)
    high, low = split(rows)
    waves = dot(jnp.concatenate([high, low], axis=1), ahead_x)
    waves = waves + dot(high, ahead_x_low)
    high, low = split(waves * green[...])
    both = dot(high, back_x)
    rows = both[:, :128] + both[:, 128:] + dot(low, back_x[:, :128])
    levels = jnp.concatenate([rows[G * c : G * c + G, :] for c in range(16)], axis=1)
    levels = dot(back_y, thrice(levels))
    for c in range(16):
        tiles = [levels[8 * q : 8 * q + 8, 128 * c : 128 * c + 128] for q in range(4)]
        for i, tile in enumerate(exchange_groups(tiles)):
            k = 4 * c + i
            work[8 * k : 8 * k + 8, :] = tile

    levels = jnp.concatenate([work[pl.ds(s, G, stride=8), :] for s in range(8)], axis=1)
    field = dot(fixed[128:160, 768:960], thrice(levels))
    for s in range(8):
        out[pl.ds(s, N, stride=8), :] = field[:, 128 * s : 128 * s + 128]


def cube_root(value):
    rough = jnp.exp(jnp.log(jnp.where(value > 0.0, value, 1.0)) * (1.0 / 3.0))
    finer = rough - (rough - value / (rough * rough)) * (1.0 / 3.0)
    return jnp.where(value > 0.0, finer, 0.0)


def gradient_kernel(pairs, phi, code, field, plane, dens, other, out, terms):
    numbers = pair_numbers(pairs)
    quarters = []
    for q in range(4):
        quarters.append(plane[q] - EXCHANGE_COEF * cube_root(dens[q] + other[q]))
    for n in range(N):
        terms[n] = jnp.zeros((8, 128), F32)
    for p in range(N):
        a, b = numbers[p]
        value = jnp.where(code[a] == code[b], field[p], 0.0)
        terms[a] = terms[a] + value * phi[b]
        terms[b] = terms[b] + value * phi[a]
    for n in range(N):
        quarter = code[n]
        local = jnp.where(
            quarter < 1.5,
            jnp.where(quarter < 0.5, quarters[0], quarters[1]),
            jnp.where(quarter < 2.5, quarters[2], quarters[3]),
        )
        out[n] = local * phi[n] - MIXING * terms[n]


def unpack_kernel(offsets, planes, out):
    oy = jnp.max(offsets[0:1, :])
    ox = jnp.max(offsets[1:2, :])
    chunks = torus_roll(lambda c: planes[pl.ds(c, N, stride=8), :], oy, ox)
    for s in range(8):
        out[0, :, 128 * s : 128 * s + 128] = chunks[s]


def shape(dims, dtype=F32):
    return jax.ShapeDtypeStruct(dims, dtype)


def constants():
    basis = np.concatenate(axis_basis(), axis=1)
    order = np.array([4 * s + q for q in range(4) for s in range(8)])

    def left(matrix):
        high, low = np_split(matrix)
        return np.concatenate([high, low, high], axis=1)

    high, low = np_split(np.kron(np.eye(4), basis))
    back_high, back_low = np_split(np.kron(np.eye(4), basis.T))
    fixed = np.zeros((256, 1024), jnp.bfloat16)
    fixed[:128, :256] = high
    fixed[128:, :256] = high
    fixed[:128, 256:512] = low
    fixed[:, 512:640] = back_high
    fixed[:, 640:768] = back_low
    fixed[:G, 768:864] = left(basis.T)
    fixed[G : 2 * G, 768:864] = left(basis[order].T)
    fixed[128:160, 768:960] = left(basis)
    fixed[160:192, 768:960] = left(basis[order])
    return jnp.asarray(fixed)


def exchange(x):
    return lax.all_to_all(x, "own", 0, 0, tiled=True)


def kernel(call, out_shape, in_specs, name, vmem, scratch=(), flops=0, moved=0):
    many = isinstance(out_shape, list)
    return pl.pallas_call(
        call,
        out_shape=out_shape,
        in_specs=in_specs,
        out_specs=[VM] * len(out_shape) if many else VM,
        scratch_shapes=scratch,
        compiler_params=pltpu.CompilerParams(vmem_limit_bytes=vmem << 20),
        cost_estimate=pl.CostEstimate(flops=flops, bytes_accessed=moved, transcendentals=0),
        name=name,
    )


def swapped(x, bits):
    return lax.ppermute(x, "grp", [(g, g ^ bits) for g in range(8)])


def body(orbitals, offsets, pairs, ext_pot):
    owner = lax.axis_index("own")
    fixed = constants()
    pairs = pairs.T

    sent = kernel(
        pack_kernel,
        shape((N, 16, 128), BF16),
        [SM, VM],
        "pack",
        60,
        [pltpu.VMEM((8 * N, 128), F32)],
        moved=200_000,
    )(offsets, orbitals)
    sent, fixed, pairs, ext_pot = lax.optimization_barrier((sent, fixed, pairs, ext_pot))
    recv = exchange(sent)

    fixed, pairs, offsets, green = kernel(
        table_kernel,
        [
            shape((256, 1024), BF16),
            shape((16, 128), jnp.int32),
            shape((8, 128), jnp.int32),
            shape((1024, 256)),
        ],
        [SM, SM, VM, VM],
        "tables",
        16,
        flops=2_000_000,
        moved=3_000_000,
    )(owner.reshape(1), offsets, fixed, pairs)
    plane = lax.dynamic_slice_in_dim(ext_pot, owner, 1, 0).astype(F32)
    plane = plane.reshape(2, B, 2, B).transpose(0, 2, 1, 3).reshape(4, 8, 128)
    recv, fixed, pairs, offsets, green, plane = lax.optimization_barrier(
        (recv, fixed, pairs, offsets, green, plane)
    )

    planes = shape((N, 8, 128))
    rho, dens, phi, code, place = kernel(
        pair_kernel,
        [planes, shape((4, 8, 128)), planes, planes, shape((8, 128))],
        [VM, VM],
        "pair_products",
        4,
        moved=600_000,
    )(pairs, recv)

    mine = exchange(rho)
    others = [swapped(dens, step) for step in (2, 4, 6)]
    field = kernel(
        solve_kernel,
        shape((8 * N, 128)),
        [VM] * 4,
        "solve",
        16,
        [pltpu.VMEM((8 * G, 128), F32)],
        flops=1_000_000_000,
        moved=3_000_000,
    )(place, mine.reshape(8 * N, 128), fixed, green)
    fields = exchange(field.reshape(N, 8, 128))
    dens = (dens + others[1]) + (others[0] + others[2])
    other = swapped(dens, 1)

    gradient = kernel(
        gradient_kernel,
        shape((N, 8, 128)),
        [VM] * 7,
        "gradient_planes",
        4,
        [pltpu.VMEM((N, 8, 128), F32)],
        moved=600_000,
    )(pairs, phi, code, fields, plane, dens, other)
    back = exchange(gradient)

    return kernel(
        unpack_kernel, shape((1, BZ, B * B)), [VM, VM], "unpack", 4, moved=300_000
    )(offsets, back.reshape(8 * N, 128))


def solution(mesh):
    spec = P(("grp", "own"), None, None)
    in_specs = (spec, P(("grp", "own"), None), P("grp", None), P())
    return jax.shard_map(body, mesh=mesh, in_specs=in_specs, out_specs=spec, check_vma=False)
```

```python
import math

import jax
import jax.numpy as jnp
import numpy as np
from jax import lax
from jax.experimental import pallas as pl
from jax.experimental.pallas import tpu as pltpu
from jax.sharding import PartitionSpec as P

B = 32
BZ = 32
G = 64
N = 32
SCREEN = 0.0025
MIXING = 0.25
EXCHANGE_COEF = (3.0 / math.pi) ** (1.0 / 3.0)
F32 = jnp.float32
BF16 = jnp.bfloat16
VM = pl.BlockSpec(memory_space=pltpu.VMEM)
SM = pl.BlockSpec(memory_space=pltpu.SMEM)


def axis_basis():
    position = np.arange(B) - 15.5
    cosine = np.cos(2 * np.pi / G * np.outer(position, np.arange(B)))
    sine = np.sin(2 * np.pi / G * np.outer(position, np.arange(1, B + 1)))
    return cosine, sine


def split(value):
    high = value.astype(BF16)
    low = (value - high.astype(F32)).astype(BF16)
    return high, low


def np_split(value):
    value = value.astype(np.float32)
    high = value.astype(jnp.bfloat16)
    low = (value - high.astype(np.float32)).astype(jnp.bfloat16)
    return high, low


def dot(a, b):
    return jnp.dot(a, b, preferred_element_type=F32)


def torus_roll(load, by_y, by_x):
    lane = lax.broadcasted_iota(jnp.int32, (N, 128), 1)
    by_y = lax.rem(by_y, B)
    by_x = lax.rem(by_x, B)
    rows = lax.div(by_y, 4)
    rest = lax.rem(by_y, 4)
    shift = rest * B + by_x
    near = lax.rem(128 - shift, 128)
    far = lax.rem(128 + B - shift, 128)
    inside = lax.rem(lane, B) < B - by_x
    same = lax.div(lane, B) < 4 - rest
    moved = []
    for s in range(8):
        chunk = load(lax.rem(rows + s, 8))
        moved.append(
            jnp.where(inside, pltpu.roll(chunk, near, 1), pltpu.roll(chunk, far, 1))
        )
    return [jnp.where(same, moved[s], moved[(s + 1) % 8]) for s in range(8)]


def pack_kernel(offsets, box, out, planes):
    oy = offsets[0, 0]
    ox = offsets[0, 1]

    def load(c):
        return box[0, :, pl.ds(pl.multiple_of(c * 128, 128), 128)].astype(F32)

    chunks = torus_roll(load, B - lax.rem(oy, B), B - lax.rem(ox, B))
    for s in range(8):
        planes[pl.ds(s, N, stride=8), :] = chunks[s]
    row = lax.broadcasted_iota(jnp.int32, (8, 128), 0)
    extra = jnp.where(
        row == 0, oy.astype(F32), jnp.where(row == 1, ox.astype(F32), 0.0)
    )
    for z in range(N):
        both = jnp.concatenate([planes[8 * z : 8 * z + 8, :], extra], axis=0)
        out[z] = both.astype(BF16)


def pair_numbers(pairs):
    words = [jnp.max(pairs[r : r + 1, 0:1]) for r in range(11)]
    numbers = []
    for p in range(N):
        pair = lax.shift_right_logical(words[p // 3], jnp.int32(10 * (p % 3)))
        second = lax.bitwise_and(pair, jnp.int32(31))
        first = lax.bitwise_and(lax.shift_right_logical(pair, jnp.int32(5)), jnp.int32(31))
        numbers.append((first, second))
    return numbers


def pair_kernel(pairs, recv, rho, dens, phi, code, place):
    numbers = pair_numbers(pairs)
    first = jnp.max(pairs[11:12, 0:1])
    row = lax.broadcasted_iota(jnp.int32, (8, 128), 0)
    lane = lax.broadcasted_iota(jnp.int32, (8, 128), 1)
    y = (row * 4 + lax.div(lane, B)).astype(F32)
    x = lax.rem(lane, B).astype(F32)
    total = [jnp.zeros((8, 128), F32) for _ in range(4)]
    for n in range(N):
        value = recv[n].astype(F32)
        plane = value[:8]
        below = jnp.where(y < value[8:9], 2.0, 0.0)
        quarter = below + jnp.where(x < value[9:10], 1.0, 0.0)
        phi[n] = plane
        code[n] = quarter
        square = plane * plane
        for q in range(4):
            total[q] = total[q] + jnp.where(quarter == float(q), square, 0.0)
    for g in range(8):
        for q in range(4):
            dens[g, q] = total[q]
    place[...] = recv[first].astype(F32)[8:]
    for p in range(N):
        a, b = numbers[p]
        rho[p] = jnp.where(code[a] == code[b], phi[a] * phi[b], 0.0)


def wave(index):
    return jnp.where(index < B, index, index - (B - 1))


def weigh(index, value):
    k = wave(index)
    return jnp.where((k == 0) | (k == B), value * 0.5, value)


def square(index):
    k = 2.0 * math.pi / G * wave(index).astype(F32)
    return k * k


def table_kernel(owner, corner, fixed_in, pairs_in, fixed, pairs, offsets, green):
    fixed[...] = fixed_in[...]
    row = lax.broadcasted_iota(jnp.int32, (16, N), 0)
    spot = lax.broadcasted_iota(jnp.int32, (16, N), 1) - 3 * row
    both = pairs_in[0:1, :] * 32 + pairs_in[1:2, :]
    own = lax.broadcasted_iota(jnp.int32, (1, N), 1) == owner[0]
    word = jnp.max(jnp.where(own, pairs_in[0:1, :], 0), axis=1, keepdims=True)
    word = jnp.where(row[:, :1] == 11, word, 0)
    for i in range(3):
        part = jnp.max(jnp.where(spot == i, both, 0), axis=1, keepdims=True)
        word = word + part * (1024**i)
    pairs[...] = jnp.broadcast_to(word, (16, 128))
    offsets[:1, :] = jnp.full((1, 128), corner[0, 0], jnp.int32)
    offsets[1:2, :] = jnp.full((1, 128), corner[0, 1], jnp.int32)
    ky = lax.broadcasted_iota(jnp.int32, (G, 256), 0)
    lane = lax.broadcasted_iota(jnp.int32, (G, 256), 1)
    kx = lax.rem(lane, G)
    level = square(ky) + square(kx) + SCREEN
    weight = weigh(ky, weigh(kx, jnp.full((G, 256), 4.0 * math.pi * 8.0 / G**3, F32)))
    top = lax.div(lax.broadcasted_iota(jnp.int32, (8, 256), 1), G)
    for part in range(16):
        kz = top + 4 * part
        factor = weigh(kz, jnp.ones((8, 256), F32))[:1]
        green[G * part : G * part + G, :] = weight * factor / (level + square(kz)[:1])


def exchange_groups(tiles):
    group = lax.div(lax.broadcasted_iota(jnp.int32, (8, 128), 1), B)
    low = group < 2
    even = lax.rem(group, 2) == 0
    t0, t1, t2, t3 = tiles

    def far(first, second):
        return (
            jnp.where(low, first, pltpu.roll(second, 64, 1)),
            jnp.where(low, pltpu.roll(first, 64, 1), second),
        )

    def near(first, second):
        return (
            jnp.where(even, first, pltpu.roll(second, 32, 1)),
            jnp.where(even, pltpu.roll(first, 96, 1), second),
        )

    u0, u2 = far(t0, t2)
    u1, u3 = far(t1, t3)
    v0, v1 = near(u0, u1)
    v2, v3 = near(u2, u3)
    return [v0, v1, v2, v3]


def thrice(value):
    high, low = split(value)
    return jnp.concatenate([high, high, low], axis=0)


def turn(table, wave_index, cell, start):
    odd = lax.rem(wave(wave_index), 2) == 1
    return jnp.where(odd & (cell < start), -table.astype(F32), table.astype(F32)).astype(BF16)


def solve_kernel(place, rho, fixed, green, out, work):
    oy = jnp.max(place[0:1, :]).astype(jnp.int32)
    ox = jnp.max(place[1:2, :]).astype(jnp.int32)

    def index(dims, axis):
        return lax.broadcasted_iota(jnp.int32, dims, axis)

    def row_of(k):
        k = lax.rem(k, B)
        return lax.rem(k, 8) * 4 + lax.div(k, 8)

    ahead_y = turn(
        fixed[G : 2 * G, 768:864], index((G, 96), 0), row_of(index((G, 96), 1)), oy
    )
    back_y = turn(
        fixed[160:192, 768:960],
        lax.rem(index((N, 192), 1), G),
        row_of(index((N, 192), 0)),
        oy,
    )
    square = (256, 256)
    wave_x = lax.rem(index(square, 1), G)
    cell_x = lax.rem(index(square, 0), B)
    ahead_x = turn(fixed[:, :256], wave_x, cell_x, ox)
    ahead_x_low = turn(fixed[:128, 256:512], wave_x[:128], cell_x[:128], ox)
    wave_x = lax.rem(index(square, 0), G)
    cell_x = lax.rem(index(square, 1), B)
    back_x = turn(fixed[:, 512:768], wave_x, cell_x, ox)

    chunks = [rho[pl.ds(s, N, stride=8), :] for s in range(8)]
    waves = dot(fixed[:G, 768:864], thrice(jnp.concatenate(chunks, axis=1)))
    for s in range(8):
        work[pl.ds(s, G, stride=8), :] = waves[:, 128 * s : 128 * s + 128]

    turned = []
    for c in range(16):
        tiles = [work[8 * k : 8 * k + 8, :] for k in range(4 * c, 4 * c + 4)]
        turned.append(jnp.concatenate(exchange_groups(tiles), axis=0))
    waves = dot(ahead_y, thrice(jnp.concatenate(turned, axis=1)))
    rows = jnp.concatenate([waves[:, 128 * c : 128 * c + 128] for c in range(16)], axis=0)
    high, low = split(rows)
    waves = dot(jnp.concatenate([high, low], axis=1), ahead_x)
    waves = waves + dot(high, ahead_x_low)
    high, low = split(waves * green[...])
    both = dot(high, back_x)
    rows = both[:, :128] + both[:, 128:] + dot(low, back_x[:, :128])
    levels = jnp.concatenate([rows[G * c : G * c + G, :] for c in range(16)], axis=1)
    levels = dot(back_y, thrice(levels))
    for c in range(16):
        tiles = [levels[8 * q : 8 * q + 8, 128 * c : 128 * c + 128] for q in range(4)]
        for i, tile in enumerate(exchange_groups(tiles)):
            k = 4 * c + i
            work[8 * k : 8 * k + 8, :] = tile

    levels = jnp.concatenate([work[pl.ds(s, G, stride=8), :] for s in range(8)], axis=1)
    field = dot(fixed[128:160, 768:960], thrice(levels))
    for s in range(8):
        out[pl.ds(s, N, stride=8), :] = field[:, 128 * s : 128 * s + 128]


def cube_root(value):
    rough = jnp.exp(jnp.log(jnp.where(value > 0.0, value, 1.0)) * (1.0 / 3.0))
    finer = rough - (rough - value / (rough * rough)) * (1.0 / 3.0)
    return jnp.where(value > 0.0, finer, 0.0)


def gradient_kernel(pairs, phi, code, field, plane, gathered, out, terms, dens, sem):
    fetch = pltpu.make_async_copy(gathered.at[:, 0], dens, sem)
    fetch.start()
    numbers = pair_numbers(pairs)
    for n in range(N):
        terms[n] = jnp.zeros((8, 128), F32)
    for p in range(N):
        a, b = numbers[p]
        value = jnp.where(code[a] == code[b], field[p], 0.0)
        terms[a] = terms[a] + value * phi[b]
        terms[b] = terms[b] + value * phi[a]
    fetch.wait()
    quarters = []
    for q in range(4):
        total = dens[0, q]
        for g in range(1, 8):
            total = total + dens[g, q]
        quarters.append(plane[q] - EXCHANGE_COEF * cube_root(total))
    for n in range(N):
        quarter = code[n]
        local = jnp.where(
            quarter < 1.5,
            jnp.where(quarter < 0.5, quarters[0], quarters[1]),
            jnp.where(quarter < 2.5, quarters[2], quarters[3]),
        )
        out[n] = local * phi[n] - MIXING * terms[n]


def unpack_kernel(offsets, planes, out):
    oy = jnp.max(offsets[0:1, :])
    ox = jnp.max(offsets[1:2, :])
    chunks = torus_roll(lambda c: planes[pl.ds(c, N, stride=8), :], oy, ox)
    for s in range(8):
        out[0, :, 128 * s : 128 * s + 128] = chunks[s]


def shape(dims, dtype=F32):
    return jax.ShapeDtypeStruct(dims, dtype)


def constants():
    basis = np.concatenate(axis_basis(), axis=1)
    order = np.array([4 * s + q for q in range(4) for s in range(8)])

    def left(matrix):
        high, low = np_split(matrix)
        return np.concatenate([high, low, high], axis=1)

    high, low = np_split(np.kron(np.eye(4), basis))
    back_high, back_low = np_split(np.kron(np.eye(4), basis.T))
    fixed = np.zeros((256, 1024), jnp.bfloat16)
    fixed[:128, :256] = high
    fixed[128:, :256] = high
    fixed[:128, 256:512] = low
    fixed[:, 512:640] = back_high
    fixed[:, 640:768] = back_low
    fixed[:G, 768:864] = left(basis.T)
    fixed[G : 2 * G, 768:864] = left(basis[order].T)
    fixed[128:160, 768:960] = left(basis)
    fixed[160:192, 768:960] = left(basis[order])
    return jnp.asarray(fixed)


def exchange(x):
    return lax.all_to_all(x, "own", 0, 0, tiled=True)


def kernel(call, out_shape, in_specs, name, vmem, scratch=(), flops=0, moved=0):
    many = isinstance(out_shape, list)
    return pl.pallas_call(
        call,
        out_shape=out_shape,
        in_specs=in_specs,
        out_specs=[VM] * len(out_shape) if many else VM,
        scratch_shapes=scratch,
        compiler_params=pltpu.CompilerParams(vmem_limit_bytes=vmem << 20),
        cost_estimate=pl.CostEstimate(flops=flops, bytes_accessed=moved, transcendentals=0),
        name=name,
    )


def body(orbitals, offsets, pairs, ext_pot):
    owner = lax.axis_index("own")
    fixed = constants()
    pairs = pairs.T

    sent = kernel(
        pack_kernel,
        shape((N, 16, 128), BF16),
        [SM, VM],
        "pack",
        60,
        [pltpu.VMEM((8 * N, 128), F32)],
        moved=200_000,
    )(offsets, orbitals)
    sent, fixed, pairs, ext_pot = lax.optimization_barrier((sent, fixed, pairs, ext_pot))
    recv = exchange(sent)

    fixed, pairs, offsets, green = kernel(
        table_kernel,
        [
            shape((256, 1024), BF16),
            shape((16, 128), jnp.int32),
            shape((8, 128), jnp.int32),
            shape((1024, 256)),
        ],
        [SM, SM, VM, VM],
        "tables",
        16,
        flops=2_000_000,
        moved=3_000_000,
    )(owner.reshape(1), offsets, fixed, pairs)
    plane = lax.dynamic_slice_in_dim(ext_pot, owner, 1, 0).astype(F32)
    plane = plane.reshape(2, B, 2, B).transpose(0, 2, 1, 3).reshape(4, 8, 128)
    recv, fixed, pairs, offsets, green, plane = lax.optimization_barrier(
        (recv, fixed, pairs, offsets, green, plane)
    )

    planes = shape((N, 8, 128))
    rho, dens, phi, code, place = kernel(
        pair_kernel,
        [planes, shape((8, 4, 8, 128)), planes, planes, shape((8, 128))],
        [VM, VM],
        "pair_products",
        4,
        moved=600_000,
    )(pairs, recv)

    mine = exchange(rho)
    gathered = lax.all_gather(dens, "grp", axis=0)
    field = kernel(
        solve_kernel,
        shape((8 * N, 128)),
        [VM] * 4,
        "solve",
        16,
        [pltpu.VMEM((8 * G, 128), F32)],
        flops=1_000_000_000,
        moved=3_000_000,
    )(place, mine.reshape(8 * N, 128), fixed, green)
    fields = exchange(field.reshape(N, 8, 128))
    gradient = kernel(
        gradient_kernel,
        shape((N, 8, 128)),
        [VM] * 5 + [pl.BlockSpec(memory_space=pltpu.HBM)],
        "gradient_planes",
        53,
        [
            pltpu.VMEM((N, 8, 128), F32),
            pltpu.VMEM((8, 4, 8, 128), F32),
            pltpu.SemaphoreType.DMA(()),
        ],
        moved=600_000,
    )(pairs, phi, code, fields, plane, gathered)
    back = exchange(gradient)

    return kernel(
        unpack_kernel, shape((1, BZ, B * B)), [VM, VM], "unpack", 4, moved=300_000
    )(offsets, back.reshape(8 * N, 128))


def solution(mesh):
    spec = P(("grp", "own"), None, None)
    in_specs = (spec, P(("grp", "own"), None), P("grp", None), P())
    return jax.shard_map(body, mesh=mesh, in_specs=in_specs, out_specs=spec, check_vma=False)
```

```python
import math

import jax
import jax.numpy as jnp
import numpy as np
from jax import lax
from jax.experimental import pallas as pl
from jax.experimental.pallas import tpu as pltpu
from jax.sharding import PartitionSpec as P

B = 32
BZ = 32
G = 64
N = 32
SCREEN = 0.0025
MIXING = 0.25
EXCHANGE_COEF = (3.0 / math.pi) ** (1.0 / 3.0)
F32 = jnp.float32
BF16 = jnp.bfloat16
VM = pl.BlockSpec(memory_space=pltpu.VMEM)
SM = pl.BlockSpec(memory_space=pltpu.SMEM)


def axis_basis():
    position = np.arange(B) - 15.5
    cosine = np.cos(2 * np.pi / G * np.outer(position, np.arange(B)))
    sine = np.sin(2 * np.pi / G * np.outer(position, np.arange(1, B + 1)))
    return cosine, sine


def split(value):
    high = value.astype(BF16)
    low = (value - high.astype(F32)).astype(BF16)
    return high, low


def np_split(value):
    value = value.astype(np.float32)
    high = value.astype(jnp.bfloat16)
    low = (value - high.astype(np.float32)).astype(jnp.bfloat16)
    return high, low


def dot(a, b):
    return jnp.dot(a, b, preferred_element_type=F32)


def torus_roll(load, by_y, by_x):
    lane = lax.broadcasted_iota(jnp.int32, (N, 128), 1)
    by_y = lax.rem(by_y, B)
    by_x = lax.rem(by_x, B)
    rows = lax.div(by_y, 4)
    rest = lax.rem(by_y, 4)
    shift = rest * B + by_x
    near = lax.rem(128 - shift, 128)
    far = lax.rem(128 + B - shift, 128)
    inside = lax.rem(lane, B) < B - by_x
    same = lax.div(lane, B) < 4 - rest
    moved = []
    for s in range(8):
        chunk = load(lax.rem(rows + s, 8))
        moved.append(
            jnp.where(inside, pltpu.roll(chunk, near, 1), pltpu.roll(chunk, far, 1))
        )
    return [jnp.where(same, moved[s], moved[(s + 1) % 8]) for s in range(8)]


def pack_kernel(offsets, box, out, planes):
    oy = offsets[0, 0]
    ox = offsets[0, 1]

    def load(c):
        return box[0, :, pl.ds(pl.multiple_of(c * 128, 128), 128)].astype(F32)

    chunks = torus_roll(load, B - lax.rem(oy, B), B - lax.rem(ox, B))
    for s in range(8):
        planes[pl.ds(s, N, stride=8), :] = chunks[s]
    row = lax.broadcasted_iota(jnp.int32, (8, 128), 0)
    extra = jnp.where(
        row == 0, oy.astype(F32), jnp.where(row == 1, ox.astype(F32), 0.0)
    )
    for z in range(N):
        both = jnp.concatenate([planes[8 * z : 8 * z + 8, :], extra], axis=0)
        out[z] = both.astype(BF16)


def pair_numbers(pairs):
    words = [jnp.max(pairs[r : r + 1, 0:1]) for r in range(11)]
    numbers = []
    for p in range(N):
        pair = lax.shift_right_logical(words[p // 3], jnp.int32(10 * (p % 3)))
        second = lax.bitwise_and(pair, jnp.int32(31))
        first = lax.bitwise_and(lax.shift_right_logical(pair, jnp.int32(5)), jnp.int32(31))
        numbers.append((first, second))
    return numbers


def pair_kernel(pairs, recv, rho, dens, phi, code, place):
    numbers = pair_numbers(pairs)
    first = jnp.max(pairs[11:12, 0:1])
    row = lax.broadcasted_iota(jnp.int32, (8, 128), 0)
    lane = lax.broadcasted_iota(jnp.int32, (8, 128), 1)
    y = (row * 4 + lax.div(lane, B)).astype(F32)
    x = lax.rem(lane, B).astype(F32)
    total = [jnp.zeros((8, 128), F32) for _ in range(4)]
    for n in range(N):
        value = recv[n].astype(F32)
        plane = value[:8]
        below = jnp.where(y < value[8:9], 2.0, 0.0)
        quarter = below + jnp.where(x < value[9:10], 1.0, 0.0)
        phi[n] = plane
        code[n] = quarter
        square = plane * plane
        for q in range(4):
            total[q] = total[q] + jnp.where(quarter == float(q), square, 0.0)
    for q in range(4):
        dens[q] = total[q]
    place[...] = recv[first].astype(F32)[8:]
    for p in range(N):
        a, b = numbers[p]
        rho[p] = jnp.where(code[a] == code[b], phi[a] * phi[b], 0.0)


def wave(index):
    return jnp.where(index < B, index, index - (B - 1))


def weigh(index, value):
    k = wave(index)
    return jnp.where((k == 0) | (k == B), value * 0.5, value)


def square(index):
    k = 2.0 * math.pi / G * wave(index).astype(F32)
    return k * k


def table_kernel(owner, corner, fixed_in, pairs_in, fixed, pairs, offsets, green):
    fixed[...] = fixed_in[...]
    row = lax.broadcasted_iota(jnp.int32, (16, N), 0)
    spot = lax.broadcasted_iota(jnp.int32, (16, N), 1) - 3 * row
    both = pairs_in[0:1, :] * 32 + pairs_in[1:2, :]
    own = lax.broadcasted_iota(jnp.int32, (1, N), 1) == owner[0]
    word = jnp.max(jnp.where(own, pairs_in[0:1, :], 0), axis=1, keepdims=True)
    word = jnp.where(row[:, :1] == 11, word, 0)
    for i in range(3):
        part = jnp.max(jnp.where(spot == i, both, 0), axis=1, keepdims=True)
        word = word + part * (1024**i)
    pairs[...] = jnp.broadcast_to(word, (16, 128))
    offsets[:1, :] = jnp.full((1, 128), corner[0, 0], jnp.int32)
    offsets[1:2, :] = jnp.full((1, 128), corner[0, 1], jnp.int32)
    ky = lax.broadcasted_iota(jnp.int32, (G, 256), 0)
    lane = lax.broadcasted_iota(jnp.int32, (G, 256), 1)
    kx = lax.rem(lane, G)
    level = square(ky) + square(kx) + SCREEN
    weight = weigh(ky, weigh(kx, jnp.full((G, 256), 4.0 * math.pi * 8.0 / G**3, F32)))
    top = lax.div(lax.broadcasted_iota(jnp.int32, (8, 256), 1), G)
    for part in range(16):
        kz = top + 4 * part
        factor = weigh(kz, jnp.ones((8, 256), F32))[:1]
        green[G * part : G * part + G, :] = weight * factor / (level + square(kz)[:1])


def exchange_groups(tiles):
    group = lax.div(lax.broadcasted_iota(jnp.int32, (8, 128), 1), B)
    low = group < 2
    even = lax.rem(group, 2) == 0
    t0, t1, t2, t3 = tiles

    def far(first, second):
        return (
            jnp.where(low, first, pltpu.roll(second, 64, 1)),
            jnp.where(low, pltpu.roll(first, 64, 1), second),
        )

    def near(first, second):
        return (
            jnp.where(even, first, pltpu.roll(second, 32, 1)),
            jnp.where(even, pltpu.roll(first, 96, 1), second),
        )

    u0, u2 = far(t0, t2)
    u1, u3 = far(t1, t3)
    v0, v1 = near(u0, u1)
    v2, v3 = near(u2, u3)
    return [v0, v1, v2, v3]


def thrice(value):
    high, low = split(value)
    return jnp.concatenate([high, high, low], axis=0)


def turn(table, wave_index, cell, start):
    odd = lax.rem(wave(wave_index), 2) == 1
    return jnp.where(odd & (cell < start), -table.astype(F32), table.astype(F32)).astype(BF16)


def solve_kernel(place, rho, fixed, green, out, work):
    oy = jnp.max(place[0:1, :]).astype(jnp.int32)
    ox = jnp.max(place[1:2, :]).astype(jnp.int32)

    def index(dims, axis):
        return lax.broadcasted_iota(jnp.int32, dims, axis)

    def row_of(k):
        k = lax.rem(k, B)
        return lax.rem(k, 8) * 4 + lax.div(k, 8)

    ahead_y = turn(
        fixed[G : 2 * G, 768:864], index((G, 96), 0), row_of(index((G, 96), 1)), oy
    )
    back_y = turn(
        fixed[160:192, 768:960],
        lax.rem(index((N, 192), 1), G),
        row_of(index((N, 192), 0)),
        oy,
    )
    square = (256, 256)
    wave_x = lax.rem(index(square, 1), G)
    cell_x = lax.rem(index(square, 0), B)
    ahead_x = turn(fixed[:, :256], wave_x, cell_x, ox)
    ahead_x_low = turn(fixed[:128, 256:512], wave_x[:128], cell_x[:128], ox)
    wave_x = lax.rem(index(square, 0), G)
    cell_x = lax.rem(index(square, 1), B)
    back_x = turn(fixed[:, 512:768], wave_x, cell_x, ox)

    chunks = [rho[pl.ds(s, N, stride=8), :] for s in range(8)]
    waves = dot(fixed[:G, 768:864], thrice(jnp.concatenate(chunks, axis=1)))
    for s in range(8):
        work[pl.ds(s, G, stride=8), :] = waves[:, 128 * s : 128 * s + 128]

    turned = []
    for c in range(16):
        tiles = [work[8 * k : 8 * k + 8, :] for k in range(4 * c, 4 * c + 4)]
        turned.append(jnp.concatenate(exchange_groups(tiles), axis=0))
    waves = dot(ahead_y, thrice(jnp.concatenate(turned, axis=1)))
    rows = jnp.concatenate([waves[:, 128 * c : 128 * c + 128] for c in range(16)], axis=0)
    high, low = split(rows)
    waves = dot(jnp.concatenate([high, low], axis=1), ahead_x)
    waves = waves + dot(high, ahead_x_low)
    high, low = split(waves * green[...])
    both = dot(high, back_x)
    rows = both[:, :128] + both[:, 128:] + dot(low, back_x[:, :128])
    levels = jnp.concatenate([rows[G * c : G * c + G, :] for c in range(16)], axis=1)
    levels = dot(back_y, thrice(levels))
    for c in range(16):
        tiles = [levels[8 * q : 8 * q + 8, 128 * c : 128 * c + 128] for q in range(4)]
        for i, tile in enumerate(exchange_groups(tiles)):
            k = 4 * c + i
            work[8 * k : 8 * k + 8, :] = tile

    levels = jnp.concatenate([work[pl.ds(s, G, stride=8), :] for s in range(8)], axis=1)
    field = dot(fixed[128:160, 768:960], thrice(levels))
    for s in range(8):
        out[pl.ds(s, N, stride=8), :] = field[:, 128 * s : 128 * s + 128]


def cube_root(value):
    rough = jnp.exp(jnp.log(jnp.where(value > 0.0, value, 1.0)) * (1.0 / 3.0))
    finer = rough - (rough - value / (rough * rough)) * (1.0 / 3.0)
    return jnp.where(value > 0.0, finer, 0.0)


def gradient_kernel(pairs, phi, code, field, plane, dens, other, out, terms):
    numbers = pair_numbers(pairs)
    quarters = []
    for q in range(4):
        quarters.append(plane[q] - EXCHANGE_COEF * cube_root(dens[q] + other[q]))
    for n in range(N):
        terms[n] = jnp.zeros((8, 128), F32)
    for p in range(N):
        a, b = numbers[p]
        value = jnp.where(code[a] == code[b], field[p], 0.0)
        terms[a] = terms[a] + value * phi[b]
        terms[b] = terms[b] + value * phi[a]
    for n in range(N):
        quarter = code[n]
        local = jnp.where(
            quarter < 1.5,
            jnp.where(quarter < 0.5, quarters[0], quarters[1]),
            jnp.where(quarter < 2.5, quarters[2], quarters[3]),
        )
        out[n] = local * phi[n] - MIXING * terms[n]


def unpack_kernel(offsets, planes, out):
    oy = jnp.max(offsets[0:1, :])
    ox = jnp.max(offsets[1:2, :])
    chunks = torus_roll(lambda c: planes[pl.ds(c, N, stride=8), :], oy, ox)
    for s in range(8):
        out[0, :, 128 * s : 128 * s + 128] = chunks[s]


def shape(dims, dtype=F32):
    return jax.ShapeDtypeStruct(dims, dtype)


def constants():
    basis = np.concatenate(axis_basis(), axis=1)
    order = np.array([4 * s + q for q in range(4) for s in range(8)])

    def left(matrix):
        high, low = np_split(matrix)
        return np.concatenate([high, low, high], axis=1)

    high, low = np_split(np.kron(np.eye(4), basis))
    back_high, back_low = np_split(np.kron(np.eye(4), basis.T))
    fixed = np.zeros((256, 1024), jnp.bfloat16)
    fixed[:128, :256] = high
    fixed[128:, :256] = high
    fixed[:128, 256:512] = low
    fixed[:, 512:640] = back_high
    fixed[:, 640:768] = back_low
    fixed[:G, 768:864] = left(basis.T)
    fixed[G : 2 * G, 768:864] = left(basis[order].T)
    fixed[128:160, 768:960] = left(basis)
    fixed[160:192, 768:960] = left(basis[order])
    return jnp.asarray(fixed)


def exchange(x):
    return lax.all_to_all(x, "own", 0, 0, tiled=True)


def kernel(call, out_shape, in_specs, name, vmem, scratch=(), flops=0, moved=0):
    many = isinstance(out_shape, list)
    return pl.pallas_call(
        call,
        out_shape=out_shape,
        in_specs=in_specs,
        out_specs=[VM] * len(out_shape) if many else VM,
        scratch_shapes=scratch,
        compiler_params=pltpu.CompilerParams(vmem_limit_bytes=vmem << 20),
        cost_estimate=pl.CostEstimate(flops=flops, bytes_accessed=moved, transcendentals=0),
        name=name,
    )


def swapped(x, bits):
    return lax.ppermute(x, "grp", [(g, g ^ bits) for g in range(8)])


def body(orbitals, offsets, pairs, ext_pot):
    owner = lax.axis_index("own")
    fixed = constants()
    pairs = pairs.T

    sent = kernel(
        pack_kernel,
        shape((N, 16, 128), BF16),
        [SM, VM],
        "pack",
        60,
        [pltpu.VMEM((8 * N, 128), F32)],
        moved=200_000,
    )(offsets, orbitals)
    sent, fixed, pairs, ext_pot = lax.optimization_barrier((sent, fixed, pairs, ext_pot))
    recv = exchange(sent)

    fixed, pairs, offsets, green = kernel(
        table_kernel,
        [
            shape((256, 1024), BF16),
            shape((16, 128), jnp.int32),
            shape((8, 128), jnp.int32),
            shape((1024, 256)),
        ],
        [SM, SM, VM, VM],
        "tables",
        16,
        flops=2_000_000,
        moved=3_000_000,
    )(owner.reshape(1), offsets, fixed, pairs)
    plane = lax.dynamic_slice_in_dim(ext_pot, owner, 1, 0).astype(F32)
    plane = plane.reshape(2, B, 2, B).transpose(0, 2, 1, 3).reshape(4, 8, 128)
    recv, fixed, pairs, offsets, green, plane = lax.optimization_barrier(
        (recv, fixed, pairs, offsets, green, plane)
    )

    planes = shape((N, 8, 128))
    rho, dens, phi, code, place = kernel(
        pair_kernel,
        [planes, shape((4, 8, 128)), planes, planes, shape((8, 128))],
        [VM, VM],
        "pair_products",
        4,
        moved=600_000,
    )(pairs, recv)

    mine = exchange(rho)
    dens = dens + swapped(dens, 2)
    dens = dens + swapped(dens, 4)
    mine, dens = lax.optimization_barrier((mine, dens))
    other = swapped(dens, 1)
    field = kernel(
        solve_kernel,
        shape((8 * N, 128)),
        [VM] * 4,
        "solve",
        16,
        [pltpu.VMEM((8 * G, 128), F32)],
        flops=1_000_000_000,
        moved=3_000_000,
    )(place, mine.reshape(8 * N, 128), fixed, green)
    field, other = lax.optimization_barrier((field, other))
    fields = exchange(field.reshape(N, 8, 128))

    gradient = kernel(
        gradient_kernel,
        shape((N, 8, 128)),
        [VM] * 7,
        "gradient_planes",
        4,
        [pltpu.VMEM((N, 8, 128), F32)],
        moved=600_000,
    )(pairs, phi, code, fields, plane, dens, other)
    back = exchange(gradient)

    return kernel(
        unpack_kernel, shape((1, BZ, B * B)), [VM, VM], "unpack", 4, moved=300_000
    )(offsets, back.reshape(8 * N, 128))


def solution(mesh):
    spec = P(("grp", "own"), None, None)
    in_specs = (spec, P(("grp", "own"), None), P("grp", None), P())
    return jax.shard_map(body, mesh=mesh, in_specs=in_specs, out_specs=spec, check_vma=False)
```

```python
import math

import jax
import jax.numpy as jnp
import numpy as np
from jax import lax
from jax.experimental import pallas as pl
from jax.experimental.pallas import tpu as pltpu
from jax.sharding import PartitionSpec as P

B = 32
BZ = 32
G = 64
N = 32
SCREEN = 0.0025
MIXING = 0.25
EXCHANGE_COEF = (3.0 / math.pi) ** (1.0 / 3.0)
F32 = jnp.float32
BF16 = jnp.bfloat16
VM = pl.BlockSpec(memory_space=pltpu.VMEM)
SM = pl.BlockSpec(memory_space=pltpu.SMEM)


def axis_basis():
    position = np.arange(B) - 15.5
    cosine = np.cos(2 * np.pi / G * np.outer(position, np.arange(B)))
    sine = np.sin(2 * np.pi / G * np.outer(position, np.arange(1, B + 1)))
    return cosine, sine


def split(value):
    high = value.astype(BF16)
    low = (value - high.astype(F32)).astype(BF16)
    return high, low


def np_split(value):
    value = value.astype(np.float32)
    high = value.astype(jnp.bfloat16)
    low = (value - high.astype(np.float32)).astype(jnp.bfloat16)
    return high, low


def dot(a, b):
    return jnp.dot(a, b, preferred_element_type=F32)


def torus_roll(load, by_y, by_x):
    lane = lax.broadcasted_iota(jnp.int32, (N, 128), 1)
    by_y = lax.rem(by_y, B)
    by_x = lax.rem(by_x, B)
    rows = lax.div(by_y, 4)
    rest = lax.rem(by_y, 4)
    shift = rest * B + by_x
    near = lax.rem(128 - shift, 128)
    far = lax.rem(128 + B - shift, 128)
    inside = lax.rem(lane, B) < B - by_x
    same = lax.div(lane, B) < 4 - rest
    moved = []
    for s in range(8):
        chunk = load(lax.rem(rows + s, 8))
        moved.append(
            jnp.where(inside, pltpu.roll(chunk, near, 1), pltpu.roll(chunk, far, 1))
        )
    return [jnp.where(same, moved[s], moved[(s + 1) % 8]) for s in range(8)]


def pack_kernel(offsets, box, out, planes):
    oy = offsets[0, 0]
    ox = offsets[0, 1]

    def load(c):
        return box[0, :, pl.ds(pl.multiple_of(c * 128, 128), 128)].astype(F32)

    chunks = torus_roll(load, B - lax.rem(oy, B), B - lax.rem(ox, B))
    for s in range(8):
        planes[pl.ds(s, N, stride=8), :] = chunks[s]
    row = lax.broadcasted_iota(jnp.int32, (8, 128), 0)
    extra = jnp.where(
        row == 0, oy.astype(F32), jnp.where(row == 1, ox.astype(F32), 0.0)
    )
    for z in range(N):
        both = jnp.concatenate([planes[8 * z : 8 * z + 8, :], extra], axis=0)
        out[z] = both.astype(BF16)


def pair_numbers(pairs):
    words = [jnp.max(pairs[r : r + 1, 0:1]) for r in range(11)]
    numbers = []
    for p in range(N):
        pair = lax.shift_right_logical(words[p // 3], jnp.int32(10 * (p % 3)))
        second = lax.bitwise_and(pair, jnp.int32(31))
        first = lax.bitwise_and(lax.shift_right_logical(pair, jnp.int32(5)), jnp.int32(31))
        numbers.append((first, second))
    return numbers


def pair_kernel(pairs, recv, rho, dens, phi, code, place):
    numbers = pair_numbers(pairs)
    first = jnp.max(pairs[11:12, 0:1])
    row = lax.broadcasted_iota(jnp.int32, (8, 128), 0)
    lane = lax.broadcasted_iota(jnp.int32, (8, 128), 1)
    y = (row * 4 + lax.div(lane, B)).astype(F32)
    x = lax.rem(lane, B).astype(F32)
    total = [jnp.zeros((8, 128), F32) for _ in range(4)]
    for n in range(N):
        value = recv[n].astype(F32)
        plane = value[:8]
        below = jnp.where(y < value[8:9], 2.0, 0.0)
        quarter = below + jnp.where(x < value[9:10], 1.0, 0.0)
        phi[n] = plane
        code[n] = quarter
        square = plane * plane
        for q in range(4):
            total[q] = total[q] + jnp.where(quarter == float(q), square, 0.0)
    for q in range(4):
        dens[q] = total[q]
    place[...] = recv[first].astype(F32)[8:]
    for p in range(N):
        a, b = numbers[p]
        rho[p] = jnp.where(code[a] == code[b], phi[a] * phi[b], 0.0)


def wave(index):
    return jnp.where(index < B, index, index - (B - 1))


def weigh(index, value):
    k = wave(index)
    return jnp.where((k == 0) | (k == B), value * 0.5, value)


def square(index):
    k = 2.0 * math.pi / G * wave(index).astype(F32)
    return k * k


def table_kernel(owner, corner, fixed_in, pairs_in, fixed, pairs, offsets, green):
    fixed[...] = fixed_in[...]
    row = lax.broadcasted_iota(jnp.int32, (16, N), 0)
    spot = lax.broadcasted_iota(jnp.int32, (16, N), 1) - 3 * row
    both = pairs_in[0:1, :] * 32 + pairs_in[1:2, :]
    own = lax.broadcasted_iota(jnp.int32, (1, N), 1) == owner[0]
    word = jnp.max(jnp.where(own, pairs_in[0:1, :], 0), axis=1, keepdims=True)
    word = jnp.where(row[:, :1] == 11, word, 0)
    for i in range(3):
        part = jnp.max(jnp.where(spot == i, both, 0), axis=1, keepdims=True)
        word = word + part * (1024**i)
    pairs[...] = jnp.broadcast_to(word, (16, 128))
    offsets[:1, :] = jnp.full((1, 128), corner[0, 0], jnp.int32)
    offsets[1:2, :] = jnp.full((1, 128), corner[0, 1], jnp.int32)
    ky = lax.broadcasted_iota(jnp.int32, (G, 256), 0)
    lane = lax.broadcasted_iota(jnp.int32, (G, 256), 1)
    kx = lax.rem(lane, G)
    level = square(ky) + square(kx) + SCREEN
    weight = weigh(ky, weigh(kx, jnp.full((G, 256), 4.0 * math.pi * 8.0 / G**3, F32)))
    top = lax.div(lax.broadcasted_iota(jnp.int32, (8, 256), 1), G)
    for part in range(16):
        kz = top + 4 * part
        factor = weigh(kz, jnp.ones((8, 256), F32))[:1]
        green[G * part : G * part + G, :] = weight * factor / (level + square(kz)[:1])


def exchange_groups(tiles):
    group = lax.div(lax.broadcasted_iota(jnp.int32, (8, 128), 1), B)
    low = group < 2
    even = lax.rem(group, 2) == 0
    t0, t1, t2, t3 = tiles

    def far(first, second):
        return (
            jnp.where(low, first, pltpu.roll(second, 64, 1)),
            jnp.where(low, pltpu.roll(first, 64, 1), second),
        )

    def near(first, second):
        return (
            jnp.where(even, first, pltpu.roll(second, 32, 1)),
            jnp.where(even, pltpu.roll(first, 96, 1), second),
        )

    u0, u2 = far(t0, t2)
    u1, u3 = far(t1, t3)
    v0, v1 = near(u0, u1)
    v2, v3 = near(u2, u3)
    return [v0, v1, v2, v3]


def thrice(value):
    high, low = split(value)
    return jnp.concatenate([high, high, low], axis=0)


def turn(table, wave_index, cell, start):
    odd = lax.rem(wave(wave_index), 2) == 1
    return jnp.where(odd & (cell < start), -table.astype(F32), table.astype(F32)).astype(BF16)


def solve_kernel(place, rho, fixed, green, out, work):
    oy = jnp.max(place[0:1, :]).astype(jnp.int32)
    ox = jnp.max(place[1:2, :]).astype(jnp.int32)

    def index(dims, axis):
        return lax.broadcasted_iota(jnp.int32, dims, axis)

    def row_of(k):
        k = lax.rem(k, B)
        return lax.rem(k, 8) * 4 + lax.div(k, 8)

    ahead_y = turn(
        fixed[G : 2 * G, 768:864], index((G, 96), 0), row_of(index((G, 96), 1)), oy
    )
    back_y = turn(
        fixed[160:192, 768:960],
        lax.rem(index((N, 192), 1), G),
        row_of(index((N, 192), 0)),
        oy,
    )
    square = (256, 256)
    wave_x = lax.rem(index(square, 1), G)
    cell_x = lax.rem(index(square, 0), B)
    ahead_x = turn(fixed[:, :256], wave_x, cell_x, ox)
    ahead_x_low = turn(fixed[:128, 256:512], wave_x[:128], cell_x[:128], ox)
    wave_x = lax.rem(index(square, 0), G)
    cell_x = lax.rem(index(square, 1), B)
    back_x = turn(fixed[:, 512:768], wave_x, cell_x, ox)

    chunks = [rho[pl.ds(s, N, stride=8), :] for s in range(8)]
    waves = dot(fixed[:G, 768:864], thrice(jnp.concatenate(chunks, axis=1)))
    for s in range(8):
        work[pl.ds(s, G, stride=8), :] = waves[:, 128 * s : 128 * s + 128]

    turned = []
    for c in range(16):
        tiles = [work[8 * k : 8 * k + 8, :] for k in range(4 * c, 4 * c + 4)]
        turned.append(jnp.concatenate(exchange_groups(tiles), axis=0))
    waves = dot(ahead_y, thrice(jnp.concatenate(turned, axis=1)))
    rows = jnp.concatenate([waves[:, 128 * c : 128 * c + 128] for c in range(16)], axis=0)
    halves = []
    for half in range(2):
        high, low = split(rows[512 * half : 512 * half + 512])
        waves = dot(jnp.concatenate([high, low], axis=1), ahead_x)
        halves.append(waves + dot(high, ahead_x_low))
    pieces = []
    for half in range(2):
        high, low = split(halves[half] * green[512 * half : 512 * half + 512, :])
        both = dot(high, back_x)
        pieces.append(both[:, :128] + both[:, 128:] + dot(low, back_x[:, :128]))
    rows = jnp.concatenate(pieces, axis=0)
    levels = jnp.concatenate([rows[G * c : G * c + G, :] for c in range(16)], axis=1)
    levels = dot(back_y, thrice(levels))
    for c in range(16):
        tiles = [levels[8 * q : 8 * q + 8, 128 * c : 128 * c + 128] for q in range(4)]
        for i, tile in enumerate(exchange_groups(tiles)):
            k = 4 * c + i
            work[8 * k : 8 * k + 8, :] = tile

    levels = jnp.concatenate([work[pl.ds(s, G, stride=8), :] for s in range(8)], axis=1)
    field = dot(fixed[128:160, 768:960], thrice(levels))
    for s in range(8):
        out[pl.ds(s, N, stride=8), :] = field[:, 128 * s : 128 * s + 128]


def cube_root(value):
    rough = jnp.exp(jnp.log(jnp.where(value > 0.0, value, 1.0)) * (1.0 / 3.0))
    finer = rough - (rough - value / (rough * rough)) * (1.0 / 3.0)
    return jnp.where(value > 0.0, finer, 0.0)


def gradient_kernel(pairs, phi, code, field, plane, dens, other, out, terms):
    numbers = pair_numbers(pairs)
    quarters = []
    for q in range(4):
        quarters.append(plane[q] - EXCHANGE_COEF * cube_root(dens[q] + other[q]))
    for n in range(N):
        terms[n] = jnp.zeros((8, 128), F32)
    for p in range(N):
        a, b = numbers[p]
        value = jnp.where(code[a] == code[b], field[p], 0.0)
        terms[a] = terms[a] + value * phi[b]
        terms[b] = terms[b] + value * phi[a]
    for n in range(N):
        quarter = code[n]
        local = jnp.where(
            quarter < 1.5,
            jnp.where(quarter < 0.5, quarters[0], quarters[1]),
            jnp.where(quarter < 2.5, quarters[2], quarters[3]),
        )
        out[n] = local * phi[n] - MIXING * terms[n]


def unpack_kernel(offsets, planes, out):
    oy = jnp.max(offsets[0:1, :])
    ox = jnp.max(offsets[1:2, :])
    chunks = torus_roll(lambda c: planes[pl.ds(c, N, stride=8), :], oy, ox)
    for s in range(8):
        out[0, :, 128 * s : 128 * s + 128] = chunks[s]


def shape(dims, dtype=F32):
    return jax.ShapeDtypeStruct(dims, dtype)


def constants():
    basis = np.concatenate(axis_basis(), axis=1)
    order = np.array([4 * s + q for q in range(4) for s in range(8)])

    def left(matrix):
        high, low = np_split(matrix)
        return np.concatenate([high, low, high], axis=1)

    high, low = np_split(np.kron(np.eye(4), basis))
    back_high, back_low = np_split(np.kron(np.eye(4), basis.T))
    fixed = np.zeros((256, 1024), jnp.bfloat16)
    fixed[:128, :256] = high
    fixed[128:, :256] = high
    fixed[:128, 256:512] = low
    fixed[:, 512:640] = back_high
    fixed[:, 640:768] = back_low
    fixed[:G, 768:864] = left(basis.T)
    fixed[G : 2 * G, 768:864] = left(basis[order].T)
    fixed[128:160, 768:960] = left(basis)
    fixed[160:192, 768:960] = left(basis[order])
    return jnp.asarray(fixed)


def exchange(x):
    return lax.all_to_all(x, "own", 0, 0, tiled=True)


def kernel(call, out_shape, in_specs, name, vmem, scratch=(), flops=0, moved=0):
    many = isinstance(out_shape, list)
    return pl.pallas_call(
        call,
        out_shape=out_shape,
        in_specs=in_specs,
        out_specs=[VM] * len(out_shape) if many else VM,
        scratch_shapes=scratch,
        compiler_params=pltpu.CompilerParams(vmem_limit_bytes=vmem << 20),
        cost_estimate=pl.CostEstimate(flops=flops, bytes_accessed=moved, transcendentals=0),
        name=name,
    )


def swapped(x, bits):
    return lax.ppermute(x, "grp", [(g, g ^ bits) for g in range(8)])


def body(orbitals, offsets, pairs, ext_pot):
    owner = lax.axis_index("own")
    fixed = constants()
    pairs = pairs.T

    sent = kernel(
        pack_kernel,
        shape((N, 16, 128), BF16),
        [SM, VM],
        "pack",
        60,
        [pltpu.VMEM((8 * N, 128), F32)],
        moved=200_000,
    )(offsets, orbitals)
    sent, fixed, pairs, ext_pot = lax.optimization_barrier((sent, fixed, pairs, ext_pot))
    recv = exchange(sent)

    fixed, pairs, offsets, green = kernel(
        table_kernel,
        [
            shape((256, 1024), BF16),
            shape((16, 128), jnp.int32),
            shape((8, 128), jnp.int32),
            shape((1024, 256)),
        ],
        [SM, SM, VM, VM],
        "tables",
        16,
        flops=2_000_000,
        moved=3_000_000,
    )(owner.reshape(1), offsets, fixed, pairs)
    plane = lax.dynamic_slice_in_dim(ext_pot, owner, 1, 0).astype(F32)
    plane = plane.reshape(2, B, 2, B).transpose(0, 2, 1, 3).reshape(4, 8, 128)
    recv, fixed, pairs, offsets, green, plane = lax.optimization_barrier(
        (recv, fixed, pairs, offsets, green, plane)
    )

    planes = shape((N, 8, 128))
    rho, dens, phi, code, place = kernel(
        pair_kernel,
        [planes, shape((4, 8, 128)), planes, planes, shape((8, 128))],
        [VM, VM],
        "pair_products",
        4,
        moved=600_000,
    )(pairs, recv)

    mine = exchange(rho)
    others = [swapped(dens, step) for step in (2, 4, 6)]
    field = kernel(
        solve_kernel,
        shape((8 * N, 128)),
        [VM] * 4,
        "solve",
        16,
        [pltpu.VMEM((8 * G, 128), F32)],
        flops=1_000_000_000,
        moved=3_000_000,
    )(place, mine.reshape(8 * N, 128), fixed, green)
    fields = exchange(field.reshape(N, 8, 128))
    dens = (dens + others[1]) + (others[0] + others[2])
    other = swapped(dens, 1)

    gradient = kernel(
        gradient_kernel,
        shape((N, 8, 128)),
        [VM] * 7,
        "gradient_planes",
        4,
        [pltpu.VMEM((N, 8, 128), F32)],
        moved=600_000,
    )(pairs, phi, code, fields, plane, dens, other)
    back = exchange(gradient)

    return kernel(
        unpack_kernel, shape((1, BZ, B * B)), [VM, VM], "unpack", 4, moved=300_000
    )(offsets, back.reshape(8 * N, 128))


def solution(mesh):
    spec = P(("grp", "own"), None, None)
    in_specs = (spec, P(("grp", "own"), None), P("grp", None), P())
    return jax.shard_map(body, mesh=mesh, in_specs=in_specs, out_specs=spec, check_vma=False)
```

```python
import math

import jax
import jax.numpy as jnp
import numpy as np
from jax import lax
from jax.experimental import pallas as pl
from jax.experimental.pallas import tpu as pltpu
from jax.sharding import PartitionSpec as P

B = 32
BZ = 32
G = 64
N = 32
SCREEN = 0.0025
MIXING = 0.25
EXCHANGE_COEF = (3.0 / math.pi) ** (1.0 / 3.0)
F32 = jnp.float32
BF16 = jnp.bfloat16
VM = pl.BlockSpec(memory_space=pltpu.VMEM)
SM = pl.BlockSpec(memory_space=pltpu.SMEM)


def axis_basis():
    position = np.arange(B) - 15.5
    cosine = np.cos(2 * np.pi / G * np.outer(position, np.arange(B)))
    sine = np.sin(2 * np.pi / G * np.outer(position, np.arange(1, B + 1)))
    return cosine, sine


def split(value):
    high = value.astype(BF16)
    low = (value - high.astype(F32)).astype(BF16)
    return high, low


def np_split(value):
    value = value.astype(np.float32)
    high = value.astype(jnp.bfloat16)
    low = (value - high.astype(np.float32)).astype(jnp.bfloat16)
    return high, low


def dot(a, b):
    return jnp.dot(a, b, preferred_element_type=F32)


def torus_roll(load, by_y, by_x):
    lane = lax.broadcasted_iota(jnp.int32, (N, 128), 1)
    by_y = lax.rem(by_y, B)
    by_x = lax.rem(by_x, B)
    rows = lax.div(by_y, 4)
    rest = lax.rem(by_y, 4)
    shift = rest * B + by_x
    near = lax.rem(128 - shift, 128)
    far = lax.rem(128 + B - shift, 128)
    inside = lax.rem(lane, B) < B - by_x
    same = lax.div(lane, B) < 4 - rest
    moved = []
    for s in range(8):
        chunk = load(lax.rem(rows + s, 8))
        moved.append(
            jnp.where(inside, pltpu.roll(chunk, near, 1), pltpu.roll(chunk, far, 1))
        )
    return [jnp.where(same, moved[s], moved[(s + 1) % 8]) for s in range(8)]


def pack_kernel(offsets, box, out, planes):
    oy = offsets[0, 0]
    ox = offsets[0, 1]

    def load(c):
        return box[0, :, pl.ds(pl.multiple_of(c * 128, 128), 128)].astype(F32)

    chunks = torus_roll(load, B - lax.rem(oy, B), B - lax.rem(ox, B))
    for s in range(8):
        planes[pl.ds(s, N, stride=8), :] = chunks[s]
    row = lax.broadcasted_iota(jnp.int32, (8, 128), 0)
    extra = jnp.where(
        row == 0, oy.astype(F32), jnp.where(row == 1, ox.astype(F32), 0.0)
    )
    for z in range(N):
        both = jnp.concatenate([planes[8 * z : 8 * z + 8, :], extra], axis=0)
        out[z] = both.astype(BF16)


def pair_numbers(pairs):
    words = [jnp.max(pairs[r : r + 1, 0:1]) for r in range(11)]
    numbers = []
    for p in range(N):
        pair = lax.shift_right_logical(words[p // 3], jnp.int32(10 * (p % 3)))
        second = lax.bitwise_and(pair, jnp.int32(31))
        first = lax.bitwise_and(lax.shift_right_logical(pair, jnp.int32(5)), jnp.int32(31))
        numbers.append((first, second))
    return numbers


def pair_kernel(pairs, recv, rho, dens, phi, code, place, made, sem):
    numbers = pair_numbers(pairs)
    first = jnp.max(pairs[11:12, 0:1])
    row = lax.broadcasted_iota(jnp.int32, (8, 128), 0)
    lane = lax.broadcasted_iota(jnp.int32, (8, 128), 1)
    y = (row * 4 + lax.div(lane, B)).astype(F32)
    x = lax.rem(lane, B).astype(F32)
    total = [jnp.zeros((8, 128), F32) for _ in range(4)]
    for n in range(N):
        value = recv[n].astype(F32)
        plane = value[:8]
        below = jnp.where(y < value[8:9], 2.0, 0.0)
        quarter = below + jnp.where(x < value[9:10], 1.0, 0.0)
        phi[n] = plane
        code[n] = quarter
    for p in range(N):
        a, b = numbers[p]
        made[p] = jnp.where(code[a] == code[b], phi[a] * phi[b], 0.0)
    send = pltpu.make_async_copy(made, rho, sem)
    send.start()
    place[...] = recv[first].astype(F32)[8:]
    for n in range(N):
        square = phi[n] * phi[n]
        for q in range(4):
            total[q] = total[q] + jnp.where(code[n] == float(q), square, 0.0)
    for q in range(4):
        dens[q] = total[q]
    send.wait()


def wave(index):
    return jnp.where(index < B, index, index - (B - 1))


def weigh(index, value):
    k = wave(index)
    return jnp.where((k == 0) | (k == B), value * 0.5, value)


def square(index):
    k = 2.0 * math.pi / G * wave(index).astype(F32)
    return k * k


def table_kernel(owner, corner, fixed_in, pairs_in, fixed, pairs, offsets, green):
    fixed[...] = fixed_in[...]
    row = lax.broadcasted_iota(jnp.int32, (16, N), 0)
    spot = lax.broadcasted_iota(jnp.int32, (16, N), 1) - 3 * row
    both = pairs_in[0:1, :] * 32 + pairs_in[1:2, :]
    own = lax.broadcasted_iota(jnp.int32, (1, N), 1) == owner[0]
    word = jnp.max(jnp.where(own, pairs_in[0:1, :], 0), axis=1, keepdims=True)
    word = jnp.where(row[:, :1] == 11, word, 0)
    for i in range(3):
        part = jnp.max(jnp.where(spot == i, both, 0), axis=1, keepdims=True)
        word = word + part * (1024**i)
    pairs[...] = jnp.broadcast_to(word, (16, 128))
    offsets[:1, :] = jnp.full((1, 128), corner[0, 0], jnp.int32)
    offsets[1:2, :] = jnp.full((1, 128), corner[0, 1], jnp.int32)
    ky = lax.broadcasted_iota(jnp.int32, (G, 256), 0)
    lane = lax.broadcasted_iota(jnp.int32, (G, 256), 1)
    kx = lax.rem(lane, G)
    level = square(ky) + square(kx) + SCREEN
    weight = weigh(ky, weigh(kx, jnp.full((G, 256), 4.0 * math.pi * 8.0 / G**3, F32)))
    top = lax.div(lax.broadcasted_iota(jnp.int32, (8, 256), 1), G)
    for part in range(16):
        kz = top + 4 * part
        factor = weigh(kz, jnp.ones((8, 256), F32))[:1]
        green[G * part : G * part + G, :] = weight * factor / (level + square(kz)[:1])


def exchange_groups(tiles):
    group = lax.div(lax.broadcasted_iota(jnp.int32, (8, 128), 1), B)
    low = group < 2
    even = lax.rem(group, 2) == 0
    t0, t1, t2, t3 = tiles

    def far(first, second):
        return (
            jnp.where(low, first, pltpu.roll(second, 64, 1)),
            jnp.where(low, pltpu.roll(first, 64, 1), second),
        )

    def near(first, second):
        return (
            jnp.where(even, first, pltpu.roll(second, 32, 1)),
            jnp.where(even, pltpu.roll(first, 96, 1), second),
        )

    u0, u2 = far(t0, t2)
    u1, u3 = far(t1, t3)
    v0, v1 = near(u0, u1)
    v2, v3 = near(u2, u3)
    return [v0, v1, v2, v3]


def thrice(value):
    high, low = split(value)
    return jnp.concatenate([high, high, low], axis=0)


def turn(table, wave_index, cell, start):
    odd = lax.rem(wave(wave_index), 2) == 1
    return jnp.where(odd & (cell < start), -table.astype(F32), table.astype(F32)).astype(BF16)


def solve_kernel(place, rho, fixed, green, out, work):
    oy = jnp.max(place[0:1, :]).astype(jnp.int32)
    ox = jnp.max(place[1:2, :]).astype(jnp.int32)

    def index(dims, axis):
        return lax.broadcasted_iota(jnp.int32, dims, axis)

    def row_of(k):
        k = lax.rem(k, B)
        return lax.rem(k, 8) * 4 + lax.div(k, 8)

    ahead_y = turn(
        fixed[G : 2 * G, 768:864], index((G, 96), 0), row_of(index((G, 96), 1)), oy
    )
    back_y = turn(
        fixed[160:192, 768:960],
        lax.rem(index((N, 192), 1), G),
        row_of(index((N, 192), 0)),
        oy,
    )
    square = (256, 256)
    wave_x = lax.rem(index(square, 1), G)
    cell_x = lax.rem(index(square, 0), B)
    ahead_x = turn(fixed[:, :256], wave_x, cell_x, ox)
    ahead_x_low = turn(fixed[:128, 256:512], wave_x[:128], cell_x[:128], ox)
    wave_x = lax.rem(index(square, 0), G)
    cell_x = lax.rem(index(square, 1), B)
    back_x = turn(fixed[:, 512:768], wave_x, cell_x, ox)

    chunks = [rho[pl.ds(s, N, stride=8), :] for s in range(8)]
    waves = dot(fixed[:G, 768:864], thrice(jnp.concatenate(chunks, axis=1)))
    for s in range(8):
        work[pl.ds(s, G, stride=8), :] = waves[:, 128 * s : 128 * s + 128]

    turned = []
    for c in range(16):
        tiles = [work[8 * k : 8 * k + 8, :] for k in range(4 * c, 4 * c + 4)]
        turned.append(jnp.concatenate(exchange_groups(tiles), axis=0))
    waves = dot(ahead_y, thrice(jnp.concatenate(turned, axis=1)))
    rows = jnp.concatenate([waves[:, 128 * c : 128 * c + 128] for c in range(16)], axis=0)
    halves = []
    for half in range(2):
        high, low = split(rows[512 * half : 512 * half + 512])
        waves = dot(jnp.concatenate([high, low], axis=1), ahead_x)
        halves.append(waves + dot(high, ahead_x_low))
    pieces = []
    for half in range(2):
        high, low = split(halves[half] * green[512 * half : 512 * half + 512, :])
        both = dot(high, back_x)
        pieces.append(both[:, :128] + both[:, 128:] + dot(low, back_x[:, :128]))
    rows = jnp.concatenate(pieces, axis=0)
    levels = jnp.concatenate([rows[G * c : G * c + G, :] for c in range(16)], axis=1)
    levels = dot(back_y, thrice(levels))
    for c in range(16):
        tiles = [levels[8 * q : 8 * q + 8, 128 * c : 128 * c + 128] for q in range(4)]
        for i, tile in enumerate(exchange_groups(tiles)):
            k = 4 * c + i
            work[8 * k : 8 * k + 8, :] = tile

    levels = jnp.concatenate([work[pl.ds(s, G, stride=8), :] for s in range(8)], axis=1)
    field = dot(fixed[128:160, 768:960], thrice(levels))
    for s in range(8):
        out[pl.ds(s, N, stride=8), :] = field[:, 128 * s : 128 * s + 128]


def cube_root(value):
    rough = jnp.exp(jnp.log(jnp.where(value > 0.0, value, 1.0)) * (1.0 / 3.0))
    finer = rough - (rough - value / (rough * rough)) * (1.0 / 3.0)
    return jnp.where(value > 0.0, finer, 0.0)


def gradient_kernel(pairs, phi, code, field, plane, dens, other, out, terms):
    numbers = pair_numbers(pairs)
    quarters = []
    for q in range(4):
        quarters.append(plane[q] - EXCHANGE_COEF * cube_root(dens[q] + other[q]))
    for n in range(N):
        terms[n] = jnp.zeros((8, 128), F32)
    for p in range(N):
        a, b = numbers[p]
        value = jnp.where(code[a] == code[b], field[p], 0.0)
        terms[a] = terms[a] + value * phi[b]
        terms[b] = terms[b] + value * phi[a]
    for n in range(N):
        quarter = code[n]
        local = jnp.where(
            quarter < 1.5,
            jnp.where(quarter < 0.5, quarters[0], quarters[1]),
            jnp.where(quarter < 2.5, quarters[2], quarters[3]),
        )
        out[n] = local * phi[n] - MIXING * terms[n]


def unpack_kernel(offsets, planes, out):
    oy = jnp.max(offsets[0:1, :])
    ox = jnp.max(offsets[1:2, :])
    chunks = torus_roll(lambda c: planes[pl.ds(c, N, stride=8), :], oy, ox)
    for s in range(8):
        out[0, :, 128 * s : 128 * s + 128] = chunks[s]


def shape(dims, dtype=F32):
    return jax.ShapeDtypeStruct(dims, dtype)


def constants():
    basis = np.concatenate(axis_basis(), axis=1)
    order = np.array([4 * s + q for q in range(4) for s in range(8)])

    def left(matrix):
        high, low = np_split(matrix)
        return np.concatenate([high, low, high], axis=1)

    high, low = np_split(np.kron(np.eye(4), basis))
    back_high, back_low = np_split(np.kron(np.eye(4), basis.T))
    fixed = np.zeros((256, 1024), jnp.bfloat16)
    fixed[:128, :256] = high
    fixed[128:, :256] = high
    fixed[:128, 256:512] = low
    fixed[:, 512:640] = back_high
    fixed[:, 640:768] = back_low
    fixed[:G, 768:864] = left(basis.T)
    fixed[G : 2 * G, 768:864] = left(basis[order].T)
    fixed[128:160, 768:960] = left(basis)
    fixed[160:192, 768:960] = left(basis[order])
    return jnp.asarray(fixed)


def exchange(x):
    return lax.all_to_all(x, "own", 0, 0, tiled=True)


def kernel(call, out_shape, in_specs, name, vmem, scratch=(), flops=0, moved=0):
    many = isinstance(out_shape, list)
    return pl.pallas_call(
        call,
        out_shape=out_shape,
        in_specs=in_specs,
        out_specs=[VM] * len(out_shape) if many else VM,
        scratch_shapes=scratch,
        compiler_params=pltpu.CompilerParams(vmem_limit_bytes=vmem << 20),
        cost_estimate=pl.CostEstimate(flops=flops, bytes_accessed=moved, transcendentals=0),
        name=name,
    )


def swapped(x, bits):
    return lax.ppermute(x, "grp", [(g, g ^ bits) for g in range(8)])


def body(orbitals, offsets, pairs, ext_pot):
    owner = lax.axis_index("own")
    fixed = constants()
    pairs = pairs.T

    sent = kernel(
        pack_kernel,
        shape((N, 16, 128), BF16),
        [SM, VM],
        "pack",
        60,
        [pltpu.VMEM((8 * N, 128), F32)],
        moved=200_000,
    )(offsets, orbitals)
    sent, fixed, pairs, ext_pot = lax.optimization_barrier((sent, fixed, pairs, ext_pot))
    recv = exchange(sent)

    fixed, pairs, offsets, green = kernel(
        table_kernel,
        [
            shape((256, 1024), BF16),
            shape((16, 128), jnp.int32),
            shape((8, 128), jnp.int32),
            shape((1024, 256)),
        ],
        [SM, SM, VM, VM],
        "tables",
        16,
        flops=2_000_000,
        moved=3_000_000,
    )(owner.reshape(1), offsets, fixed, pairs)
    plane = lax.dynamic_slice_in_dim(ext_pot, owner, 1, 0).astype(F32)
    plane = plane.reshape(2, B, 2, B).transpose(0, 2, 1, 3).reshape(4, 8, 128)
    recv, fixed, pairs, offsets, green, plane = lax.optimization_barrier(
        (recv, fixed, pairs, offsets, green, plane)
    )

    planes = shape((N, 8, 128))
    rho, dens, phi, code, place = pl.pallas_call(
        pair_kernel,
        out_shape=[planes, shape((4, 8, 128)), planes, planes, shape((8, 128))],
        in_specs=[VM, VM],
        out_specs=[pl.BlockSpec(memory_space=pltpu.HBM)] + [VM] * 4,
        scratch_shapes=[pltpu.VMEM((N, 8, 128), F32), pltpu.SemaphoreType.DMA(())],
        compiler_params=pltpu.CompilerParams(vmem_limit_bytes=4 << 20),
        cost_estimate=pl.CostEstimate(flops=0, bytes_accessed=600_000, transcendentals=0),
        name="pair_products",
    )(pairs, recv)

    mine = exchange(rho)
    others = [swapped(dens, step) for step in (2, 4, 6)]
    field = kernel(
        solve_kernel,
        shape((8 * N, 128)),
        [VM] * 4,
        "solve",
        16,
        [pltpu.VMEM((8 * G, 128), F32)],
        flops=1_000_000_000,
        moved=3_000_000,
    )(place, mine.reshape(8 * N, 128), fixed, green)
    fields = exchange(field.reshape(N, 8, 128))
    dens = (dens + others[1]) + (others[0] + others[2])
    other = swapped(dens, 1)

    gradient = kernel(
        gradient_kernel,
        shape((N, 8, 128)),
        [VM] * 7,
        "gradient_planes",
        4,
        [pltpu.VMEM((N, 8, 128), F32)],
        moved=600_000,
    )(pairs, phi, code, fields, plane, dens, other)
    back = exchange(gradient)

    return kernel(
        unpack_kernel, shape((1, BZ, B * B)), [VM, VM], "unpack", 4, moved=300_000
    )(offsets, back.reshape(8 * N, 128))


def solution(mesh):
    spec = P(("grp", "own"), None, None)
    in_specs = (spec, P(("grp", "own"), None), P("grp", None), P())
    return jax.shard_map(body, mesh=mesh, in_specs=in_specs, out_specs=spec, check_vma=False)
```

```python
import math

import jax
import jax.numpy as jnp
import numpy as np
from jax import lax
from jax.experimental import pallas as pl
from jax.experimental.pallas import tpu as pltpu
from jax.sharding import PartitionSpec as P

B = 32
BZ = 32
G = 64
N = 32
SCREEN = 0.0025
MIXING = 0.25
EXCHANGE_COEF = (3.0 / math.pi) ** (1.0 / 3.0)
F32 = jnp.float32
BF16 = jnp.bfloat16
VM = pl.BlockSpec(memory_space=pltpu.VMEM)
SM = pl.BlockSpec(memory_space=pltpu.SMEM)


def axis_basis():
    position = np.arange(B) - 15.5
    cosine = np.cos(2 * np.pi / G * np.outer(position, np.arange(B)))
    sine = np.sin(2 * np.pi / G * np.outer(position, np.arange(1, B + 1)))
    return cosine, sine


def split(value):
    high = value.astype(BF16)
    low = (value - high.astype(F32)).astype(BF16)
    return high, low


def np_split(value):
    value = value.astype(np.float32)
    high = value.astype(jnp.bfloat16)
    low = (value - high.astype(np.float32)).astype(jnp.bfloat16)
    return high, low


def dot(a, b):
    return jnp.dot(a, b, preferred_element_type=F32)


def torus_roll(load, by_y, by_x):
    lane = lax.broadcasted_iota(jnp.int32, (N, 128), 1)
    by_y = lax.rem(by_y, B)
    by_x = lax.rem(by_x, B)
    rows = lax.div(by_y, 4)
    rest = lax.rem(by_y, 4)
    shift = rest * B + by_x
    near = lax.rem(128 - shift, 128)
    far = lax.rem(128 + B - shift, 128)
    inside = lax.rem(lane, B) < B - by_x
    same = lax.div(lane, B) < 4 - rest
    moved = []
    for s in range(8):
        chunk = load(lax.rem(rows + s, 8))
        moved.append(
            jnp.where(inside, pltpu.roll(chunk, near, 1), pltpu.roll(chunk, far, 1))
        )
    return [jnp.where(same, moved[s], moved[(s + 1) % 8]) for s in range(8)]


def pack_kernel(offsets, box, out, planes):
    oy = offsets[0, 0]
    ox = offsets[0, 1]

    def load(c):
        return box[0, :, pl.ds(pl.multiple_of(c * 128, 128), 128)].astype(F32)

    chunks = torus_roll(load, B - lax.rem(oy, B), B - lax.rem(ox, B))
    for s in range(8):
        planes[pl.ds(s, N, stride=8), :] = chunks[s]
    row = lax.broadcasted_iota(jnp.int32, (8, 128), 0)
    extra = jnp.where(
        row == 0, oy.astype(F32), jnp.where(row == 1, ox.astype(F32), 0.0)
    )
    for z in range(N):
        both = jnp.concatenate([planes[8 * z : 8 * z + 8, :], extra], axis=0)
        out[z] = both.astype(BF16)


def pair_numbers(pairs):
    words = [jnp.max(pairs[r : r + 1, 0:1]) for r in range(11)]
    numbers = []
    for p in range(N):
        pair = lax.shift_right_logical(words[p // 3], jnp.int32(10 * (p % 3)))
        second = lax.bitwise_and(pair, jnp.int32(31))
        first = lax.bitwise_and(lax.shift_right_logical(pair, jnp.int32(5)), jnp.int32(31))
        numbers.append((first, second))
    return numbers


def pair_kernel(pairs, recv, rho, dens, phi, code, place, made, sem):
    numbers = pair_numbers(pairs)
    first = jnp.max(pairs[11:12, 0:1])
    row = lax.broadcasted_iota(jnp.int32, (8, 128), 0)
    lane = lax.broadcasted_iota(jnp.int32, (8, 128), 1)
    y = (row * 4 + lax.div(lane, B)).astype(F32)
    x = lax.rem(lane, B).astype(F32)
    total = [jnp.zeros((8, 128), F32) for _ in range(4)]
    for n in range(N):
        value = recv[n].astype(F32)
        plane = value[:8]
        below = jnp.where(y < value[8:9], 2.0, 0.0)
        quarter = below + jnp.where(x < value[9:10], 1.0, 0.0)
        phi[n] = plane
        code[n] = quarter
    for p in range(N):
        a, b = numbers[p]
        made[p] = jnp.where(code[a] == code[b], phi[a] * phi[b], 0.0)
    send = pltpu.make_async_copy(made, rho, sem)
    send.start()
    place[...] = recv[first].astype(F32)[8:]
    for n in range(N):
        square = phi[n] * phi[n]
        for q in range(4):
            total[q] = total[q] + jnp.where(code[n] == float(q), square, 0.0)
    for q in range(4):
        dens[q] = total[q]
    send.wait()


def wave(index):
    return jnp.where(index < B, index, index - (B - 1))


def weigh(index, value):
    k = wave(index)
    return jnp.where((k == 0) | (k == B), value * 0.5, value)


def square(index):
    k = 2.0 * math.pi / G * wave(index).astype(F32)
    return k * k


def table_kernel(owner, corner, fixed_in, pairs_in, fixed, pairs, offsets, green):
    fixed[...] = fixed_in[...]
    row = lax.broadcasted_iota(jnp.int32, (16, N), 0)
    spot = lax.broadcasted_iota(jnp.int32, (16, N), 1) - 3 * row
    both = pairs_in[0:1, :] * 32 + pairs_in[1:2, :]
    own = lax.broadcasted_iota(jnp.int32, (1, N), 1) == owner[0]
    word = jnp.max(jnp.where(own, pairs_in[0:1, :], 0), axis=1, keepdims=True)
    word = jnp.where(row[:, :1] == 11, word, 0)
    for i in range(3):
        part = jnp.max(jnp.where(spot == i, both, 0), axis=1, keepdims=True)
        word = word + part * (1024**i)
    pairs[...] = jnp.broadcast_to(word, (16, 128))
    offsets[:1, :] = jnp.full((1, 128), corner[0, 0], jnp.int32)
    offsets[1:2, :] = jnp.full((1, 128), corner[0, 1], jnp.int32)
    ky = lax.broadcasted_iota(jnp.int32, (G, 256), 0)
    lane = lax.broadcasted_iota(jnp.int32, (G, 256), 1)
    kx = lax.rem(lane, G)
    level = square(ky) + square(kx) + SCREEN
    weight = weigh(ky, weigh(kx, jnp.full((G, 256), 4.0 * math.pi * 8.0 / G**3, F32)))
    top = lax.div(lax.broadcasted_iota(jnp.int32, (8, 256), 1), G)
    for part in range(16):
        kz = top + 4 * part
        factor = weigh(kz, jnp.ones((8, 256), F32))[:1]
        green[G * part : G * part + G, :] = weight * factor / (level + square(kz)[:1])


def exchange_groups(tiles):
    group = lax.div(lax.broadcasted_iota(jnp.int32, (8, 128), 1), B)
    low = group < 2
    even = lax.rem(group, 2) == 0
    t0, t1, t2, t3 = tiles

    def far(first, second):
        return (
            jnp.where(low, first, pltpu.roll(second, 64, 1)),
            jnp.where(low, pltpu.roll(first, 64, 1), second),
        )

    def near(first, second):
        return (
            jnp.where(even, first, pltpu.roll(second, 32, 1)),
            jnp.where(even, pltpu.roll(first, 96, 1), second),
        )

    u0, u2 = far(t0, t2)
    u1, u3 = far(t1, t3)
    v0, v1 = near(u0, u1)
    v2, v3 = near(u2, u3)
    return [v0, v1, v2, v3]


def thrice(value):
    high, low = split(value)
    return jnp.concatenate([high, high, low], axis=0)


def turn(table, wave_index, cell, start):
    odd = lax.rem(wave(wave_index), 2) == 1
    return jnp.where(odd & (cell < start), -table.astype(F32), table.astype(F32)).astype(BF16)


def solve_kernel(place, rho, fixed, green, out, work):
    oy = jnp.max(place[0:1, :]).astype(jnp.int32)
    ox = jnp.max(place[1:2, :]).astype(jnp.int32)

    def index(dims, axis):
        return lax.broadcasted_iota(jnp.int32, dims, axis)

    def row_of(k):
        k = lax.rem(k, B)
        return lax.rem(k, 8) * 4 + lax.div(k, 8)

    ahead_y = turn(
        fixed[G : 2 * G, 768:864], index((G, 96), 0), row_of(index((G, 96), 1)), oy
    )
    back_y = turn(
        fixed[160:192, 768:960],
        lax.rem(index((N, 192), 1), G),
        row_of(index((N, 192), 0)),
        oy,
    )
    square = (256, 256)
    wave_x = lax.rem(index(square, 1), G)
    cell_x = lax.rem(index(square, 0), B)
    ahead_x = turn(fixed[:, :256], wave_x, cell_x, ox)
    ahead_x_low = turn(fixed[:128, 256:512], wave_x[:128], cell_x[:128], ox)
    wave_x = lax.rem(index(square, 0), G)
    cell_x = lax.rem(index(square, 1), B)
    back_x = turn(fixed[:, 512:768], wave_x, cell_x, ox)

    chunks = [rho[pl.ds(s, N, stride=8), :] for s in range(8)]
    waves = dot(fixed[:G, 768:864], thrice(jnp.concatenate(chunks, axis=1)))
    for s in range(8):
        work[pl.ds(s, G, stride=8), :] = waves[:, 128 * s : 128 * s + 128]

    turned = []
    for c in range(16):
        tiles = [work[8 * k : 8 * k + 8, :] for k in range(4 * c, 4 * c + 4)]
        turned.append(jnp.concatenate(exchange_groups(tiles), axis=0))
    waves = dot(ahead_y, thrice(jnp.concatenate(turned, axis=1)))
    rows = jnp.concatenate([waves[:, 128 * c : 128 * c + 128] for c in range(16)], axis=0)
    halves = []
    for half in range(2):
        high, low = split(rows[512 * half : 512 * half + 512])
        waves = dot(jnp.concatenate([high, low], axis=1), ahead_x)
        halves.append(waves + dot(high, ahead_x_low))
    pieces = []
    for half in range(2):
        high, low = split(halves[half] * green[512 * half : 512 * half + 512, :])
        both = dot(high, back_x)
        pieces.append(both[:, :128] + both[:, 128:] + dot(low, back_x[:, :128]))
    rows = jnp.concatenate(pieces, axis=0)
    levels = jnp.concatenate([rows[G * c : G * c + G, :] for c in range(16)], axis=1)
    levels = dot(back_y, thrice(levels))
    for c in range(16):
        tiles = [levels[8 * q : 8 * q + 8, 128 * c : 128 * c + 128] for q in range(4)]
        for i, tile in enumerate(exchange_groups(tiles)):
            k = 4 * c + i
            work[8 * k : 8 * k + 8, :] = tile

    levels = jnp.concatenate([work[pl.ds(s, G, stride=8), :] for s in range(8)], axis=1)
    field = dot(fixed[128:160, 768:960], thrice(levels))
    for s in range(8):
        out[pl.ds(s, N, stride=8), :] = field[:, 128 * s : 128 * s + 128]


def cube_root(value):
    rough = jnp.exp(jnp.log(jnp.where(value > 0.0, value, 1.0)) * (1.0 / 3.0))
    finer = rough - (rough - value / (rough * rough)) * (1.0 / 3.0)
    return jnp.where(value > 0.0, finer, 0.0)


def gradient_kernel(pairs, phi, code, field, plane, dens, other, out, terms):
    numbers = pair_numbers(pairs)
    quarters = []
    for q in range(4):
        quarters.append(plane[q] - EXCHANGE_COEF * cube_root(dens[q] + other[q]))
    for n in range(N):
        terms[n] = jnp.zeros((8, 128), F32)
    for p in range(N):
        a, b = numbers[p]
        value = jnp.where(code[a] == code[b], field[p], 0.0)
        terms[a] = terms[a] + value * phi[b]
        terms[b] = terms[b] + value * phi[a]
    for n in range(N):
        quarter = code[n]
        local = jnp.where(
            quarter < 1.5,
            jnp.where(quarter < 0.5, quarters[0], quarters[1]),
            jnp.where(quarter < 2.5, quarters[2], quarters[3]),
        )
        out[n] = local * phi[n] - MIXING * terms[n]


def unpack_kernel(offsets, planes, out):
    oy = jnp.max(offsets[0:1, :])
    ox = jnp.max(offsets[1:2, :])
    chunks = torus_roll(lambda c: planes[pl.ds(c, N, stride=8), :], oy, ox)
    for s in range(8):
        out[0, :, 128 * s : 128 * s + 128] = chunks[s]


def shape(dims, dtype=F32):
    return jax.ShapeDtypeStruct(dims, dtype)


def constants():
    basis = np.concatenate(axis_basis(), axis=1)
    order = np.array([4 * s + q for q in range(4) for s in range(8)])

    def left(matrix):
        high, low = np_split(matrix)
        return np.concatenate([high, low, high], axis=1)

    high, low = np_split(np.kron(np.eye(4), basis))
    back_high, back_low = np_split(np.kron(np.eye(4), basis.T))
    fixed = np.zeros((256, 1024), jnp.bfloat16)
    fixed[:128, :256] = high
    fixed[128:, :256] = high
    fixed[:128, 256:512] = low
    fixed[:, 512:640] = back_high
    fixed[:, 640:768] = back_low
    fixed[:G, 768:864] = left(basis.T)
    fixed[G : 2 * G, 768:864] = left(basis[order].T)
    fixed[128:160, 768:960] = left(basis)
    fixed[160:192, 768:960] = left(basis[order])
    return jnp.asarray(fixed)


def exchange(x):
    return lax.all_to_all(x, "own", 0, 0, tiled=True)


def kernel(call, out_shape, in_specs, name, vmem, scratch=(), flops=0, moved=0):
    many = isinstance(out_shape, list)
    return pl.pallas_call(
        call,
        out_shape=out_shape,
        in_specs=in_specs,
        out_specs=[VM] * len(out_shape) if many else VM,
        scratch_shapes=scratch,
        compiler_params=pltpu.CompilerParams(vmem_limit_bytes=vmem << 20),
        cost_estimate=pl.CostEstimate(flops=flops, bytes_accessed=moved, transcendentals=0),
        name=name,
    )


def swapped(x, bits):
    return lax.ppermute(x, "grp", [(g, g ^ bits) for g in range(8)])


def body(orbitals, offsets, pairs, ext_pot):
    owner = lax.axis_index("own")
    fixed = constants()
    pairs = pairs.T

    sent = kernel(
        pack_kernel,
        shape((N, 16, 128), BF16),
        [SM, VM],
        "pack",
        60,
        [pltpu.VMEM((8 * N, 128), F32)],
        moved=200_000,
    )(offsets, orbitals)
    sent, fixed, pairs, ext_pot = lax.optimization_barrier((sent, fixed, pairs, ext_pot))
    recv = exchange(sent)

    fixed, pairs, offsets, green = kernel(
        table_kernel,
        [
            shape((256, 1024), BF16),
            shape((16, 128), jnp.int32),
            shape((8, 128), jnp.int32),
            shape((1024, 256)),
        ],
        [SM, SM, VM, VM],
        "tables",
        16,
        flops=2_000_000,
        moved=3_000_000,
    )(owner.reshape(1), offsets, fixed, pairs)
    plane = lax.dynamic_slice_in_dim(ext_pot, owner, 1, 0).astype(F32)
    plane = plane.reshape(2, B, 2, B).transpose(0, 2, 1, 3).reshape(4, 8, 128)
    recv, fixed, pairs, offsets, green, plane = lax.optimization_barrier(
        (recv, fixed, pairs, offsets, green, plane)
    )

    planes = shape((N, 8, 128))
    rho, dens, phi, code, place = pl.pallas_call(
        pair_kernel,
        out_shape=[planes, shape((4, 8, 128)), planes, planes, shape((8, 128))],
        in_specs=[VM, VM],
        out_specs=[pl.BlockSpec(memory_space=pltpu.HBM)] + [VM] * 4,
        scratch_shapes=[pltpu.VMEM((N, 8, 128), F32), pltpu.SemaphoreType.DMA(())],
        compiler_params=pltpu.CompilerParams(vmem_limit_bytes=4 << 20),
        cost_estimate=pl.CostEstimate(flops=0, bytes_accessed=600_000, transcendentals=0),
        name="pair_products",
    )(pairs, recv)

    mine = exchange(rho)
    others = [swapped(dens, bits) for bits in (2, 4, 6)]
    dens = (dens + others[1]) + (others[0] + others[2])
    mine, dens = lax.optimization_barrier((mine, dens))
    other = swapped(dens, 1)
    field = kernel(
        solve_kernel,
        shape((8 * N, 128)),
        [VM] * 4,
        "solve",
        16,
        [pltpu.VMEM((8 * G, 128), F32)],
        flops=1_000_000_000,
        moved=3_000_000,
    )(place, mine.reshape(8 * N, 128), fixed, green)
    field, other = lax.optimization_barrier((field, other))
    fields = exchange(field.reshape(N, 8, 128))

    gradient = kernel(
        gradient_kernel,
        shape((N, 8, 128)),
        [VM] * 7,
        "gradient_planes",
        4,
        [pltpu.VMEM((N, 8, 128), F32)],
        moved=600_000,
    )(pairs, phi, code, fields, plane, dens, other)
    back = exchange(gradient)

    return kernel(
        unpack_kernel, shape((1, BZ, B * B)), [VM, VM], "unpack", 4, moved=300_000
    )(offsets, back.reshape(8 * N, 128))


def solution(mesh):
    spec = P(("grp", "own"), None, None)
    in_specs = (spec, P(("grp", "own"), None), P("grp", None), P())
    return jax.shard_map(body, mesh=mesh, in_specs=in_specs, out_specs=spec, check_vma=False)
```

```python
import math

import jax
import jax.numpy as jnp
import numpy as np
from jax import lax
from jax.experimental import pallas as pl
from jax.experimental.pallas import tpu as pltpu
from jax.sharding import PartitionSpec as P

B = 32
BZ = 32
G = 64
N = 32
SCREEN = 0.0025
MIXING = 0.25
EXCHANGE_COEF = (3.0 / math.pi) ** (1.0 / 3.0)
F32 = jnp.float32
BF16 = jnp.bfloat16
VM = pl.BlockSpec(memory_space=pltpu.VMEM)
SM = pl.BlockSpec(memory_space=pltpu.SMEM)


def axis_basis():
    position = np.arange(B) - 15.5
    cosine = np.cos(2 * np.pi / G * np.outer(position, np.arange(B)))
    sine = np.sin(2 * np.pi / G * np.outer(position, np.arange(1, B + 1)))
    return cosine, sine


def split(value):
    high = value.astype(BF16)
    low = (value - high.astype(F32)).astype(BF16)
    return high, low


def np_split(value):
    value = value.astype(np.float32)
    high = value.astype(jnp.bfloat16)
    low = (value - high.astype(np.float32)).astype(jnp.bfloat16)
    return high, low


def dot(a, b):
    return jnp.dot(a, b, preferred_element_type=F32)


def torus_roll(load, by_y, by_x):
    lane = lax.broadcasted_iota(jnp.int32, (N, 128), 1)
    by_y = lax.rem(by_y, B)
    by_x = lax.rem(by_x, B)
    rows = lax.div(by_y, 4)
    rest = lax.rem(by_y, 4)
    shift = rest * B + by_x
    near = lax.rem(128 - shift, 128)
    far = lax.rem(128 + B - shift, 128)
    inside = lax.rem(lane, B) < B - by_x
    same = lax.div(lane, B) < 4 - rest
    moved = []
    for s in range(8):
        chunk = load(lax.rem(rows + s, 8))
        moved.append(
            jnp.where(inside, pltpu.roll(chunk, near, 1), pltpu.roll(chunk, far, 1))
        )
    return [jnp.where(same, moved[s], moved[(s + 1) % 8]) for s in range(8)]


def pack_kernel(offsets, box, out, planes):
    oy = offsets[0, 0]
    ox = offsets[0, 1]

    def load(c):
        return box[0, :, pl.ds(pl.multiple_of(c * 128, 128), 128)].astype(F32)

    chunks = torus_roll(load, B - lax.rem(oy, B), B - lax.rem(ox, B))
    for s in range(8):
        planes[pl.ds(s, N, stride=8), :] = chunks[s]
    row = lax.broadcasted_iota(jnp.int32, (8, 128), 0)
    extra = jnp.where(
        row == 0, oy.astype(F32), jnp.where(row == 1, ox.astype(F32), 0.0)
    )
    for z in range(N):
        both = jnp.concatenate([planes[8 * z : 8 * z + 8, :], extra], axis=0)
        out[z] = both.astype(BF16)


def pair_numbers(pairs):
    words = [jnp.max(pairs[r : r + 1, 0:1]) for r in range(11)]
    numbers = []
    for p in range(N):
        pair = lax.shift_right_logical(words[p // 3], jnp.int32(10 * (p % 3)))
        second = lax.bitwise_and(pair, jnp.int32(31))
        first = lax.bitwise_and(lax.shift_right_logical(pair, jnp.int32(5)), jnp.int32(31))
        numbers.append((first, second))
    return numbers


def pair_kernel(pairs, recv, rho, dens, phi, code, place, made, sem):
    numbers = pair_numbers(pairs)
    first = jnp.max(pairs[11:12, 0:1])
    row = lax.broadcasted_iota(jnp.int32, (8, 128), 0)
    lane = lax.broadcasted_iota(jnp.int32, (8, 128), 1)
    y = (row * 4 + lax.div(lane, B)).astype(F32)
    x = lax.rem(lane, B).astype(F32)
    total = [jnp.zeros((8, 128), F32) for _ in range(4)]
    for n in range(N):
        value = recv[n].astype(F32)
        plane = value[:8]
        below = jnp.where(y < value[8:9], 2.0, 0.0)
        quarter = below + jnp.where(x < value[9:10], 1.0, 0.0)
        phi[n] = plane
        code[n] = quarter
    for p in range(N):
        a, b = numbers[p]
        made[p] = jnp.where(code[a] == code[b], phi[a] * phi[b], 0.0)
    send = pltpu.make_async_copy(made, rho, sem)
    send.start()
    place[...] = recv[first].astype(F32)[8:]
    for n in range(N):
        square = phi[n] * phi[n]
        for q in range(4):
            total[q] = total[q] + jnp.where(code[n] == float(q), square, 0.0)
    for q in range(4):
        dens[q] = total[q]
    send.wait()


def wave(index):
    return jnp.where(index < B, index, index - (B - 1))


def weigh(index, value):
    k = wave(index)
    return jnp.where((k == 0) | (k == B), value * 0.5, value)


def square(index):
    k = 2.0 * math.pi / G * wave(index).astype(F32)
    return k * k


def table_kernel(owner, corner, fixed_in, pairs_in, fixed, pairs, offsets, green):
    fixed[...] = fixed_in[...]
    row = lax.broadcasted_iota(jnp.int32, (16, N), 0)
    spot = lax.broadcasted_iota(jnp.int32, (16, N), 1) - 3 * row
    both = pairs_in[0:1, :] * 32 + pairs_in[1:2, :]
    own = lax.broadcasted_iota(jnp.int32, (1, N), 1) == owner[0]
    word = jnp.max(jnp.where(own, pairs_in[0:1, :], 0), axis=1, keepdims=True)
    word = jnp.where(row[:, :1] == 11, word, 0)
    for i in range(3):
        part = jnp.max(jnp.where(spot == i, both, 0), axis=1, keepdims=True)
        word = word + part * (1024**i)
    pairs[...] = jnp.broadcast_to(word, (16, 128))
    offsets[:1, :] = jnp.full((1, 128), corner[0, 0], jnp.int32)
    offsets[1:2, :] = jnp.full((1, 128), corner[0, 1], jnp.int32)
    ky = lax.broadcasted_iota(jnp.int32, (G, 256), 0)
    lane = lax.broadcasted_iota(jnp.int32, (G, 256), 1)
    kx = lax.rem(lane, G)
    level = square(ky) + square(kx) + SCREEN
    weight = weigh(ky, weigh(kx, jnp.full((G, 256), 4.0 * math.pi * 8.0 / G**3, F32)))
    top = lax.div(lax.broadcasted_iota(jnp.int32, (8, 256), 1), G)
    for part in range(16):
        kz = top + 4 * part
        factor = weigh(kz, jnp.ones((8, 256), F32))[:1]
        green[G * part : G * part + G, :] = weight * factor / (level + square(kz)[:1])


def exchange_groups(tiles):
    group = lax.div(lax.broadcasted_iota(jnp.int32, (8, 128), 1), B)
    low = group < 2
    even = lax.rem(group, 2) == 0
    t0, t1, t2, t3 = tiles

    def far(first, second):
        return (
            jnp.where(low, first, pltpu.roll(second, 64, 1)),
            jnp.where(low, pltpu.roll(first, 64, 1), second),
        )

    def near(first, second):
        return (
            jnp.where(even, first, pltpu.roll(second, 32, 1)),
            jnp.where(even, pltpu.roll(first, 96, 1), second),
        )

    u0, u2 = far(t0, t2)
    u1, u3 = far(t1, t3)
    v0, v1 = near(u0, u1)
    v2, v3 = near(u2, u3)
    return [v0, v1, v2, v3]


def thrice(value):
    high, low = split(value)
    return jnp.concatenate([high, high, low], axis=0)


def turn(table, wave_index, cell, start):
    odd = lax.rem(wave(wave_index), 2) == 1
    return jnp.where(odd & (cell < start), -table.astype(F32), table.astype(F32)).astype(BF16)


def solve_kernel(place, rho, fixed, green, out, work):
    oy = jnp.max(place[0:1, :]).astype(jnp.int32)
    ox = jnp.max(place[1:2, :]).astype(jnp.int32)

    def index(dims, axis):
        return lax.broadcasted_iota(jnp.int32, dims, axis)

    def row_of(k):
        k = lax.rem(k, B)
        return lax.rem(k, 8) * 4 + lax.div(k, 8)

    ahead_y = turn(
        fixed[G : 2 * G, 768:864], index((G, 96), 0), row_of(index((G, 96), 1)), oy
    )
    back_y = turn(
        fixed[160:192, 768:960],
        lax.rem(index((N, 192), 1), G),
        row_of(index((N, 192), 0)),
        oy,
    )
    square = (256, 256)
    wave_x = lax.rem(index(square, 1), G)
    cell_x = lax.rem(index(square, 0), B)
    ahead_x = turn(fixed[:, :256], wave_x, cell_x, ox)
    ahead_x_low = turn(fixed[:128, 256:512], wave_x[:128], cell_x[:128], ox)
    wave_x = lax.rem(index(square, 0), G)
    cell_x = lax.rem(index(square, 1), B)
    back_x = turn(fixed[:, 512:768], wave_x, cell_x, ox)

    chunks = [rho[pl.ds(s, N, stride=8), :] for s in range(8)]
    waves = dot(fixed[:G, 768:864], thrice(jnp.concatenate(chunks, axis=1)))
    for s in range(8):
        work[pl.ds(s, G, stride=8), :] = waves[:, 128 * s : 128 * s + 128]

    turned = []
    for c in range(16):
        tiles = [work[8 * k : 8 * k + 8, :] for k in range(4 * c, 4 * c + 4)]
        turned.append(jnp.concatenate(exchange_groups(tiles), axis=0))
    waves = dot(ahead_y, thrice(jnp.concatenate(turned, axis=1)))
    rows = jnp.concatenate([waves[:, 128 * c : 128 * c + 128] for c in range(16)], axis=0)
    both_x = jnp.concatenate([ahead_x, ahead_x_low], axis=0)
    halves = []
    for half in range(2):
        high, low = split(rows[512 * half : 512 * half + 512])
        halves.append(dot(jnp.concatenate([high, low, high], axis=1), both_x))
    pieces = []
    for half in range(2):
        high, low = split(halves[half] * green[512 * half : 512 * half + 512, :])
        both = dot(high, back_x)
        pieces.append(both[:, :128] + both[:, 128:] + dot(low, back_x[:, :128]))
    rows = jnp.concatenate(pieces, axis=0)
    levels = jnp.concatenate([rows[G * c : G * c + G, :] for c in range(16)], axis=1)
    levels = dot(back_y, thrice(levels))
    for c in range(16):
        tiles = [levels[8 * q : 8 * q + 8, 128 * c : 128 * c + 128] for q in range(4)]
        for i, tile in enumerate(exchange_groups(tiles)):
            k = 4 * c + i
            work[8 * k : 8 * k + 8, :] = tile

    levels = jnp.concatenate([work[pl.ds(s, G, stride=8), :] for s in range(8)], axis=1)
    field = dot(fixed[128:160, 768:960], thrice(levels))
    for s in range(8):
        out[pl.ds(s, N, stride=8), :] = field[:, 128 * s : 128 * s + 128]


def cube_root(value):
    rough = jnp.exp(jnp.log(jnp.where(value > 0.0, value, 1.0)) * (1.0 / 3.0))
    finer = rough - (rough - value / (rough * rough)) * (1.0 / 3.0)
    return jnp.where(value > 0.0, finer, 0.0)


def gradient_kernel(pairs, phi, code, field, plane, dens, other, out, terms):
    numbers = pair_numbers(pairs)
    quarters = []
    for q in range(4):
        quarters.append(plane[q] - EXCHANGE_COEF * cube_root(dens[q] + other[q]))
    for n in range(N):
        terms[n] = jnp.zeros((8, 128), F32)
    for p in range(N):
        a, b = numbers[p]
        value = jnp.where(code[a] == code[b], field[p], 0.0)
        terms[a] = terms[a] + value * phi[b]
        terms[b] = terms[b] + value * phi[a]
    for n in range(N):
        quarter = code[n]
        local = jnp.where(
            quarter < 1.5,
            jnp.where(quarter < 0.5, quarters[0], quarters[1]),
            jnp.where(quarter < 2.5, quarters[2], quarters[3]),
        )
        out[n] = local * phi[n] - MIXING * terms[n]


def unpack_kernel(offsets, planes, out):
    oy = jnp.max(offsets[0:1, :])
    ox = jnp.max(offsets[1:2, :])
    chunks = torus_roll(lambda c: planes[pl.ds(c, N, stride=8), :], oy, ox)
    for s in range(8):
        out[0, :, 128 * s : 128 * s + 128] = chunks[s]


def shape(dims, dtype=F32):
    return jax.ShapeDtypeStruct(dims, dtype)


def constants():
    basis = np.concatenate(axis_basis(), axis=1)
    order = np.array([4 * s + q for q in range(4) for s in range(8)])

    def left(matrix):
        high, low = np_split(matrix)
        return np.concatenate([high, low, high], axis=1)

    high, low = np_split(np.kron(np.eye(4), basis))
    back_high, back_low = np_split(np.kron(np.eye(4), basis.T))
    fixed = np.zeros((256, 1024), jnp.bfloat16)
    fixed[:128, :256] = high
    fixed[128:, :256] = high
    fixed[:128, 256:512] = low
    fixed[:, 512:640] = back_high
    fixed[:, 640:768] = back_low
    fixed[:G, 768:864] = left(basis.T)
    fixed[G : 2 * G, 768:864] = left(basis[order].T)
    fixed[128:160, 768:960] = left(basis)
    fixed[160:192, 768:960] = left(basis[order])
    return jnp.asarray(fixed)


def exchange(x):
    return lax.all_to_all(x, "own", 0, 0, tiled=True)


def kernel(call, out_shape, in_specs, name, vmem, scratch=(), flops=0, moved=0):
    many = isinstance(out_shape, list)
    return pl.pallas_call(
        call,
        out_shape=out_shape,
        in_specs=in_specs,
        out_specs=[VM] * len(out_shape) if many else VM,
        scratch_shapes=scratch,
        compiler_params=pltpu.CompilerParams(vmem_limit_bytes=vmem << 20),
        cost_estimate=pl.CostEstimate(flops=flops, bytes_accessed=moved, transcendentals=0),
        name=name,
    )


def swapped(x, bits):
    return lax.ppermute(x, "grp", [(g, g ^ bits) for g in range(8)])


def body(orbitals, offsets, pairs, ext_pot):
    owner = lax.axis_index("own")
    fixed = constants()
    pairs = pairs.T

    sent = kernel(
        pack_kernel,
        shape((N, 16, 128), BF16),
        [SM, VM],
        "pack",
        60,
        [pltpu.VMEM((8 * N, 128), F32)],
        moved=200_000,
    )(offsets, orbitals)
    sent, fixed, pairs, ext_pot = lax.optimization_barrier((sent, fixed, pairs, ext_pot))
    recv = exchange(sent)

    fixed, pairs, offsets, green = kernel(
        table_kernel,
        [
            shape((256, 1024), BF16),
            shape((16, 128), jnp.int32),
            shape((8, 128), jnp.int32),
            shape((1024, 256)),
        ],
        [SM, SM, VM, VM],
        "tables",
        16,
        flops=2_000_000,
        moved=3_000_000,
    )(owner.reshape(1), offsets, fixed, pairs)
    plane = lax.dynamic_slice_in_dim(ext_pot, owner, 1, 0).astype(F32)
    plane = plane.reshape(2, B, 2, B).transpose(0, 2, 1, 3).reshape(4, 8, 128)
    recv, fixed, pairs, offsets, green, plane = lax.optimization_barrier(
        (recv, fixed, pairs, offsets, green, plane)
    )

    planes = shape((N, 8, 128))
    rho, dens, phi, code, place = pl.pallas_call(
        pair_kernel,
        out_shape=[planes, shape((4, 8, 128)), planes, planes, shape((8, 128))],
        in_specs=[VM, VM],
        out_specs=[pl.BlockSpec(memory_space=pltpu.HBM)] + [VM] * 4,
        scratch_shapes=[pltpu.VMEM((N, 8, 128), F32), pltpu.SemaphoreType.DMA(())],
        compiler_params=pltpu.CompilerParams(vmem_limit_bytes=4 << 20),
        cost_estimate=pl.CostEstimate(flops=0, bytes_accessed=600_000, transcendentals=0),
        name="pair_products",
    )(pairs, recv)

    mine = exchange(rho)
    others = [swapped(dens, step) for step in (2, 4, 6)]
    field = kernel(
        solve_kernel,
        shape((8 * N, 128)),
        [VM] * 4,
        "solve",
        16,
        [pltpu.VMEM((8 * G, 128), F32)],
        flops=1_000_000_000,
        moved=3_000_000,
    )(place, mine.reshape(8 * N, 128), fixed, green)
    fields = exchange(field.reshape(N, 8, 128))
    dens = (dens + others[1]) + (others[0] + others[2])
    other = swapped(dens, 1)

    gradient = kernel(
        gradient_kernel,
        shape((N, 8, 128)),
        [VM] * 7,
        "gradient_planes",
        4,
        [pltpu.VMEM((N, 8, 128), F32)],
        moved=600_000,
    )(pairs, phi, code, fields, plane, dens, other)
    back = exchange(gradient)

    return kernel(
        unpack_kernel, shape((1, BZ, B * B)), [VM, VM], "unpack", 4, moved=300_000
    )(offsets, back.reshape(8 * N, 128))


def solution(mesh):
    spec = P(("grp", "own"), None, None)
    in_specs = (spec, P(("grp", "own"), None), P("grp", None), P())
    return jax.shard_map(body, mesh=mesh, in_specs=in_specs, out_specs=spec, check_vma=False)
```
